32 devices in a mesh: expert: 4 (over x, core), shard: 8 (over z, y).
Axes of the slice: x: 2, y: 2, z: 4, core: 2. Of those that a mesh axis runs over, the one named last changes fastest.
Arguments:
- tokens: bfloat16 [4096, 2048], P(('expert', 'shard')), may hold values from -6 to 6
- cotangent: bfloat16 [4096, 2048], P(('expert', 'shard')), may hold values from -6 to 6
- segments: int32 [32, 128], P(('expert', 'shard')), may hold values from 0 to 7, never falling along the last dimension, each value on 1 to 64 neighbouring positions
- att_routes: int32 [4096, 2], P(('expert', 'shard')), may hold values from 0 to 3, all different within a row
- mlp_routes: int32 [4096, 2], P(('expert', 'shard')), may hold values from 0 to 3, all different within a row
- slot_order: int32 [32, 256], P(('expert', 'shard')), may hold values from 0 to 255, each once within a row
- norm_gains: bfloat16 [2048, 2], P('shard'), may hold values from 0.5 to 1.5
- kv_weight: bfloat16 [2048, 4096], P('shard'), may hold values from -0.125 to 0.125
- router_weight: bfloat16 [2048, 8], P('shard'), may hold values from -0.09375 to 0.09375
- query_weight: bfloat16 [4, 2048, 2048], P('expert', 'shard'), may hold values from -0.125 to 0.125
- output_weight: bfloat16 [4, 2048, 2048], P('expert', 'shard'), may hold values from -0.375 to 0.375
- gate_up_weight: bfloat16 [4, 2048, 11264], P('expert', 'shard'), may hold values from -0.125 to 0.125
- down_weight: bfloat16 [4, 2048, 5632], P('expert', 'shard'), may hold values from -0.15625 to 0.15625
Outputs:
- block_out: bfloat16 [4096, 2048], P(('expert', 'shard'))
- input_grad: float32 [4096, 2048], P(('expert', 'shard'))
- gains_grad: float32 [2048, 2], P('shard')
- keyval_grad: float32 [2048, 4096], P('shard')
- router_grad: float32 [2048, 8], P('shard')
- query_weight_grad: float32 [4, 2048, 2048], P('expert', 'shard')
- output_weight_grad: float32 [4, 2048, 2048], P('expert', 'shard')
- gate_up_grad: float32 [4, 2048, 11264], P('expert', 'shard')
- down_grad: float32 [4, 2048, 5632], P('expert', 'shard')
The draws below stay inside these ranges and needn't reach their ends.
Inputs may be any that keep to these rules, and one draw needn't show every extreme that they name: `att_routes`: each token names two different attention experts. `mlp_routes`: each token names two different feed-forward experts. `slot_order`: each row names every pair of its sequence once. `segments`: segment numbers never fall along a sequence; each sequence holds 8 documents, the longest of 64 tokens.
All inputs are finite; a program needn't handle non-finite values.
Results may differ from the reference program's by a relative error of at most 0.02.
Values may be sent and summed in bfloat16 or wider, within the bound.
No kernel may reach another device: no remote copies, remote signals or barrier semaphores. Data moves between devices by JAX's collectives and lax.ppermute only.
A program may use at most 640 MiB of HBM per device.

```python
import math
import jax
import jax.numpy as jnp
import numpy as np
from jax import lax

D = 2048
HEADS = 16
HEAD_DIM = 128
FF = 5632
TOK_DEV = 128
EXPERTS = 4
TOKENS = 4096
CAP = 64
SEGS = 8
DOC_MAX = 64
DEVICES = 32


def levels(rng, dims, pieces, smallest, largest):
    gain, own = 1.0, jax.random.fold_in(rng, 6)
    for dim, blocks in pieces:
        steps = jnp.exp(jax.random.uniform(jax.random.fold_in(own, dim), (blocks,), jnp.float32, smallest / len(pieces), largest / len(pieces)))
        gain = gain * jnp.repeat(steps, dims[dim] // blocks).reshape([-1 if axis == dim else 1 for axis in range(len(dims))])
    return gain


def picks_of(key, rows, number_of, top, lift):
    sequence = jax.random.permutation(jax.random.fold_in(key, 1), number_of)
    favour = sequence
    for power in range(3):
        favour = favour * favour // number_of
    favour = favour * lift // number_of
    lots = jax.random.randint(jax.random.fold_in(key, 2), (rows, number_of), 0, 4096) + favour
    sure = jax.random.permutation(jax.random.fold_in(key, 3), rows)[jnp.arange(number_of) % rows]
    lots = jnp.where(jnp.arange(rows)[:, None] == sure[None, :], 1 << 14, lots)
    merit = lots * number_of + jnp.arange(number_of)
    return lax.top_k(merit.astype(jnp.int32), top)[1].astype(jnp.int32)


def profile(amount, total, most, slope):
    portions = [(1 << 20) // math.isqrt(grade ** slope) + 1 for grade in range(2, amount + 1)]
    surplus, given = total - most - (amount - 1), [1] * (amount - 1)
    while surplus > 0:
        candidates = [i for i in range(amount - 1) if given[i] < most]
        whole, left = sum([portions[i] for i in candidates]), surplus
        for i in candidates:
            addition = min(most - given[i], max(1, left * portions[i] // whole), surplus)
            given[i] = given[i] + addition
            surplus = surplus - addition
    return np.array([most] + given)


def ragged_sizes(key, count, total, limit, lean):
    if count == 2:
        one = jax.random.randint(key, (), max(1, total - limit), min(limit, total - 1) + 1)
        return jnp.stack([one, total - one])
    lengths = jnp.asarray(profile(count, total, limit, lean), jnp.int32)
    pairs = (count - 1) // 2
    source_of, sink = lengths[1:1 + 2 * pairs:2], lengths[2:2 + 2 * pairs:2]
    slack = jnp.minimum(source_of - 1, limit - sink)
    moved = jax.random.randint(jax.random.fold_in(key, 1), (pairs,), 0, 1 << 20) % (slack + 1)
    lengths = lengths.at[1:1 + 2 * pairs:2].set(source_of - moved).at[2:2 + 2 * pairs:2].set(sink + moved)
    return lengths[jax.random.permutation(jax.random.fold_in(key, 2), count)]


def gaussian(own_key, extent, width, reach, cuts=(), kind=jnp.bfloat16):
    array = jax.random.normal(own_key, extent, jnp.float32) * width
    if len(cuts) > 0:
        array = levels(own_key, extent, cuts, -0.22, 0.18) * array
    return jnp.clip(array, min=-reach, max=reach).astype(kind)


def setup_inputs(seed: int = 0) -> dict:
    seeds = jax.random.split(jax.random.key(seed), 14)
    return {
        "tokens": gaussian(seeds[0], (TOKENS, D), 1.0, 6.0, ((0, 32),)),
        "cotangent": gaussian(seeds[1], (TOKENS, D), 1.0, 6.0, ((0, 32),)),
        "segments": jax.vmap(lambda own: jnp.searchsorted(jnp.cumsum(ragged_sizes(own, SEGS, TOK_DEV, DOC_MAX, 1)), jnp.arange(TOK_DEV), side="right"))(jax.random.split(seeds[2], DEVICES)).reshape((DEVICES, TOK_DEV)).astype(jnp.int32),
        "att_routes": picks_of(seeds[3], TOKENS, EXPERTS, 2, 4096),
        "mlp_routes": picks_of(seeds[4], TOKENS, EXPERTS, 2, 4096),
        "slot_order": jax.vmap(lambda own: jax.random.permutation(own, 2 * TOK_DEV))(jax.random.split(seeds[5], DEVICES)).reshape((DEVICES, 2 * TOK_DEV)).astype(jnp.int32),
        "norm_gains": jnp.clip(1.0 + 0.1 * jax.random.normal(seeds[6], (D, 2), jnp.float32), 0.5, 1.5).astype(jnp.bfloat16),
        "kv_weight": gaussian(seeds[7], (D, 2 * D), D ** -0.5, 0.125, ((0, 8),)),
        "router_weight": gaussian(seeds[8], (D, 2 * EXPERTS), (2 * D) ** -0.5, 0.09375, ((0, 8),)),
        "query_weight": gaussian(seeds[9], (EXPERTS, D, D), D ** -0.5, 0.125, ((0, 4), (1, 8))),
        "output_weight": gaussian(seeds[10], (EXPERTS, D, D), (D // 8) ** -0.5, 0.375, ((0, 4), (1, 8))),
        "gate_up_weight": gaussian(seeds[11], (EXPERTS, D, 2 * FF), D ** -0.5, 0.125, ((0, 4), (1, 8))),
        "down_weight": gaussian(seeds[12], (EXPERTS, D, FF), (FF // 4) ** -0.5, 0.15625, ((0, 4), (1, 8))),
    }


EPSILON = 1e-05
NEGATIVE = -1e+30
HIGHEST = lax.Precision.HIGHEST

@jax.custom_vjp
def low(v):
    return lax.optimization_barrier(v.astype(jnp.bfloat16)).astype(jnp.float32)

@jax.custom_vjp
def low_back(v):
    return v

def low_keep(v):
    return (low(v), None)

def low_pass(kept, grad):
    return (grad,)

def back_keep(v):
    return (v, None)

def back_low(kept, grad):
    return (low(grad),)
low.defvjp(low_keep, low_pass)
low_back.defvjp(back_keep, back_low)

def slot_table(routes, fill_order):
    pair_count = 2 * TOK_DEV
    pair_index = jnp.arange(pair_count, dtype=jnp.int32)
    pair_expert = jnp.concatenate([routes[:, 0], routes[:, 1]])
    ordered = pair_expert[fill_order]
    onehot = (ordered[:, None] == jnp.arange(EXPERTS, dtype=jnp.int32)[None, :]).astype(jnp.int32)
    earlier = jnp.cumsum(onehot, axis=0) - onehot
    position = lax.optimization_barrier(jnp.sum(earlier * onehot, axis=1)).astype(jnp.int32)
    target = (ordered * CAP + position).astype(jnp.int32)
    placing = (target[:, None] == pair_index[None, :]) & (position < CAP)[:, None]
    reorder = fill_order[:, None] == pair_index[None, :]
    return jnp.dot(placing.T.astype(jnp.float32), reorder.astype(jnp.float32), preferred_element_type=jnp.float32)

def rms_norm(values, gain_row):
    return values * lax.rsqrt(lax.optimization_barrier(jnp.mean(values * values, axis=-1, keepdims=True)) + EPSILON) * gain_row

def chosen_gates(logits, routes):
    return jax.nn.softmax(jnp.take_along_axis(logits, routes, axis=-1), axis=-1)

def attend(operands):
    query_pairs, keyvals, segment_rows = operands
    seq_count = query_pairs.shape[0]
    queries = query_pairs.reshape(seq_count, 2, TOK_DEV, HEADS, HEAD_DIM)
    key_heads = keyvals[..., :D].reshape(seq_count, TOK_DEV, HEADS, HEAD_DIM)
    value_heads = keyvals[..., D:].reshape(seq_count, TOK_DEV, HEADS, HEAD_DIM)
    scores = low_back(jnp.einsum('gkqhd,gshd->gkhqs', queries, key_heads, precision=HIGHEST) * HEAD_DIM ** (-0.5))
    positions = jnp.arange(TOK_DEV)
    allowed = (positions[:, None] >= positions[None, :])[None] & (segment_rows[:, :, None] == segment_rows[:, None, :])
    masked = jnp.where(allowed[:, None, None], scores, NEGATIVE)
    row_max = lax.optimization_barrier(jnp.max(masked, axis=-1, keepdims=True))
    exponent = jnp.exp(masked - row_max)
    softmax_out = low(exponent / lax.optimization_barrier(jnp.sum(exponent, axis=-1, keepdims=True)))
    mixed_heads = jnp.einsum('gkhqs,gshd->gkqhd', softmax_out, value_heads, precision=HIGHEST)
    return mixed_heads.reshape(seq_count, 2 * TOK_DEV, D)

def expert_ffn(operands):
    slot_rows, gate_up_e, down_e = operands
    gate_up = low_back(jnp.dot(slot_rows, gate_up_e, precision=HIGHEST, preferred_element_type=jnp.float32))
    activated = low(jax.nn.silu(gate_up[:, :FF]) * gate_up[:, FF:])
    return low_back(low(jnp.dot(activated, down_e.T, precision=HIGHEST, preferred_element_type=jnp.float32)))

def forward(inputs, gains, keyval_weight, router_weight, query_weight, output_weight, gate_up_weight, down_weight, att_table, mlp_table, segment_rows, att_routes, mlp_routes):
    sequences = TOKENS // TOK_DEV
    group_size = min(sequences, max(1, 4096 // TOK_DEV))
    groups = sequences // group_size
    seq_rows = inputs.reshape(sequences, TOK_DEV, D)
    normed_one = low(rms_norm(seq_rows, gains[:, 0]))
    keyvals = low_back(low(jnp.einsum('ntd,de->nte', normed_one, keyval_weight, precision=HIGHEST)))
    gate_att = chosen_gates(jnp.einsum('ntd,de->nte', normed_one, router_weight[:, :EXPERTS], precision=HIGHEST), att_routes)
    att_rows = low_back(jnp.einsum('nsp,npd->nsd', att_table, jnp.concatenate([normed_one, normed_one], axis=1), precision=HIGHEST))
    query_slots = low_back(low(jnp.einsum('necd,edf->necf', att_rows.reshape(sequences, EXPERTS, CAP, D), query_weight, precision=HIGHEST)))
    query_pairs = jnp.einsum('nsp,nsf->npf', att_table, query_slots.reshape(sequences, 2 * TOK_DEV, D), precision=HIGHEST)
    mixed = lax.map(jax.checkpoint(attend), (query_pairs.reshape(groups, group_size, 2 * TOK_DEV, D), keyvals.reshape(groups, group_size, TOK_DEV, 2 * D), segment_rows.reshape(groups, group_size, TOK_DEV)))
    mixed = mixed.reshape(sequences, 2 * TOK_DEV, D)
    mixed_slots = low_back(low(jnp.einsum('nsp,npd->nsd', att_table, mixed, precision=HIGHEST)))
    att_out = low_back(low(jnp.einsum('necf,edf->necd', mixed_slots.reshape(sequences, EXPERTS, CAP, D), output_weight, precision=HIGHEST)))
    att_pairs = jnp.einsum('nsp,nsd->npd', att_table, att_out.reshape(sequences, 2 * TOK_DEV, D), precision=HIGHEST)
    hidden = seq_rows + gate_att[..., 0:1] * att_pairs[:, :TOK_DEV] + gate_att[..., 1:2] * att_pairs[:, TOK_DEV:]
    normed_two = low(rms_norm(hidden, gains[:, 1]))
    gate_mlp = chosen_gates(jnp.einsum('ntd,de->nte', normed_two, router_weight[:, EXPERTS:], precision=HIGHEST), mlp_routes)
    ffn_rows = low_back(jnp.einsum('nsp,npd->nsd', mlp_table, jnp.concatenate([normed_two, normed_two], axis=1), precision=HIGHEST))
    by_expert = ffn_rows.reshape(sequences, EXPERTS, CAP, D).transpose(1, 0, 2, 3).reshape(EXPERTS, sequences * CAP, D)
    ffn_out = lax.map(jax.checkpoint(expert_ffn), (by_expert, gate_up_weight, down_weight))
    ffn_out = ffn_out.reshape(EXPERTS, sequences, CAP, D).transpose(1, 0, 2, 3).reshape(sequences, 2 * TOK_DEV, D)
    ffn_pairs = jnp.einsum('nsp,nsd->npd', mlp_table, ffn_out, precision=HIGHEST)
    result = hidden + gate_mlp[..., 0:1] * ffn_pairs[:, :TOK_DEV] + gate_mlp[..., 1:2] * ffn_pairs[:, TOK_DEV:]
    return result.reshape(TOKENS, D)

def reference(tokens, cotangent, segments, att_routes, mlp_routes, slot_order, norm_gains, kv_weight, router_weight, query_weight, output_weight, gate_up_weight, down_weight):
    sequences = TOKENS // TOK_DEV
    att_seq = att_routes.reshape(sequences, TOK_DEV, 2)
    mlp_seq = mlp_routes.reshape(sequences, TOK_DEV, 2)
    att_table = jax.vmap(slot_table)(att_seq, slot_order)
    mlp_table = jax.vmap(slot_table)(mlp_seq, slot_order)
    floats = tuple((item.astype(jnp.float32) for item in (tokens, norm_gains, kv_weight, router_weight, query_weight, output_weight, gate_up_weight, down_weight)))

    def block_fn(*params):
        return forward(*params, att_table, mlp_table, segments, att_seq, mlp_seq)
    result, pullback = jax.vjp(block_fn, *floats)
    grads = pullback(cotangent.astype(jnp.float32))
    return (result.astype(jnp.bfloat16), grads[0], grads[1], grads[2], grads[3], grads[4], grads[5], grads[6], grads[7])
```

```python
import jax
import jax.numpy as jnp
from jax import lax
from jax.sharding import Mesh
from jax.sharding import PartitionSpec as P

D = 2048
HEADS = 16
HEAD_DIM = 128
FF = 5632
Z = 4

EPSILON = 1e-05
NEGATIVE = -1e30
HIGHEST = lax.Precision.HIGHEST
CONTRACT_FIRST = (((0,), (0,)), ((), ()))
CONTRACT_LAST = (((1,), (1,)), ((), ()))
BF16 = jnp.bfloat16
F32 = jnp.float32


def slot_table(routes, fill_order, experts):
    pair_count = 2 * routes.shape[0]
    capacity = pair_count // experts
    pair_index = jnp.arange(pair_count, dtype=jnp.int32)
    pair_expert = jnp.concatenate([routes[:, 0], routes[:, 1]]).astype(F32)
    reorder = (fill_order[:, None] == pair_index[None, :]).astype(F32)
    ordered = jnp.dot(reorder, pair_expert, precision=HIGHEST)
    onehot = (ordered[:, None] == jnp.arange(experts, dtype=F32)[None, :]).astype(F32)
    below_mask = (pair_index[:, None] > pair_index[None, :]).astype(F32)
    earlier = jnp.dot(below_mask, onehot, precision=HIGHEST)
    position = jnp.sum(earlier * onehot, axis=1)
    target = ordered * capacity + position
    placing = (
        (target[:, None] == pair_index.astype(F32)[None, :]) & (position < capacity)[:, None]
    ).astype(F32)
    return lax.dot_general(placing, reorder, CONTRACT_FIRST, precision=HIGHEST).astype(BF16)


def select_rows(table, pair_rows):
    return jnp.dot(table, pair_rows, preferred_element_type=F32).astype(BF16)


def spread_rows(table, slot_rows):
    return lax.dot_general(table, slot_rows, CONTRACT_FIRST, preferred_element_type=F32).astype(BF16)


def chosen_gates(logits, routes, experts):
    expert_ids = jnp.arange(experts, dtype=jnp.int32)[None, :]
    first_logit = jnp.sum(jnp.where(routes[:, 0:1] == expert_ids, logits, 0.0), axis=1)
    second_logit = jnp.sum(jnp.where(routes[:, 1:2] == expert_ids, logits, 0.0), axis=1)
    return jax.nn.softmax(jnp.stack([first_logit, second_logit], axis=1), axis=1)


def gate_logit_grad(gate_pair, gate_grad, routes, experts):
    expert_ids = jnp.arange(experts, dtype=jnp.int32)[None, :]
    chosen_grad = gate_pair * (gate_grad - jnp.sum(gate_pair * gate_grad, axis=1, keepdims=True))
    first_part = chosen_grad[:, 0:1] * (routes[:, 0:1] == expert_ids).astype(F32)
    return first_part + chosen_grad[:, 1:2] * (routes[:, 1:2] == expert_ids).astype(F32)


def norm_back(values, scale, gain_row, normed_grad):
    scaled = normed_grad * gain_row
    return scale * (
        scaled - values * scale * scale * jnp.mean(scaled * values, axis=1, keepdims=True)
    )


def attend_forward(queries, key_heads, value_heads, allowed):
    tok_rows = key_heads.shape[0]
    scores = jnp.einsum("kqhd,shd->khqs", queries, key_heads, preferred_element_type=F32) * (
        HEAD_DIM ** (-0.5)
    )
    masked = jnp.where(allowed[None, None], scores, NEGATIVE)
    row_max = jnp.max(masked, axis=-1, keepdims=True)
    exponent = jnp.exp(masked - row_max)
    totals = jnp.sum(exponent, axis=-1, keepdims=True)
    softmax_out = (exponent / totals).astype(BF16)
    mixed = jnp.einsum("khqs,shd->kqhd", softmax_out, value_heads, preferred_element_type=F32)
    mixed = mixed.astype(BF16).reshape(2 * tok_rows, HEADS * HEAD_DIM)
    return mixed, (row_max + jnp.log(totals))[..., 0]


def attend_backward(queries, key_heads, value_heads, allowed, log_sums, mixed_grad):
    tok_rows = key_heads.shape[0]
    scale_factor = HEAD_DIM ** (-0.5)
    scores = (
        jnp.einsum("kqhd,shd->khqs", queries, key_heads, preferred_element_type=F32) * scale_factor
    )
    softmax_out = jnp.where(allowed[None, None], jnp.exp(scores - log_sums[..., None]), 0.0)
    prob_grad = jnp.einsum("kqhd,shd->khqs", mixed_grad, value_heads, preferred_element_type=F32)
    score_grad = (
        softmax_out * (prob_grad - jnp.sum(softmax_out * prob_grad, axis=-1, keepdims=True))
    ).astype(BF16)
    query_grad = (
        jnp.einsum("khqs,shd->kqhd", score_grad, key_heads, preferred_element_type=F32)
        * scale_factor
    )
    key_grad = (
        jnp.einsum("khqs,kqhd->shd", score_grad, queries, preferred_element_type=F32) * scale_factor
    )
    value_grad = jnp.einsum(
        "khqs,kqhd->shd", softmax_out.astype(BF16), mixed_grad, preferred_element_type=F32
    )
    return (
        query_grad.reshape(2 * tok_rows, D),
        key_grad.reshape(tok_rows, D),
        value_grad.reshape(tok_rows, D),
    )


def pick(choices, index):
    result = choices[0]
    for i in range(1, len(choices)):
        result = jnp.where(index == i, choices[i], result)
    return result


def per_device(
    tokens,
    cotangent,
    segments,
    att_routes,
    mlp_routes,
    slot_order,
    norm_gains,
    kv_weight,
    router_weight,
    query_weight,
    output_weight,
    gate_up_weight,
    down_weight,
):
    tok_rows = tokens.shape[0]
    experts = lax.axis_size("expert") * query_weight.shape[0]
    ycount = lax.axis_size("y")
    capacity = 2 * tok_rows // experts
    part = norm_gains.shape[0]
    half = D // ycount
    kv_cols = 2 * D // experts
    slice_ff = FF // Z
    pieces = tok_rows // capacity
    y_index = lax.axis_index("y")
    e_index = lax.axis_index("expert")

    def y_major(v):
        return jnp.concatenate(
            [
                v[:, (z * ycount + y) * part : (z * ycount + y + 1) * part]
                for y in range(ycount)
                for z in range(Z)
            ],
            axis=1,
        )

    def natural(v):
        return jnp.concatenate(
            [
                v[:, (y * Z + z) * part : (y * Z + z + 1) * part]
                for z in range(Z)
                for y in range(ycount)
            ],
            axis=1,
        )

    def halves(v):
        return [v[..., y * half : (y + 1) * half] for y in range(ycount)]

    def own_first(v):
        h = halves(v)
        return jnp.concatenate(
            [pick([h[(i + k) % ycount] for i in range(ycount)], y_index) for k in range(ycount)],
            axis=-1,
        )

    def own_first_back(v):
        h = halves(v)
        return jnp.concatenate(
            [pick([h[(j - i) % ycount] for i in range(ycount)], y_index) for j in range(ycount)],
            axis=-1,
        )

    def exchange(v, axes):
        return lax.all_to_all(v, axes, split_axis=0, concat_axis=0, tiled=True)

    def pack(v):
        return jnp.concatenate(
            [v[..., i * capacity : (i + 1) * capacity, :] for i in range(pieces)], axis=-1
        )

    def unpack(v):
        return jnp.concatenate(
            [v[..., i * kv_cols : (i + 1) * kv_cols] for i in range(pieces)], axis=-2
        )

    both = ("expert", "y")

    small = lax.all_gather(
        jnp.concatenate([norm_gains, router_weight], axis=1), ("y", "z"), axis=0, tiled=True
    )
    kv_part = lax.dynamic_slice_in_dim(kv_weight, e_index * kv_cols, kv_cols, 1)
    wide_query = lax.all_gather(query_weight[0], "z", axis=0, tiled=True)
    wide_kv = lax.all_gather(kv_part, "z", axis=0, tiled=True)
    wide_output = lax.all_gather(output_weight[0], "z", axis=0, tiled=True)

    def across_y(own):
        parts = [own]
        for k in range(1, ycount):
            parts.append(lax.ppermute(own, "y", [(i, (i - k) % ycount) for i in range(ycount)]))
        return jnp.concatenate(parts, axis=0)

    gu = gate_up_weight[0]
    gu_send = jnp.stack(
        [
            jnp.concatenate(
                [
                    gu[:, z * slice_ff : (z + 1) * slice_ff],
                    gu[:, FF + z * slice_ff : FF + (z + 1) * slice_ff],
                ],
                axis=1,
            )
            for z in range(Z)
        ]
    )
    down_send = jnp.stack(
        [down_weight[0][:, z * slice_ff : (z + 1) * slice_ff] for z in range(Z)]
    )
    wide_gate_up = across_y(exchange(gu_send, "z").reshape(half, 2 * slice_ff))
    wide_down = across_y(exchange(down_send, "z").reshape(half, slice_ff))

    segment_row = segments[0]
    fill_order = slot_order[0]
    positions = jnp.arange(tok_rows)
    allowed = (positions[:, None] >= positions[None, :]) & (
        segment_row[:, None] == segment_row[None, :]
    )
    table_att = slot_table(att_routes, fill_order, experts)
    table_mlp = slot_table(mlp_routes, fill_order, experts)
    token_att = table_att[:, :tok_rows] + table_att[:, tok_rows:]
    token_mlp = table_mlp[:, :tok_rows] + table_mlp[:, tok_rows:]

    gain_one = small[:, 0].astype(F32)
    gain_two = small[:, 1].astype(F32)
    router_att = small[:, 2 : 2 + experts]
    router_mlp = small[:, 2 + experts :]
    inputs = y_major(tokens).astype(F32)
    grad_out = y_major(cotangent).astype(F32)
    scale_one = lax.rsqrt(jnp.mean(inputs * inputs, axis=1, keepdims=True) + EPSILON)
    normed_one = (inputs * scale_one * gain_one).astype(BF16)

    att_slots_in = select_rows(token_att, normed_one).reshape(experts, capacity, D)
    send = jnp.stack(
        [
            jnp.concatenate([s, jnp.broadcast_to(n[None], (experts, tok_rows, half))], axis=1)
            for s, n in zip(halves(att_slots_in), halves(normed_one))
        ],
        axis=1,
    )
    got = exchange(send.reshape(experts * ycount, capacity + tok_rows, half), both)
    query_in = got[:, :capacity].reshape(experts * ycount * capacity, half)
    kv_in = got[:, capacity:].reshape(experts * ycount * tok_rows, half)
    query_part = jnp.dot(query_in, wide_query, preferred_element_type=F32).astype(BF16)
    kv_out = jnp.dot(kv_in, wide_kv, preferred_element_type=F32).astype(BF16)
    back = jnp.concatenate(
        [
            query_part.reshape(experts * ycount, capacity, D),
            pack(kv_out.reshape(experts * ycount, tok_rows, kv_cols)),
        ],
        axis=1,
    )
    back = exchange(back, both).reshape(experts, ycount, 2 * capacity, D)
    summed = jnp.sum(back.astype(F32), axis=1).astype(BF16)
    query_slots = summed[:, :capacity].reshape(2 * tok_rows, D)
    kv_parts = unpack(summed[:, capacity:])
    keyvals = jnp.concatenate([kv_parts[e] for e in range(experts)], axis=-1)
    key_heads = keyvals[:, :D].reshape(tok_rows, HEADS, HEAD_DIM)
    value_heads = keyvals[:, D:].reshape(tok_rows, HEADS, HEAD_DIM)
    router_logits = jnp.dot(normed_one, router_att, preferred_element_type=F32)
    gate_att = chosen_gates(router_logits, att_routes, experts)
    query_pairs = spread_rows(table_att, query_slots)
    queries = query_pairs.reshape(2, tok_rows, HEADS, HEAD_DIM)
    mixed_heads, log_sums = attend_forward(queries, key_heads, value_heads, allowed)

    def to_rows(v):
        v = v.reshape(experts, 1, capacity, D)
        v = jnp.broadcast_to(v, (experts, ycount, capacity, D))
        return exchange(v.reshape(experts * ycount, capacity, D), both)

    def from_halves(v):
        v = exchange(v.reshape(experts * ycount, capacity, half), both)
        v = v.reshape(experts, ycount, capacity, half)
        return jnp.concatenate([v[:, y] for y in range(ycount)], axis=-1).reshape(2 * tok_rows, D)

    mixed_in = to_rows(select_rows(table_att, mixed_heads)).reshape(-1, D)
    projected = lax.dot_general(
        mixed_in, wide_output, CONTRACT_LAST, preferred_element_type=F32
    ).astype(BF16)
    att_pairs = (
        spread_rows(table_att, from_halves(projected)).astype(F32).reshape(2, tok_rows, D)
    )
    hidden = inputs + gate_att[:, 0:1] * att_pairs[0] + gate_att[:, 1:2] * att_pairs[1]
    scale_two = lax.rsqrt(jnp.mean(hidden * hidden, axis=1, keepdims=True) + EPSILON)
    normed_two = (hidden * scale_two * gain_two).astype(BF16)
    mlp_logits = jnp.dot(normed_two, router_mlp, preferred_element_type=F32)
    gate_mlp = chosen_gates(mlp_logits, mlp_routes, experts)

    gated_pairs = own_first(
        jnp.concatenate([gate_mlp[:, 0:1] * grad_out, gate_mlp[:, 1:2] * grad_out], axis=0).astype(
            BF16
        )
    )
    ffn_send = select_rows(token_mlp, own_first(normed_two)).reshape(experts, capacity, D)
    gated_send = select_rows(table_mlp, gated_pairs).reshape(experts, capacity, D)
    ffn_local = exchange(ffn_send, "expert").reshape(2 * tok_rows, D)
    gated_local = exchange(gated_send, "expert").reshape(2 * tok_rows, D)
    ffn_rows = lax.all_gather(ffn_local, "z", axis=0, tiled=True)
    gated_rows = lax.all_gather(gated_local, "z", axis=0, tiled=True)
    gate_up = jnp.dot(ffn_rows, wide_gate_up, preferred_element_type=F32)
    gate_part = gate_up[:, :slice_ff]
    up_part = gate_up[:, slice_ff:]
    sigma = jax.nn.sigmoid(gate_part)
    activated = (gate_part * sigma * up_part).astype(BF16)
    out_part = lax.dot_general(
        activated, wide_down, CONTRACT_LAST, preferred_element_type=F32
    ).astype(BF16)
    act_grad = jnp.dot(gated_rows, wide_down, preferred_element_type=F32)
    gate_grad = act_grad * up_part * sigma * (1.0 + gate_part * (1.0 - sigma))
    up_grad = act_grad * gate_part * sigma
    gate_up_grad = jnp.concatenate([gate_grad, up_grad], axis=-1).astype(BF16)
    row_part = lax.dot_general(
        gate_up_grad, wide_gate_up, CONTRACT_LAST, preferred_element_type=F32
    ).astype(BF16)

    def from_parts(v):
        v = lax.psum_scatter(v, "z", scatter_dimension=0, tiled=True)
        v = exchange(v.reshape(experts, capacity, D), "expert").reshape(2 * tok_rows, D)
        return own_first_back(spread_rows(table_mlp, v)).astype(F32).reshape(2, tok_rows, D)

    ffn_row_pairs = from_parts(row_part)
    ffn_pairs = from_parts(out_part)
    block_out = (hidden + gate_mlp[:, 0:1] * ffn_pairs[0] + gate_mlp[:, 1:2] * ffn_pairs[1]).astype(
        BF16
    )

    def outer(left_rows, right_rows):
        return lax.dot_general(left_rows, right_rows, CONTRACT_FIRST, preferred_element_type=F32)

    def ffn_weight_grad(left, right):
        full = outer(left, right)
        own = full[:half]
        for k in range(1, ycount):
            moved = full[k * half : (k + 1) * half].astype(BF16)
            own = own + lax.ppermute(
                moved, "y", [(i, (i + k) % ycount) for i in range(ycount)]
            ).astype(F32)
        cols = right.shape[1]
        return exchange(own.astype(BF16).reshape(Z, part, cols), "z").astype(F32)

    gu_grads = ffn_weight_grad(ffn_rows, gate_up_grad)
    down_grads = ffn_weight_grad(gated_rows, activated)
    gate_up_weight_grad = jnp.concatenate(
        [gu_grads[z, :, :slice_ff] for z in range(Z)]
        + [gu_grads[z, :, slice_ff:] for z in range(Z)],
        axis=1,
    )[None]
    down_weight_grad = jnp.concatenate([down_grads[z] for z in range(Z)], axis=1)[None]

    gate_mlp_grad = jnp.sum(grad_out[None] * ffn_pairs, axis=2).T
    logit_mlp_grad = gate_logit_grad(gate_mlp, gate_mlp_grad, mlp_routes, experts)
    normed_two_grad = (
        ffn_row_pairs[0]
        + ffn_row_pairs[1]
        + lax.dot_general(
            logit_mlp_grad, router_mlp.astype(F32), CONTRACT_LAST, precision=HIGHEST
        )
    )
    hidden_grad = grad_out + norm_back(hidden, scale_two, gain_two, normed_two_grad)
    gate_att_grad = jnp.sum(hidden_grad[None] * att_pairs, axis=2).T
    logit_att_grad = gate_logit_grad(gate_att, gate_att_grad, att_routes, experts)
    gated_hidden = jnp.concatenate(
        [gate_att[:, 0:1] * hidden_grad, gate_att[:, 1:2] * hidden_grad], axis=0
    ).astype(BF16)
    hidden_send = select_rows(table_att, gated_hidden).reshape(experts, capacity, D)
    hidden_in = exchange(
        jnp.stack(halves(hidden_send), axis=1).reshape(experts * ycount, capacity, half), both
    ).reshape(-1, half)
    head_part = jnp.dot(hidden_in, wide_output, preferred_element_type=F32).astype(BF16)
    head_part = exchange(head_part.reshape(experts * ycount, capacity, D), both)
    head_slots = jnp.sum(
        head_part.reshape(experts, ycount, capacity, D).astype(F32), axis=1
    ).astype(BF16)
    mixed_grad = spread_rows(table_att, head_slots.reshape(2 * tok_rows, D)).reshape(
        2, tok_rows, HEADS, HEAD_DIM
    )
    output_grad = lax.psum_scatter(
        outer(hidden_in, mixed_in).astype(BF16), "z", scatter_dimension=0, tiled=True
    ).astype(F32)[None]
    query_grad, key_grad, value_grad = attend_backward(
        queries, key_heads, value_heads, allowed, log_sums, mixed_grad
    )
    keyval_row_grad = jnp.concatenate([key_grad, value_grad], axis=1).astype(BF16)
    query_send = select_rows(table_att, query_grad.astype(BF16)).reshape(experts, capacity, D)
    kv_send = pack(
        jnp.stack([keyval_row_grad[:, e * kv_cols : (e + 1) * kv_cols] for e in range(experts)])
    )
    send = jnp.concatenate([query_send, kv_send], axis=1).reshape(experts, 1, 2 * capacity, D)
    send = jnp.broadcast_to(send, (experts, ycount, 2 * capacity, D))
    got = exchange(send.reshape(experts * ycount, 2 * capacity, D), both)
    query_rows = got[:, :capacity].reshape(-1, D)
    kv_rows = unpack(got[:, capacity:]).reshape(-1, kv_cols)
    input_part = lax.dot_general(
        query_rows, wide_query, CONTRACT_LAST, preferred_element_type=F32
    ).astype(BF16)
    normed_part = lax.dot_general(
        kv_rows, wide_kv, CONTRACT_LAST, preferred_element_type=F32
    ).astype(BF16)
    back = jnp.concatenate(
        [
            input_part.reshape(experts * ycount, capacity, half),
            normed_part.reshape(experts * ycount, tok_rows, half),
        ],
        axis=1,
    )
    back = exchange(back, both).reshape(experts, ycount, capacity + tok_rows, half)
    back = jnp.concatenate([back[:, y] for y in range(ycount)], axis=-1)
    input_pairs = (
        spread_rows(table_att, back[:, :capacity].reshape(2 * tok_rows, D))
        .astype(F32)
        .reshape(2, tok_rows, D)
    )
    query_weight_grad = lax.psum_scatter(
        outer(query_in, query_rows).astype(BF16), "z", scatter_dimension=0, tiled=True
    ).astype(F32)[None]
    kv_grad_part = lax.psum_scatter(
        outer(kv_in, kv_rows).astype(BF16), "z", scatter_dimension=0, tiled=True
    )
    keyval_grad = lax.all_gather(kv_grad_part, "expert", axis=1, tiled=True).astype(F32)
    normed_one_grad = (
        input_pairs[0] + input_pairs[1] + jnp.sum(back[:, capacity:].astype(F32), axis=0)
    )
    normed_one_grad = normed_one_grad + lax.dot_general(
        logit_att_grad, router_att.astype(F32), CONTRACT_LAST, precision=HIGHEST
    )
    input_grad = natural(
        hidden_grad + norm_back(inputs, scale_one, gain_one, normed_one_grad)
    )

    small_grads = jnp.concatenate(
        [
            jnp.sum(normed_one_grad * inputs * scale_one, axis=0)[None],
            jnp.sum(normed_two_grad * hidden * scale_two, axis=0)[None],
            lax.dot_general(
                logit_att_grad, normed_one.astype(F32), CONTRACT_FIRST, precision=HIGHEST
            ),
            lax.dot_general(
                logit_mlp_grad, normed_two.astype(F32), CONTRACT_FIRST, precision=HIGHEST
            ),
        ],
        axis=0,
    )
    rows = small_grads.shape[0]
    small_grads = jnp.stack(
        [small_grads[:, i * part : (i + 1) * part] for i in range(Z * ycount)]
    )
    small_grads = jnp.sum(exchange(small_grads, ("y", "z")), axis=0)
    small_grads = lax.psum(small_grads, "expert").T
    gains_grad = small_grads[:, :2]
    router_grad = small_grads[:, 2:rows]
    return (
        natural(block_out),
        input_grad,
        gains_grad,
        keyval_grad,
        router_grad,
        query_weight_grad,
        output_grad,
        gate_up_weight_grad,
        down_weight_grad,
    )


def solution(mesh):
    experts, shards = mesh.shape["expert"], mesh.shape["shard"]
    grid = Mesh(mesh.devices.reshape(experts, Z, shards // Z), ("expert", "z", "y"))
    rows = P(("expert", "z", "y"), None)
    shared = P(("z", "y"), None)
    owned = P("expert", ("z", "y"), None)
    in_specs = (rows,) * 6 + (shared,) * 3 + (owned,) * 4
    out_specs = (rows,) * 2 + (shared,) * 3 + (owned,) * 4
    return jax.shard_map(
        per_device, mesh=grid, in_specs=in_specs, out_specs=out_specs, check_vma=False
    )
```

```python
import jax
import jax.numpy as jnp
from jax import lax
from jax.sharding import Mesh
from jax.sharding import PartitionSpec as P

D = 2048
HEADS = 16
HEAD_DIM = 128
FF = 5632
Z = 4

EPSILON = 1e-05
NEGATIVE = -1e30
HIGHEST = lax.Precision.HIGHEST
CONTRACT_FIRST = (((0,), (0,)), ((), ()))
CONTRACT_LAST = (((1,), (1,)), ((), ()))
BF16 = jnp.bfloat16
F32 = jnp.float32


def slot_table(routes, fill_order, experts):
    pair_count = 2 * routes.shape[0]
    capacity = pair_count // experts
    pair_index = jnp.arange(pair_count, dtype=jnp.int32)
    pair_expert = jnp.concatenate([routes[:, 0], routes[:, 1]]).astype(F32)
    reorder = (fill_order[:, None] == pair_index[None, :]).astype(F32)
    ordered = jnp.dot(reorder, pair_expert, precision=HIGHEST)
    onehot = (ordered[:, None] == jnp.arange(experts, dtype=F32)[None, :]).astype(F32)
    below_mask = (pair_index[:, None] > pair_index[None, :]).astype(F32)
    earlier = jnp.dot(below_mask, onehot, precision=HIGHEST)
    position = jnp.sum(earlier * onehot, axis=1)
    target = ordered * capacity + position
    placing = (
        (target[:, None] == pair_index.astype(F32)[None, :]) & (position < capacity)[:, None]
    ).astype(F32)
    return lax.dot_general(placing, reorder, CONTRACT_FIRST, precision=HIGHEST).astype(BF16)


def select_rows(table, pair_rows):
    return jnp.dot(table, pair_rows, preferred_element_type=F32).astype(BF16)


def spread_rows(table, slot_rows):
    return lax.dot_general(table, slot_rows, CONTRACT_FIRST, preferred_element_type=F32).astype(BF16)


def chosen_gates(logits, routes, experts):
    expert_ids = jnp.arange(experts, dtype=jnp.int32)[None, :]
    first_logit = jnp.sum(jnp.where(routes[:, 0:1] == expert_ids, logits, 0.0), axis=1)
    second_logit = jnp.sum(jnp.where(routes[:, 1:2] == expert_ids, logits, 0.0), axis=1)
    return jax.nn.softmax(jnp.stack([first_logit, second_logit], axis=1), axis=1)


def gate_logit_grad(gate_pair, gate_grad, routes, experts):
    expert_ids = jnp.arange(experts, dtype=jnp.int32)[None, :]
    chosen_grad = gate_pair * (gate_grad - jnp.sum(gate_pair * gate_grad, axis=1, keepdims=True))
    first_part = chosen_grad[:, 0:1] * (routes[:, 0:1] == expert_ids).astype(F32)
    return first_part + chosen_grad[:, 1:2] * (routes[:, 1:2] == expert_ids).astype(F32)


def norm_back(values, scale, gain_row, normed_grad):
    scaled = normed_grad * gain_row
    return scale * (
        scaled - values * scale * scale * jnp.mean(scaled * values, axis=1, keepdims=True)
    )


def attend_forward(queries, key_heads, value_heads, allowed):
    tok_rows = key_heads.shape[0]
    scores = jnp.einsum("kqhd,shd->khqs", queries, key_heads, preferred_element_type=F32) * (
        HEAD_DIM ** (-0.5)
    )
    masked = jnp.where(allowed[None, None], scores, NEGATIVE)
    row_max = jnp.max(masked, axis=-1, keepdims=True)
    exponent = jnp.exp(masked - row_max)
    totals = jnp.sum(exponent, axis=-1, keepdims=True)
    softmax_out = (exponent / totals).astype(BF16)
    mixed = jnp.einsum("khqs,shd->kqhd", softmax_out, value_heads, preferred_element_type=F32)
    mixed = mixed.astype(BF16).reshape(2 * tok_rows, HEADS * HEAD_DIM)
    return mixed, (row_max + jnp.log(totals))[..., 0]


def attend_backward(queries, key_heads, value_heads, allowed, log_sums, mixed_grad):
    tok_rows = key_heads.shape[0]
    scale_factor = HEAD_DIM ** (-0.5)
    scores = (
        jnp.einsum("kqhd,shd->khqs", queries, key_heads, preferred_element_type=F32) * scale_factor
    )
    softmax_out = jnp.where(allowed[None, None], jnp.exp(scores - log_sums[..., None]), 0.0)
    prob_grad = jnp.einsum("kqhd,shd->khqs", mixed_grad, value_heads, preferred_element_type=F32)
    score_grad = (
        softmax_out * (prob_grad - jnp.sum(softmax_out * prob_grad, axis=-1, keepdims=True))
    ).astype(BF16)
    query_grad = (
        jnp.einsum("khqs,shd->kqhd", score_grad, key_heads, preferred_element_type=F32)
        * scale_factor
    )
    key_grad = (
        jnp.einsum("khqs,kqhd->shd", score_grad, queries, preferred_element_type=F32) * scale_factor
    )
    value_grad = jnp.einsum(
        "khqs,kqhd->shd", softmax_out.astype(BF16), mixed_grad, preferred_element_type=F32
    )
    return (
        query_grad.reshape(2 * tok_rows, D),
        key_grad.reshape(tok_rows, D),
        value_grad.reshape(tok_rows, D),
    )


def pick(choices, index):
    result = choices[0]
    for i in range(1, len(choices)):
        result = jnp.where(index == i, choices[i], result)
    return result


def split3(v):
    high = lax.reduce_precision(v, exponent_bits=8, mantissa_bits=7)
    middle = lax.reduce_precision(v - high, exponent_bits=8, mantissa_bits=7)
    return [high.astype(BF16), middle.astype(BF16), (v - high - middle).astype(BF16)]


def per_device(
    tokens,
    cotangent,
    segments,
    att_routes,
    mlp_routes,
    slot_order,
    norm_gains,
    kv_weight,
    router_weight,
    query_weight,
    output_weight,
    gate_up_weight,
    down_weight,
):
    tok_rows = tokens.shape[0]
    experts = lax.axis_size("expert") * query_weight.shape[0]
    ycount = lax.axis_size("y")
    capacity = 2 * tok_rows // experts
    part = norm_gains.shape[0]
    half = D // ycount
    kv_cols = 2 * D // experts
    slice_ff = FF // Z
    pieces = tok_rows // capacity
    y_index = lax.axis_index("y")
    e_index = lax.axis_index("expert")

    def y_major(v):
        return jnp.concatenate(
            [
                v[:, (z * ycount + y) * part : (z * ycount + y + 1) * part]
                for y in range(ycount)
                for z in range(Z)
            ],
            axis=1,
        )

    def natural(v):
        return jnp.concatenate(
            [
                v[:, (y * Z + z) * part : (y * Z + z + 1) * part]
                for z in range(Z)
                for y in range(ycount)
            ],
            axis=1,
        )

    def halves(v):
        return [v[..., y * half : (y + 1) * half] for y in range(ycount)]

    def own_first(v):
        h = halves(v)
        return jnp.concatenate(
            [pick([h[(i + k) % ycount] for i in range(ycount)], y_index) for k in range(ycount)],
            axis=-1,
        )

    def own_first_back(v):
        h = halves(v)
        return jnp.concatenate(
            [pick([h[(j - i) % ycount] for i in range(ycount)], y_index) for j in range(ycount)],
            axis=-1,
        )

    def exchange(v, axes):
        return lax.all_to_all(v, axes, split_axis=0, concat_axis=0, tiled=True)

    def pack(v):
        return jnp.concatenate(
            [v[..., i * capacity : (i + 1) * capacity, :] for i in range(pieces)], axis=-1
        )

    def unpack(v):
        return jnp.concatenate(
            [v[..., i * kv_cols : (i + 1) * kv_cols] for i in range(pieces)], axis=-2
        )

    both = ("expert", "y")

    shards = Z * ycount
    small = jnp.concatenate([norm_gains, router_weight], axis=1)
    small = jnp.pad(small, ((0, 0), (0, -small.shape[1] % 16))).T
    small = exchange(jnp.broadcast_to(small[None], (shards, *small.shape)), ("y", "z"))
    small = jnp.concatenate([small[i] for i in range(shards)], axis=1)
    kv_part = lax.dynamic_slice_in_dim(kv_weight, e_index * kv_cols, kv_cols, 1)
    wide_query = lax.all_gather(query_weight[0], "z", axis=0, tiled=True)
    wide_kv = lax.all_gather(kv_part, "z", axis=0, tiled=True)
    wide_output = lax.all_gather(output_weight[0], "z", axis=0, tiled=True)

    def across_y(own):
        parts = [own]
        for k in range(1, ycount):
            parts.append(lax.ppermute(own, "y", [(i, (i - k) % ycount) for i in range(ycount)]))
        return jnp.concatenate(parts, axis=0)

    gu = gate_up_weight[0]
    gu_send = jnp.stack(
        [
            jnp.concatenate(
                [
                    gu[:, z * slice_ff : (z + 1) * slice_ff],
                    gu[:, FF + z * slice_ff : FF + (z + 1) * slice_ff],
                ],
                axis=1,
            )
            for z in range(Z)
        ]
    )
    down_send = jnp.stack(
        [down_weight[0][:, z * slice_ff : (z + 1) * slice_ff] for z in range(Z)]
    )
    wide_gate_up = across_y(exchange(gu_send, "z").reshape(half, 2 * slice_ff))
    wide_down = across_y(exchange(down_send, "z").reshape(half, slice_ff))

    segment_row = segments[0]
    fill_order = slot_order[0]
    positions = jnp.arange(tok_rows)
    allowed = (positions[:, None] >= positions[None, :]) & (
        segment_row[:, None] == segment_row[None, :]
    )
    table_att = slot_table(att_routes, fill_order, experts)
    table_mlp = slot_table(mlp_routes, fill_order, experts)
    token_att = table_att[:, :tok_rows] + table_att[:, tok_rows:]
    token_mlp = table_mlp[:, :tok_rows] + table_mlp[:, tok_rows:]

    gain_one = small[0:1].astype(F32)
    gain_two = small[1:2].astype(F32)
    router_att = small[2 : 2 + experts]
    router_mlp = small[2 + experts : 2 + 2 * experts]
    inputs = y_major(tokens).astype(F32)
    grad_out = y_major(cotangent).astype(F32)
    scale_one = lax.rsqrt(jnp.mean(inputs * inputs, axis=1, keepdims=True) + EPSILON)
    normed_one = (inputs * scale_one * gain_one).astype(BF16)

    att_slots_in = select_rows(token_att, normed_one).reshape(experts, capacity, D)
    send = jnp.stack(
        [
            jnp.concatenate([s, jnp.broadcast_to(n[None], (experts, tok_rows, half))], axis=1)
            for s, n in zip(halves(att_slots_in), halves(normed_one))
        ],
        axis=1,
    )
    got = exchange(send.reshape(experts * ycount, capacity + tok_rows, half), both)
    query_in = got[:, :capacity].reshape(experts * ycount * capacity, half)
    kv_in = got[:, capacity:].reshape(experts * ycount * tok_rows, half)
    query_part = jnp.dot(query_in, wide_query, preferred_element_type=F32).astype(BF16)
    kv_out = jnp.dot(kv_in, wide_kv, preferred_element_type=F32).astype(BF16)
    back = jnp.concatenate(
        [
            query_part.reshape(experts * ycount, capacity, D),
            pack(kv_out.reshape(experts * ycount, tok_rows, kv_cols)),
        ],
        axis=1,
    )
    back = exchange(back, both).reshape(experts, ycount, 2 * capacity, D)
    summed = jnp.sum(back.astype(F32), axis=1).astype(BF16)
    query_slots = summed[:, :capacity].reshape(2 * tok_rows, D)
    kv_parts = unpack(summed[:, capacity:])
    keyvals = jnp.concatenate([kv_parts[e] for e in range(experts)], axis=-1)
    key_heads = keyvals[:, :D].reshape(tok_rows, HEADS, HEAD_DIM)
    value_heads = keyvals[:, D:].reshape(tok_rows, HEADS, HEAD_DIM)
    router_logits = lax.dot_general(
        normed_one, router_att, CONTRACT_LAST, preferred_element_type=F32
    )
    gate_att = chosen_gates(router_logits, att_routes, experts)
    query_pairs = spread_rows(table_att, query_slots)
    queries = query_pairs.reshape(2, tok_rows, HEADS, HEAD_DIM)
    mixed_heads, log_sums = attend_forward(queries, key_heads, value_heads, allowed)

    def to_rows(v):
        v = v.reshape(experts, 1, capacity, D)
        v = jnp.broadcast_to(v, (experts, ycount, capacity, D))
        return exchange(v.reshape(experts * ycount, capacity, D), both)

    def from_halves(v):
        v = exchange(v.reshape(experts * ycount, capacity, half), both)
        v = v.reshape(experts, ycount, capacity, half)
        return jnp.concatenate([v[:, y] for y in range(ycount)], axis=-1).reshape(2 * tok_rows, D)

    mixed_in = to_rows(select_rows(table_att, mixed_heads)).reshape(-1, D)
    projected = lax.dot_general(
        mixed_in, wide_output, CONTRACT_LAST, preferred_element_type=F32
    ).astype(BF16)
    att_pairs = (
        spread_rows(table_att, from_halves(projected)).astype(F32).reshape(2, tok_rows, D)
    )
    hidden = inputs + gate_att[:, 0:1] * att_pairs[0] + gate_att[:, 1:2] * att_pairs[1]
    scale_two = lax.rsqrt(jnp.mean(hidden * hidden, axis=1, keepdims=True) + EPSILON)
    normed_two = (hidden * scale_two * gain_two).astype(BF16)
    mlp_logits = lax.dot_general(
        normed_two, router_mlp, CONTRACT_LAST, preferred_element_type=F32
    )
    gate_mlp = chosen_gates(mlp_logits, mlp_routes, experts)

    def to_experts(rows):
        slots = jnp.einsum("zts,ztd->zsd", tables, rows, preferred_element_type=F32).astype(BF16)
        return slots.reshape(Z, experts, capacity, D).transpose(1, 0, 2, 3)

    def to_tokens(rows):
        rows = rows.transpose(1, 0, 2, 3).reshape(Z, 2 * tok_rows, D)
        return jnp.einsum("zts,zsd->ztd", tables, rows, preferred_element_type=F32).astype(BF16)

    grads_z = lax.all_gather(
        jnp.concatenate([own_first(y_major(cotangent)), token_mlp.T], axis=1), "z", axis=0
    )
    tables = grads_z[:, :, D:]
    grad_rows = exchange(to_experts(grads_z[:, :, :D]), "expert").reshape(-1, D)
    free_grad = jnp.dot(grad_rows, wide_down, preferred_element_type=F32)

    slot_gates = jnp.sum(
        table_mlp.astype(F32) * jnp.concatenate([gate_mlp[:, 0], gate_mlp[:, 1]])[None], axis=1
    )
    gate_cols = jnp.pad(
        jnp.concatenate(split3(slot_gates.reshape(2, tok_rows).T), axis=1), ((0, 0), (0, 122))
    )
    rows_z = lax.all_gather(
        jnp.concatenate([own_first(normed_two), gate_cols], axis=1), "z", axis=0
    )
    gates_z = rows_z[:, :, D:]
    gates_z = jnp.concatenate([gates_z[:, :, 0:6:2], gates_z[:, :, 1:6:2]], axis=1)
    gates_z = jnp.pad(gates_z, ((0, 0), (0, 0), (0, 125)))
    gates_z = gates_z.reshape(Z, experts, capacity, 128).transpose(1, 0, 2, 3)
    got = exchange(
        jnp.concatenate([to_experts(rows_z[:, :, :D]), gates_z], axis=-1), "expert"
    ).reshape(-1, D + 128)
    ffn_rows = got[:, :D]
    row_gates = jnp.sum(got[:, D : D + 3].astype(F32), axis=1, keepdims=True)
    gate_up = jnp.dot(ffn_rows, wide_gate_up, preferred_element_type=F32)
    gate_part = gate_up[:, :slice_ff]
    up_part = gate_up[:, slice_ff:]
    sigma = jax.nn.sigmoid(gate_part)
    activated = (gate_part * sigma * up_part).astype(BF16)
    act_grad = free_grad * row_gates
    gate_grad = act_grad * up_part * sigma * (1.0 + gate_part * (1.0 - sigma))
    up_grad = act_grad * gate_part * sigma
    gate_up_grad = jnp.concatenate([gate_grad, up_grad], axis=-1).astype(BF16)
    row_part = lax.dot_general(
        gate_up_grad, wide_gate_up, CONTRACT_LAST, preferred_element_type=F32
    ).astype(BF16)
    slot_sums = jnp.sum(activated.astype(F32) * free_grad, axis=1, keepdims=True)
    slot_sums = jnp.pad(jnp.concatenate(split3(slot_sums), axis=1), ((0, 0), (0, 125)))
    back = exchange(
        jnp.concatenate([row_part, slot_sums], axis=1).reshape(
            experts, Z, capacity, D + 128
        ),
        "expert",
    )
    sums = back[..., D : D + 3].transpose(1, 0, 2, 3).reshape(Z, 2 * tok_rows, 3)
    sums = jnp.concatenate([sums[:, :tok_rows], sums[:, tok_rows:]], axis=-1)
    z_index = lax.axis_index("z")
    sums = jnp.concatenate(
        [jnp.where(z_index == z, sums, jnp.zeros_like(sums)) for z in range(Z)], axis=-1
    )
    sums = jnp.pad(sums, ((0, 0), (0, 0), (0, 128 - 6 * Z)))
    back = lax.psum_scatter(
        jnp.concatenate([to_tokens(back[..., :D]), sums], axis=-1).reshape(-1, D + 128),
        "z",
        scatter_dimension=0,
        tiled=True,
    )
    ffn_row_grads = own_first_back(back[:, :D]).astype(F32)
    sums = back[:, D : D + 6 * Z].astype(F32).reshape(tok_rows, Z, 2, 3)
    sums = jnp.sum(sums, axis=(1, 3)).T.reshape(2 * tok_rows, 1)
    gate_mlp_grad = jnp.sum(table_mlp.astype(F32) * sums, axis=0).reshape(2, tok_rows).T

    out_part = (
        row_gates
        * lax.dot_general(activated, wide_down, CONTRACT_LAST, preferred_element_type=F32)
    ).astype(BF16)
    out_part = to_tokens(exchange(out_part.reshape(experts, Z, capacity, D), "expert"))
    ffn_out = lax.psum_scatter(
        out_part.reshape(-1, D), "z", scatter_dimension=0, tiled=True
    )
    block_out = (hidden + own_first_back(ffn_out).astype(F32)).astype(BF16)
    gated_rows = (row_gates * grad_rows.astype(F32)).astype(BF16)

    def outer(left_rows, right_rows):
        return lax.dot_general(left_rows, right_rows, CONTRACT_FIRST, preferred_element_type=F32)

    def ffn_weight_grad(left, right):
        full = outer(left, right)
        own = full[:half]
        for k in range(1, ycount):
            moved = full[k * half : (k + 1) * half].astype(BF16)
            own = own + lax.ppermute(
                moved, "y", [(i, (i + k) % ycount) for i in range(ycount)]
            ).astype(F32)
        cols = right.shape[1]
        return exchange(own.astype(BF16).reshape(Z, part, cols), "z").astype(F32)

    gu_grads = ffn_weight_grad(ffn_rows, gate_up_grad)
    down_grads = ffn_weight_grad(gated_rows, activated)
    gate_up_weight_grad = jnp.concatenate(
        [gu_grads[z, :, :slice_ff] for z in range(Z)]
        + [gu_grads[z, :, slice_ff:] for z in range(Z)],
        axis=1,
    )[None]
    down_weight_grad = jnp.concatenate([down_grads[z] for z in range(Z)], axis=1)[None]

    logit_mlp_grad = gate_logit_grad(gate_mlp, gate_mlp_grad, mlp_routes, experts)
    normed_two_grad = (
        ffn_row_grads
        + jnp.dot(logit_mlp_grad, router_mlp.astype(F32), precision=HIGHEST)
    )
    hidden_grad = grad_out + norm_back(hidden, scale_two, gain_two, normed_two_grad)
    gate_att_grad = jnp.sum(hidden_grad[None] * att_pairs, axis=2).T
    logit_att_grad = gate_logit_grad(gate_att, gate_att_grad, att_routes, experts)
    gated_hidden = jnp.concatenate(
        [gate_att[:, 0:1] * hidden_grad, gate_att[:, 1:2] * hidden_grad], axis=0
    ).astype(BF16)
    hidden_send = select_rows(table_att, gated_hidden).reshape(experts, capacity, D)
    hidden_in = exchange(
        jnp.stack(halves(hidden_send), axis=1).reshape(experts * ycount, capacity, half), both
    ).reshape(-1, half)
    head_part = jnp.dot(hidden_in, wide_output, preferred_element_type=F32).astype(BF16)
    head_part = exchange(head_part.reshape(experts * ycount, capacity, D), both)
    head_slots = jnp.sum(
        head_part.reshape(experts, ycount, capacity, D).astype(F32), axis=1
    ).astype(BF16)
    mixed_grad = spread_rows(table_att, head_slots.reshape(2 * tok_rows, D)).reshape(
        2, tok_rows, HEADS, HEAD_DIM
    )
    output_grad = lax.psum_scatter(
        outer(hidden_in, mixed_in).astype(BF16), "z", scatter_dimension=0, tiled=True
    ).astype(F32)[None]
    query_grad, key_grad, value_grad = attend_backward(
        queries, key_heads, value_heads, allowed, log_sums, mixed_grad
    )
    keyval_row_grad = jnp.concatenate([key_grad, value_grad], axis=1).astype(BF16)
    query_send = select_rows(table_att, query_grad.astype(BF16)).reshape(experts, capacity, D)
    kv_send = pack(
        jnp.stack([keyval_row_grad[:, e * kv_cols : (e + 1) * kv_cols] for e in range(experts)])
    )
    send = jnp.concatenate([query_send, kv_send], axis=1).reshape(experts, 1, 2 * capacity, D)
    send = jnp.broadcast_to(send, (experts, ycount, 2 * capacity, D))
    got = exchange(send.reshape(experts * ycount, 2 * capacity, D), both)
    query_rows = got[:, :capacity].reshape(-1, D)
    kv_rows = unpack(got[:, capacity:]).reshape(-1, kv_cols)
    input_part = lax.dot_general(
        query_rows, wide_query, CONTRACT_LAST, preferred_element_type=F32
    ).astype(BF16)
    normed_part = lax.dot_general(
        kv_rows, wide_kv, CONTRACT_LAST, preferred_element_type=F32
    ).astype(BF16)
    back = jnp.concatenate(
        [
            input_part.reshape(experts * ycount, capacity, half),
            normed_part.reshape(experts * ycount, tok_rows, half),
        ],
        axis=1,
    )
    back = exchange(back, both).reshape(experts, ycount, capacity + tok_rows, half)
    back = jnp.concatenate([back[:, y] for y in range(ycount)], axis=-1)
    input_pairs = (
        spread_rows(table_att, back[:, :capacity].reshape(2 * tok_rows, D))
        .astype(F32)
        .reshape(2, tok_rows, D)
    )
    query_weight_grad = lax.psum_scatter(
        outer(query_in, query_rows).astype(BF16), "z", scatter_dimension=0, tiled=True
    ).astype(F32)[None]
    kv_grad_part = lax.psum_scatter(
        outer(kv_in, kv_rows).astype(BF16), "z", scatter_dimension=0, tiled=True
    )
    keyval_grad = lax.all_gather(kv_grad_part, "expert", axis=1, tiled=True).astype(F32)
    normed_one_grad = (
        input_pairs[0] + input_pairs[1] + jnp.sum(back[:, capacity:].astype(F32), axis=0)
    )
    normed_one_grad = normed_one_grad + jnp.dot(
        logit_att_grad, router_att.astype(F32), precision=HIGHEST
    )
    input_grad = natural(
        hidden_grad + norm_back(inputs, scale_one, gain_one, normed_one_grad)
    )

    small_grads = jnp.concatenate(
        [
            jnp.sum(normed_one_grad * inputs * scale_one, axis=0)[None],
            jnp.sum(normed_two_grad * hidden * scale_two, axis=0)[None],
            lax.dot_general(
                logit_att_grad, normed_one.astype(F32), CONTRACT_FIRST, precision=HIGHEST
            ),
            lax.dot_general(
                logit_mlp_grad, normed_two.astype(F32), CONTRACT_FIRST, precision=HIGHEST
            ),
        ],
        axis=0,
    )
    rows = small_grads.shape[0]
    small_grads = jnp.stack(
        [small_grads[:, i * part : (i + 1) * part] for i in range(Z * ycount)]
    )
    small_grads = jnp.sum(exchange(small_grads, ("y", "z")), axis=0)
    small_grads = lax.psum(small_grads, "expert").T
    gains_grad = small_grads[:, :2]
    router_grad = small_grads[:, 2:rows]
    return (
        natural(block_out),
        input_grad,
        gains_grad,
        keyval_grad,
        router_grad,
        query_weight_grad,
        output_grad,
        gate_up_weight_grad,
        down_weight_grad,
    )


def solution(mesh):
    experts, shards = mesh.shape["expert"], mesh.shape["shard"]
    grid = Mesh(mesh.devices.reshape(experts, Z, shards // Z), ("expert", "z", "y"))
    rows = P(("expert", "z", "y"), None)
    shared = P(("z", "y"), None)
    owned = P("expert", ("z", "y"), None)
    in_specs = (rows,) * 6 + (shared,) * 3 + (owned,) * 4
    out_specs = (rows,) * 2 + (shared,) * 3 + (owned,) * 4
    return jax.shard_map(
        per_device, mesh=grid, in_specs=in_specs, out_specs=out_specs, check_vma=False
    )
```

```python
import jax
import jax.numpy as jnp
from jax import lax
from jax.sharding import Mesh
from jax.sharding import PartitionSpec as P

D = 2048
HEADS = 16
HEAD_DIM = 128
FF = 5632
Z = 4

EPSILON = 1e-05
NEGATIVE = -1e30
HIGHEST = lax.Precision.HIGHEST
CONTRACT_FIRST = (((0,), (0,)), ((), ()))
CONTRACT_LAST = (((1,), (1,)), ((), ()))
BF16 = jnp.bfloat16
F32 = jnp.float32


def slot_table(routes, fill_order, experts):
    pair_count = 2 * routes.shape[0]
    capacity = pair_count // experts
    pair_index = jnp.arange(pair_count, dtype=jnp.int32)
    pair_expert = jnp.concatenate([routes[:, 0], routes[:, 1]]).astype(F32)
    reorder = (fill_order[:, None] == pair_index[None, :]).astype(F32)
    ordered = jnp.dot(reorder, pair_expert, precision=HIGHEST)
    onehot = (ordered[:, None] == jnp.arange(experts, dtype=F32)[None, :]).astype(F32)
    below_mask = (pair_index[:, None] > pair_index[None, :]).astype(F32)
    earlier = jnp.dot(below_mask, onehot, precision=HIGHEST)
    position = jnp.sum(earlier * onehot, axis=1)
    target = ordered * capacity + position
    placing = (
        (target[:, None] == pair_index.astype(F32)[None, :]) & (position < capacity)[:, None]
    ).astype(F32)
    return lax.dot_general(placing, reorder, CONTRACT_FIRST, precision=HIGHEST).astype(BF16)


def select_rows(table, pair_rows):
    return jnp.dot(table, pair_rows, preferred_element_type=F32).astype(BF16)


def spread_rows(table, slot_rows):
    return lax.dot_general(table, slot_rows, CONTRACT_FIRST, preferred_element_type=F32).astype(BF16)


def chosen_gates(logits, routes, experts):
    expert_ids = jnp.arange(experts, dtype=jnp.int32)[None, :]
    first_logit = jnp.sum(jnp.where(routes[:, 0:1] == expert_ids, logits, 0.0), axis=1)
    second_logit = jnp.sum(jnp.where(routes[:, 1:2] == expert_ids, logits, 0.0), axis=1)
    return jax.nn.softmax(jnp.stack([first_logit, second_logit], axis=1), axis=1)


def gate_logit_grad(gate_pair, gate_grad, routes, experts):
    expert_ids = jnp.arange(experts, dtype=jnp.int32)[None, :]
    chosen_grad = gate_pair * (gate_grad - jnp.sum(gate_pair * gate_grad, axis=1, keepdims=True))
    first_part = chosen_grad[:, 0:1] * (routes[:, 0:1] == expert_ids).astype(F32)
    return first_part + chosen_grad[:, 1:2] * (routes[:, 1:2] == expert_ids).astype(F32)


def norm_back(values, scale, gain_row, normed_grad):
    scaled = normed_grad * gain_row
    return scale * (
        scaled - values * scale * scale * jnp.mean(scaled * values, axis=1, keepdims=True)
    )


def attend_forward(queries, key_heads, value_heads, allowed):
    tok_rows = key_heads.shape[0]
    scores = jnp.einsum("kqhd,shd->khqs", queries, key_heads, preferred_element_type=F32) * (
        HEAD_DIM ** (-0.5)
    )
    masked = jnp.where(allowed[None, None], scores, NEGATIVE)
    row_max = jnp.max(masked, axis=-1, keepdims=True)
    exponent = jnp.exp(masked - row_max)
    totals = jnp.sum(exponent, axis=-1, keepdims=True)
    softmax_out = (exponent / totals).astype(BF16)
    mixed = jnp.einsum("khqs,shd->kqhd", softmax_out, value_heads, preferred_element_type=F32)
    mixed = mixed.astype(BF16).reshape(2 * tok_rows, HEADS * HEAD_DIM)
    return mixed, (row_max + jnp.log(totals))[..., 0]


def attend_backward(queries, key_heads, value_heads, allowed, log_sums, mixed_grad):
    tok_rows = key_heads.shape[0]
    scale_factor = HEAD_DIM ** (-0.5)
    scores = (
        jnp.einsum("kqhd,shd->khqs", queries, key_heads, preferred_element_type=F32) * scale_factor
    )
    softmax_out = jnp.where(allowed[None, None], jnp.exp(scores - log_sums[..., None]), 0.0)
    prob_grad = jnp.einsum("kqhd,shd->khqs", mixed_grad, value_heads, preferred_element_type=F32)
    score_grad = (
        softmax_out * (prob_grad - jnp.sum(softmax_out * prob_grad, axis=-1, keepdims=True))
    ).astype(BF16)
    query_grad = (
        jnp.einsum("khqs,shd->kqhd", score_grad, key_heads, preferred_element_type=F32)
        * scale_factor
    )
    key_grad = (
        jnp.einsum("khqs,kqhd->shd", score_grad, queries, preferred_element_type=F32) * scale_factor
    )
    value_grad = jnp.einsum(
        "khqs,kqhd->shd", softmax_out.astype(BF16), mixed_grad, preferred_element_type=F32
    )
    return (
        query_grad.reshape(2 * tok_rows, D),
        key_grad.reshape(tok_rows, D),
        value_grad.reshape(tok_rows, D),
    )


def pick(choices, index):
    result = choices[0]
    for i in range(1, len(choices)):
        result = jnp.where(index == i, choices[i], result)
    return result


def split3(v):
    high = lax.reduce_precision(v, exponent_bits=8, mantissa_bits=7)
    middle = lax.reduce_precision(v - high, exponent_bits=8, mantissa_bits=7)
    return [high.astype(BF16), middle.astype(BF16), (v - high - middle).astype(BF16)]


def after(value, *others):
    return lax.optimization_barrier((value, *others))[0]


def per_device(
    tokens,
    cotangent,
    segments,
    att_routes,
    mlp_routes,
    slot_order,
    norm_gains,
    kv_weight,
    router_weight,
    query_weight,
    output_weight,
    gate_up_weight,
    down_weight,
):
    tok_rows = tokens.shape[0]
    experts = lax.axis_size("expert") * query_weight.shape[0]
    ycount = lax.axis_size("y")
    capacity = 2 * tok_rows // experts
    part = norm_gains.shape[0]
    half = D // ycount
    kv_cols = 2 * D // experts
    slice_ff = FF // Z
    pieces = tok_rows // capacity
    y_index = lax.axis_index("y")
    z_index = lax.axis_index("z")
    e_index = lax.axis_index("expert")

    def y_major(v):
        return jnp.concatenate(
            [
                v[:, (z * ycount + y) * part : (z * ycount + y + 1) * part]
                for y in range(ycount)
                for z in range(Z)
            ],
            axis=1,
        )

    def natural(v):
        return jnp.concatenate(
            [
                v[:, (y * Z + z) * part : (y * Z + z + 1) * part]
                for z in range(Z)
                for y in range(ycount)
            ],
            axis=1,
        )

    def halves(v):
        return [v[..., y * half : (y + 1) * half] for y in range(ycount)]

    def own_first(v):
        h = halves(v)
        return jnp.concatenate(
            [pick([h[(i + k) % ycount] for i in range(ycount)], y_index) for k in range(ycount)],
            axis=-1,
        )

    def own_first_back(v):
        h = halves(v)
        return jnp.concatenate(
            [pick([h[(j - i) % ycount] for i in range(ycount)], y_index) for j in range(ycount)],
            axis=-1,
        )

    def exchange(v, axes):
        return lax.all_to_all(v, axes, split_axis=0, concat_axis=0, tiled=True)

    def pack(v):
        return jnp.concatenate(
            [v[..., i * capacity : (i + 1) * capacity, :] for i in range(pieces)], axis=-1
        )

    def unpack(v):
        return jnp.concatenate(
            [v[..., i * kv_cols : (i + 1) * kv_cols] for i in range(pieces)], axis=-2
        )

    both = ("expert", "y")

    shards = Z * ycount
    small = jnp.concatenate([norm_gains, router_weight], axis=1)
    small = jnp.pad(small, ((0, 0), (0, -small.shape[1] % 16))).T
    small = exchange(jnp.broadcast_to(small[None], (shards, *small.shape)), ("y", "z"))
    small = jnp.concatenate([small[i] for i in range(shards)], axis=1)
    kv_part = lax.dynamic_slice_in_dim(kv_weight, e_index * kv_cols, kv_cols, 1)
    wide_query = lax.all_gather(query_weight[0], "z", axis=0, tiled=True)
    wide_kv = lax.all_gather(kv_part, "z", axis=0, tiled=True)
    wide_output = lax.all_gather(output_weight[0], "z", axis=0, tiled=True)

    def z_shift(v, k):
        return lax.ppermute(v, "z", [(i, (i + k) % Z) for i in range(Z)])

    def y_shift(v, k):
        return lax.ppermute(v, "y", [(i, (i + k) % ycount) for i in range(ycount)])

    def columns(weight, k):
        return lax.dynamic_slice_in_dim(weight, ((z_index + k) % Z) * slice_ff, slice_ff, 1)

    def over_z(blocks):
        return [blocks[0]] + [z_shift(blocks[k], k) for k in range(1, Z)]

    def over_y(blocks):
        return {(j, k): y_shift(blocks[k], ycount - j) for j in range(1, ycount) for k in range(Z)}

    def assemble(own, others):
        wide = jnp.zeros((D, own[0].shape[1]), BF16)
        for j in range(ycount):
            for k in range(Z):
                block = own[k] if j == 0 else others[j, k]
                row = j * half + ((z_index - k) % Z) * part
                wide = lax.dynamic_update_slice_in_dim(wide, block, row, 0)
        return wide

    gate_weight, up_weight = gate_up_weight[0][:, :FF], gate_up_weight[0][:, FF:]
    down_z = over_z([columns(down_weight[0], k) for k in range(Z)])
    gu_z = over_z(
        [
            jnp.concatenate([columns(gate_weight, k), columns(up_weight, k)], axis=1)
            for k in range(Z)
        ]
    )
    down_y = over_y(down_z)
    gu_y = over_y(gu_z)
    wide_down = assemble(down_z, down_y)
    wide_gate_up = assemble(gu_z, gu_y)

    segment_row = segments[0]
    fill_order = slot_order[0]
    positions = jnp.arange(tok_rows)
    allowed = (positions[:, None] >= positions[None, :]) & (
        segment_row[:, None] == segment_row[None, :]
    )
    table_att = slot_table(att_routes, fill_order, experts)
    table_mlp = slot_table(mlp_routes, fill_order, experts)
    token_att = table_att[:, :tok_rows] + table_att[:, tok_rows:]
    token_mlp = table_mlp[:, :tok_rows] + table_mlp[:, tok_rows:]

    gain_one = small[0:1].astype(F32)
    gain_two = small[1:2].astype(F32)
    router_att = small[2 : 2 + experts]
    router_mlp = small[2 + experts : 2 + 2 * experts]
    inputs = y_major(tokens).astype(F32)
    grad_out = y_major(cotangent).astype(F32)
    scale_one = lax.rsqrt(jnp.mean(inputs * inputs, axis=1, keepdims=True) + EPSILON)
    normed_one = (inputs * scale_one * gain_one).astype(BF16)

    def to_experts(rows):
        slots = jnp.einsum("zts,ztd->zsd", tables, rows, preferred_element_type=F32).astype(BF16)
        return slots.reshape(Z, experts, capacity, D).transpose(1, 0, 2, 3)

    def to_tokens(rows):
        rows = rows.transpose(1, 0, 2, 3).reshape(Z, 2 * tok_rows, D)
        return jnp.einsum("zts,zsd->ztd", tables, rows, preferred_element_type=F32).astype(BF16)

    grads_z = lax.all_gather(
        jnp.concatenate([own_first(y_major(cotangent)), token_mlp.T], axis=1), "z", axis=0
    )
    tables = grads_z[:, :, D:]
    grad_rows = exchange(to_experts(grads_z[:, :, :D]), "expert").reshape(-1, D)
    att_slots_in = select_rows(token_att, normed_one).reshape(experts, capacity, D)
    send = jnp.stack(
        [
            jnp.concatenate([s, jnp.broadcast_to(n[None], (experts, tok_rows, half))], axis=1)
            for s, n in zip(halves(att_slots_in), halves(normed_one))
        ],
        axis=1,
    )
    got = exchange(send.reshape(experts * ycount, capacity + tok_rows, half), both)
    query_in = got[:, :capacity].reshape(experts * ycount * capacity, half)
    kv_in = got[:, capacity:].reshape(experts * ycount * tok_rows, half)
    kv_in = after(kv_in, grad_rows, down_z[1])
    query_in = after(query_in, down_z[2], down_z[3], gu_z[1])
    query_part = jnp.dot(query_in, wide_query, preferred_element_type=F32).astype(BF16)
    kv_out = jnp.dot(kv_in, wide_kv, preferred_element_type=F32).astype(BF16)
    back = jnp.concatenate(
        [
            query_part.reshape(experts * ycount, capacity, D),
            pack(kv_out.reshape(experts * ycount, tok_rows, kv_cols)),
        ],
        axis=1,
    )
    back = exchange(back, both).reshape(experts, ycount, 2 * capacity, D)
    back = after(back, gu_z[3])
    summed = jnp.sum(back.astype(F32), axis=1).astype(BF16)
    query_slots = summed[:, :capacity].reshape(2 * tok_rows, D)
    kv_parts = unpack(summed[:, capacity:])
    keyvals = jnp.concatenate([kv_parts[e] for e in range(experts)], axis=-1)
    key_heads = keyvals[:, :D].reshape(tok_rows, HEADS, HEAD_DIM)
    value_heads = keyvals[:, D:].reshape(tok_rows, HEADS, HEAD_DIM)
    router_logits = lax.dot_general(
        normed_one, router_att, CONTRACT_LAST, preferred_element_type=F32
    )
    gate_att = chosen_gates(router_logits, att_routes, experts)
    query_pairs = spread_rows(table_att, query_slots)
    queries = query_pairs.reshape(2, tok_rows, HEADS, HEAD_DIM)
    mixed_heads, log_sums = attend_forward(queries, key_heads, value_heads, allowed)

    def to_rows(v):
        v = v.reshape(experts, 1, capacity, D)
        v = jnp.broadcast_to(v, (experts, ycount, capacity, D))
        return exchange(v.reshape(experts * ycount, capacity, D), both)

    def from_halves(v):
        v = exchange(v.reshape(experts * ycount, capacity, half), both)
        v = v.reshape(experts, ycount, capacity, half)
        return jnp.concatenate([v[:, y] for y in range(ycount)], axis=-1).reshape(2 * tok_rows, D)

    mixed_slots = after(select_rows(table_att, mixed_heads), gu_z[2], *down_y.values())
    mixed_in = to_rows(mixed_slots).reshape(-1, D)
    projected = lax.dot_general(
        mixed_in, wide_output, CONTRACT_LAST, preferred_element_type=F32
    ).astype(BF16)
    att_slots = after(from_halves(projected), *[gu_y[j, k] for j, k in gu_y if k < 2])
    att_pairs = spread_rows(table_att, att_slots).astype(F32).reshape(2, tok_rows, D)
    hidden = inputs + gate_att[:, 0:1] * att_pairs[0] + gate_att[:, 1:2] * att_pairs[1]
    scale_two = lax.rsqrt(jnp.mean(hidden * hidden, axis=1, keepdims=True) + EPSILON)
    normed_two = (hidden * scale_two * gain_two).astype(BF16)
    mlp_logits = lax.dot_general(
        normed_two, router_mlp, CONTRACT_LAST, preferred_element_type=F32
    )
    gate_mlp = chosen_gates(mlp_logits, mlp_routes, experts)

    slot_gates = jnp.sum(
        table_mlp.astype(F32) * jnp.concatenate([gate_mlp[:, 0], gate_mlp[:, 1]])[None], axis=1
    )
    gate_cols = jnp.pad(
        jnp.concatenate(split3(slot_gates.reshape(2, tok_rows).T), axis=1), ((0, 0), (0, 122))
    )
    rows_z = lax.all_gather(
        jnp.concatenate([own_first(normed_two), gate_cols], axis=1), "z", axis=0
    )
    gates_z = rows_z[:, :, D:]
    gates_z = jnp.concatenate([gates_z[:, :, 0:6:2], gates_z[:, :, 1:6:2]], axis=1)
    gates_z = jnp.pad(gates_z, ((0, 0), (0, 0), (0, 125)))
    gates_z = gates_z.reshape(Z, experts, capacity, 128).transpose(1, 0, 2, 3)
    got = exchange(
        jnp.concatenate([to_experts(rows_z[:, :, :D]), gates_z], axis=-1), "expert"
    ).reshape(-1, D + 128)
    ffn_rows = got[:, :D]
    row_gates = jnp.sum(got[:, D : D + 3].astype(F32), axis=1, keepdims=True)
    free_grad = jnp.dot(grad_rows, wide_down, preferred_element_type=F32)
    gate_up = jnp.dot(ffn_rows, wide_gate_up, preferred_element_type=F32)
    gate_part = gate_up[:, :slice_ff]
    up_part = gate_up[:, slice_ff:]
    sigma = jax.nn.sigmoid(gate_part)
    activated = (gate_part * sigma * up_part).astype(BF16)
    act_grad = free_grad * row_gates
    gate_grad = act_grad * up_part * sigma * (1.0 + gate_part * (1.0 - sigma))
    up_grad = act_grad * gate_part * sigma
    gate_up_grad = jnp.concatenate([gate_grad, up_grad], axis=-1).astype(BF16)
    row_part = lax.dot_general(
        gate_up_grad, wide_gate_up, CONTRACT_LAST, preferred_element_type=F32
    ).astype(BF16)
    slot_sums = jnp.sum(activated.astype(F32) * free_grad, axis=1, keepdims=True)
    slot_sums = jnp.pad(jnp.concatenate(split3(slot_sums), axis=1), ((0, 0), (0, 125)))
    back = exchange(
        jnp.concatenate([row_part, slot_sums], axis=1).reshape(
            experts, Z, capacity, D + 128
        ),
        "expert",
    )
    sums = back[..., D : D + 3].transpose(1, 0, 2, 3).reshape(Z, 2 * tok_rows, 3)
    sums = jnp.concatenate([sums[:, :tok_rows], sums[:, tok_rows:]], axis=-1)
    sums = jnp.concatenate(
        [jnp.where(z_index == z, sums, jnp.zeros_like(sums)) for z in range(Z)], axis=-1
    )
    sums = jnp.pad(sums, ((0, 0), (0, 0), (0, 128 - 6 * Z)))
    back = lax.psum_scatter(
        jnp.concatenate([to_tokens(back[..., :D]), sums], axis=-1).reshape(-1, D + 128),
        "z",
        scatter_dimension=0,
        tiled=True,
    )
    ffn_row_grads = own_first_back(back[:, :D]).astype(F32)
    sums = back[:, D : D + 6 * Z].astype(F32).reshape(tok_rows, Z, 2, 3)
    sums = jnp.sum(sums, axis=(1, 3)).T.reshape(2 * tok_rows, 1)
    gate_mlp_grad = jnp.sum(table_mlp.astype(F32) * sums, axis=0).reshape(2, tok_rows).T

    out_part = (
        row_gates
        * lax.dot_general(activated, wide_down, CONTRACT_LAST, preferred_element_type=F32)
    ).astype(BF16)
    out_part = to_tokens(exchange(out_part.reshape(experts, Z, capacity, D), "expert"))
    ffn_out = lax.psum_scatter(
        out_part.reshape(-1, D), "z", scatter_dimension=0, tiled=True
    )
    block_out = (hidden + own_first_back(ffn_out).astype(F32)).astype(BF16)
    gated_rows = (row_gates * grad_rows.astype(F32)).astype(BF16)

    def outer(left_rows, right_rows):
        return lax.dot_general(left_rows, right_rows, CONTRACT_FIRST, preferred_element_type=F32)

    def block(v, k):
        return lax.dynamic_index_in_dim(v, (z_index + k) % Z, 0, keepdims=False)

    def grads_over_y(left, right):
        cols = right.shape[1]
        moved = {}
        for j in range(1, ycount):
            other = outer(left[:, j * half : (j + 1) * half], right).astype(BF16)
            other = other.reshape(Z, part, cols)
            for k in (1, 2, 3, 0):
                moved[j, k] = y_shift(block(other, k), j)
        return moved

    def grads_over_z(left, right, moved):
        own = outer(left[:, :half], right).reshape(Z, part, right.shape[1])
        got = {}
        for k in (1, 2, 3, 0):
            total = block(own, k)
            for j in range(1, ycount):
                total = total + moved[j, k].astype(F32)
            got[k] = total if k == 0 else z_shift(total.astype(BF16), k)
        return got

    def in_order(got):
        return [
            pick([got[(z - i) % Z].astype(F32) for z in range(Z)], z_index) for i in range(Z)
        ]

    gu_moved = grads_over_y(ffn_rows, gate_up_grad)
    down_moved = grads_over_y(gated_rows, activated)
    gu_got = grads_over_z(ffn_rows, gate_up_grad, gu_moved)
    down_got = grads_over_z(gated_rows, activated, down_moved)
    gu_grads = in_order(gu_got)
    gate_up_weight_grad = jnp.concatenate(
        [g[:, :slice_ff] for g in gu_grads] + [g[:, slice_ff:] for g in gu_grads], axis=1
    )[None]
    down_weight_grad = jnp.concatenate(in_order(down_got), axis=1)[None]
    ffn_row_grads = after(ffn_row_grads, *[gu_moved[j, k] for j, k in gu_moved if k in (1, 2)])

    logit_mlp_grad = gate_logit_grad(gate_mlp, gate_mlp_grad, mlp_routes, experts)
    normed_two_grad = (
        ffn_row_grads
        + jnp.dot(logit_mlp_grad, router_mlp.astype(F32), precision=HIGHEST)
    )
    hidden_grad = grad_out + norm_back(hidden, scale_two, gain_two, normed_two_grad)
    gate_att_grad = jnp.sum(hidden_grad[None] * att_pairs, axis=2).T
    logit_att_grad = gate_logit_grad(gate_att, gate_att_grad, att_routes, experts)
    gated_hidden = jnp.concatenate(
        [gate_att[:, 0:1] * hidden_grad, gate_att[:, 1:2] * hidden_grad], axis=0
    ).astype(BF16)
    hidden_send = select_rows(table_att, gated_hidden).reshape(experts, capacity, D)
    hidden_in = exchange(
        jnp.stack(halves(hidden_send), axis=1).reshape(experts * ycount, capacity, half), both
    ).reshape(-1, half)
    hidden_in = after(
        hidden_in, gu_got[1], *[gu_moved[j, k] for j, k in gu_moved], *down_moved.values()
    )
    head_part = jnp.dot(hidden_in, wide_output, preferred_element_type=F32).astype(BF16)
    head_part = exchange(head_part.reshape(experts * ycount, capacity, D), both)
    head_part = after(head_part, gu_got[2])
    head_slots = jnp.sum(
        head_part.reshape(experts, ycount, capacity, D).astype(F32), axis=1
    ).astype(BF16)
    mixed_grad = spread_rows(table_att, head_slots.reshape(2 * tok_rows, D)).reshape(
        2, tok_rows, HEADS, HEAD_DIM
    )
    output_grad = lax.psum_scatter(
        outer(hidden_in, mixed_in).astype(BF16), "z", scatter_dimension=0, tiled=True
    ).astype(F32)[None]
    query_grad, key_grad, value_grad = attend_backward(
        queries, key_heads, value_heads, allowed, log_sums, mixed_grad
    )
    query_grad = after(query_grad, gu_got[3], ffn_out)
    keyval_row_grad = jnp.concatenate([key_grad, value_grad], axis=1).astype(BF16)
    query_send = select_rows(table_att, query_grad.astype(BF16)).reshape(experts, capacity, D)
    kv_send = pack(
        jnp.stack([keyval_row_grad[:, e * kv_cols : (e + 1) * kv_cols] for e in range(experts)])
    )
    send = jnp.concatenate([query_send, kv_send], axis=1).reshape(experts, 1, 2 * capacity, D)
    send = jnp.broadcast_to(send, (experts, ycount, 2 * capacity, D))
    got = exchange(send.reshape(experts * ycount, 2 * capacity, D), both)
    got = after(got, down_got[1], down_got[2], down_got[3], output_grad)
    query_rows = got[:, :capacity].reshape(-1, D)
    kv_rows = unpack(got[:, capacity:]).reshape(-1, kv_cols)
    input_part = lax.dot_general(
        query_rows, wide_query, CONTRACT_LAST, preferred_element_type=F32
    ).astype(BF16)
    normed_part = lax.dot_general(
        kv_rows, wide_kv, CONTRACT_LAST, preferred_element_type=F32
    ).astype(BF16)
    back = jnp.concatenate(
        [
            input_part.reshape(experts * ycount, capacity, half),
            normed_part.reshape(experts * ycount, tok_rows, half),
        ],
        axis=1,
    )
    back = exchange(back, both).reshape(experts, ycount, capacity + tok_rows, half)
    back = jnp.concatenate([back[:, y] for y in range(ycount)], axis=-1)
    input_pairs = (
        spread_rows(table_att, back[:, :capacity].reshape(2 * tok_rows, D))
        .astype(F32)
        .reshape(2, tok_rows, D)
    )
    query_weight_grad = lax.psum_scatter(
        outer(query_in, query_rows).astype(BF16), "z", scatter_dimension=0, tiled=True
    ).astype(F32)[None]
    kv_grad_part = lax.psum_scatter(
        outer(kv_in, kv_rows).astype(BF16), "z", scatter_dimension=0, tiled=True
    )
    keyval_grad = lax.all_gather(kv_grad_part, "expert", axis=1, tiled=True).astype(F32)
    normed_one_grad = (
        input_pairs[0] + input_pairs[1] + jnp.sum(back[:, capacity:].astype(F32), axis=0)
    )
    normed_one_grad = normed_one_grad + jnp.dot(
        logit_att_grad, router_att.astype(F32), precision=HIGHEST
    )
    input_grad = natural(
        hidden_grad + norm_back(inputs, scale_one, gain_one, normed_one_grad)
    )

    small_grads = jnp.concatenate(
        [
            jnp.sum(normed_one_grad * inputs * scale_one, axis=0)[None],
            jnp.sum(normed_two_grad * hidden * scale_two, axis=0)[None],
            lax.dot_general(
                logit_att_grad, normed_one.astype(F32), CONTRACT_FIRST, precision=HIGHEST
            ),
            lax.dot_general(
                logit_mlp_grad, normed_two.astype(F32), CONTRACT_FIRST, precision=HIGHEST
            ),
        ],
        axis=0,
    )
    rows = small_grads.shape[0]
    small_grads = jnp.stack(
        [small_grads[:, i * part : (i + 1) * part] for i in range(Z * ycount)]
    )
    small_grads = jnp.sum(exchange(small_grads, ("y", "z")), axis=0)
    small_grads = lax.psum(small_grads, "expert").T
    gains_grad = small_grads[:, :2]
    router_grad = small_grads[:, 2:rows]
    return (
        natural(block_out),
        input_grad,
        gains_grad,
        keyval_grad,
        router_grad,
        query_weight_grad,
        output_grad,
        gate_up_weight_grad,
        down_weight_grad,
    )


def solution(mesh):
    experts, shards = mesh.shape["expert"], mesh.shape["shard"]
    grid = Mesh(mesh.devices.reshape(experts, Z, shards // Z), ("expert", "z", "y"))
    rows = P(("expert", "z", "y"), None)
    shared = P(("z", "y"), None)
    owned = P("expert", ("z", "y"), None)
    in_specs = (rows,) * 6 + (shared,) * 3 + (owned,) * 4
    out_specs = (rows,) * 2 + (shared,) * 3 + (owned,) * 4
    return jax.shard_map(
        per_device, mesh=grid, in_specs=in_specs, out_specs=out_specs, check_vma=False
    )
```

```python
import jax
import jax.numpy as jnp
from jax import lax
from jax.sharding import Mesh
from jax.sharding import PartitionSpec as P

D = 2048
HEADS = 16
HEAD_DIM = 128
FF = 5632
Z = 4

EPSILON = 1e-05
NEGATIVE = -1e30
HIGHEST = lax.Precision.HIGHEST
CONTRACT_FIRST = (((0,), (0,)), ((), ()))
CONTRACT_LAST = (((1,), (1,)), ((), ()))
BF16 = jnp.bfloat16
F32 = jnp.float32


def slot_table(routes, fill_order, experts):
    pair_count = 2 * routes.shape[0]
    capacity = pair_count // experts
    pair_index = jnp.arange(pair_count, dtype=jnp.int32)
    pair_expert = jnp.concatenate([routes[:, 0], routes[:, 1]]).astype(F32)
    reorder = (fill_order[:, None] == pair_index[None, :]).astype(F32)
    ordered = jnp.dot(reorder, pair_expert, precision=HIGHEST)
    onehot = (ordered[:, None] == jnp.arange(experts, dtype=F32)[None, :]).astype(F32)
    below_mask = (pair_index[:, None] > pair_index[None, :]).astype(F32)
    earlier = jnp.dot(below_mask, onehot, precision=HIGHEST)
    position = jnp.sum(earlier * onehot, axis=1)
    target = ordered * capacity + position
    placing = (
        (target[:, None] == pair_index.astype(F32)[None, :]) & (position < capacity)[:, None]
    ).astype(F32)
    return lax.dot_general(placing, reorder, CONTRACT_FIRST, precision=HIGHEST).astype(BF16)


def select_rows(table, pair_rows):
    return jnp.dot(table, pair_rows, preferred_element_type=F32).astype(BF16)


def spread_rows(table, slot_rows):
    return lax.dot_general(table, slot_rows, CONTRACT_FIRST, preferred_element_type=F32).astype(BF16)


def chosen_gates(logits, routes, experts):
    expert_ids = jnp.arange(experts, dtype=jnp.int32)[None, :]
    first_logit = jnp.sum(jnp.where(routes[:, 0:1] == expert_ids, logits, 0.0), axis=1)
    second_logit = jnp.sum(jnp.where(routes[:, 1:2] == expert_ids, logits, 0.0), axis=1)
    return jax.nn.softmax(jnp.stack([first_logit, second_logit], axis=1), axis=1)


def gate_logit_grad(gate_pair, gate_grad, routes, experts):
    expert_ids = jnp.arange(experts, dtype=jnp.int32)[None, :]
    chosen_grad = gate_pair * (gate_grad - jnp.sum(gate_pair * gate_grad, axis=1, keepdims=True))
    first_part = chosen_grad[:, 0:1] * (routes[:, 0:1] == expert_ids).astype(F32)
    return first_part + chosen_grad[:, 1:2] * (routes[:, 1:2] == expert_ids).astype(F32)


def norm_back(values, scale, gain_row, normed_grad):
    scaled = normed_grad * gain_row
    return scale * (
        scaled - values * scale * scale * jnp.mean(scaled * values, axis=1, keepdims=True)
    )


def attend_forward(queries, key_heads, value_heads, allowed):
    tok_rows = key_heads.shape[0]
    scores = jnp.einsum("kqhd,shd->khqs", queries, key_heads, preferred_element_type=F32) * (
        HEAD_DIM ** (-0.5)
    )
    masked = jnp.where(allowed[None, None], scores, NEGATIVE)
    row_max = jnp.max(masked, axis=-1, keepdims=True)
    exponent = jnp.exp(masked - row_max)
    totals = jnp.sum(exponent, axis=-1, keepdims=True)
    softmax_out = (exponent / totals).astype(BF16)
    mixed = jnp.einsum("khqs,shd->kqhd", softmax_out, value_heads, preferred_element_type=F32)
    mixed = mixed.astype(BF16).reshape(2 * tok_rows, HEADS * HEAD_DIM)
    return mixed, (row_max + jnp.log(totals))[..., 0]


def attend_backward(queries, key_heads, value_heads, allowed, log_sums, mixed_grad):
    tok_rows = key_heads.shape[0]
    scale_factor = HEAD_DIM ** (-0.5)
    scores = (
        jnp.einsum("kqhd,shd->khqs", queries, key_heads, preferred_element_type=F32) * scale_factor
    )
    softmax_out = jnp.where(allowed[None, None], jnp.exp(scores - log_sums[..., None]), 0.0)
    prob_grad = jnp.einsum("kqhd,shd->khqs", mixed_grad, value_heads, preferred_element_type=F32)
    score_grad = (
        softmax_out * (prob_grad - jnp.sum(softmax_out * prob_grad, axis=-1, keepdims=True))
    ).astype(BF16)
    query_grad = (
        jnp.einsum("khqs,shd->kqhd", score_grad, key_heads, preferred_element_type=F32)
        * scale_factor
    )
    key_grad = (
        jnp.einsum("khqs,kqhd->shd", score_grad, queries, preferred_element_type=F32) * scale_factor
    )
    value_grad = jnp.einsum(
        "khqs,kqhd->shd", softmax_out.astype(BF16), mixed_grad, preferred_element_type=F32
    )
    return (
        query_grad.reshape(2 * tok_rows, D),
        key_grad.reshape(tok_rows, D),
        value_grad.reshape(tok_rows, D),
    )


def pick(choices, index):
    result = choices[0]
    for i in range(1, len(choices)):
        result = jnp.where(index == i, choices[i], result)
    return result


def split3(v):
    high = lax.reduce_precision(v, exponent_bits=8, mantissa_bits=7)
    middle = lax.reduce_precision(v - high, exponent_bits=8, mantissa_bits=7)
    return [high.astype(BF16), middle.astype(BF16), (v - high - middle).astype(BF16)]


def after(value, *others):
    return lax.optimization_barrier((value, *others))[0]


def per_device(
    tokens,
    cotangent,
    segments,
    att_routes,
    mlp_routes,
    slot_order,
    norm_gains,
    kv_weight,
    router_weight,
    query_weight,
    output_weight,
    gate_up_weight,
    down_weight,
):
    tok_rows = tokens.shape[0]
    experts = lax.axis_size("expert") * query_weight.shape[0]
    ycount = lax.axis_size("y")
    capacity = 2 * tok_rows // experts
    part = norm_gains.shape[0]
    half = D // ycount
    kv_cols = 2 * D // experts
    slice_ff = FF // Z
    pieces = tok_rows // capacity
    y_index = lax.axis_index("y")
    z_index = lax.axis_index("z")
    e_index = lax.axis_index("expert")

    def y_major(v):
        return jnp.concatenate(
            [
                v[:, (z * ycount + y) * part : (z * ycount + y + 1) * part]
                for y in range(ycount)
                for z in range(Z)
            ],
            axis=1,
        )

    def natural(v):
        return jnp.concatenate(
            [
                v[:, (y * Z + z) * part : (y * Z + z + 1) * part]
                for z in range(Z)
                for y in range(ycount)
            ],
            axis=1,
        )

    def halves(v):
        return [v[..., y * half : (y + 1) * half] for y in range(ycount)]

    def own_first(v):
        h = halves(v)
        return jnp.concatenate(
            [pick([h[(i + k) % ycount] for i in range(ycount)], y_index) for k in range(ycount)],
            axis=-1,
        )

    def own_first_back(v):
        h = halves(v)
        return jnp.concatenate(
            [pick([h[(j - i) % ycount] for i in range(ycount)], y_index) for j in range(ycount)],
            axis=-1,
        )

    def exchange(v, axes):
        return lax.all_to_all(v, axes, split_axis=0, concat_axis=0, tiled=True)

    def pack(v):
        return jnp.concatenate(
            [v[..., i * capacity : (i + 1) * capacity, :] for i in range(pieces)], axis=-1
        )

    def unpack(v):
        return jnp.concatenate(
            [v[..., i * kv_cols : (i + 1) * kv_cols] for i in range(pieces)], axis=-2
        )

    both = ("expert", "y")
    js = range(1, ycount)

    shards = Z * ycount
    small = jnp.concatenate([norm_gains, router_weight], axis=1)
    small = jnp.pad(small, ((0, 0), (0, -small.shape[1] % 16))).T
    small = exchange(jnp.broadcast_to(small[None], (shards, *small.shape)), ("y", "z"))
    small = jnp.concatenate([small[i] for i in range(shards)], axis=1)
    kv_part = lax.dynamic_slice_in_dim(kv_weight, e_index * kv_cols, kv_cols, 1)
    wide_both = lax.all_gather(
        jnp.concatenate([query_weight[0], kv_part], axis=1), "z", axis=0, tiled=True
    )
    wide_query, wide_kv = wide_both[:, :D], wide_both[:, D:]
    wide_output = lax.all_gather(output_weight[0], "z", axis=0, tiled=True)

    def z_shift(v, k):
        return lax.ppermute(v, "z", [(i, (i + k) % Z) for i in range(Z)])

    def y_shift(v, k):
        return lax.ppermute(v, "y", [(i, (i + k) % ycount) for i in range(ycount)])

    def columns(weight, k):
        return lax.dynamic_slice_in_dim(weight, ((z_index + k) % Z) * slice_ff, slice_ff, 1)

    def over_z(blocks):
        return [blocks[0]] + [z_shift(blocks[k], k) for k in range(1, Z)]

    def over_y(blocks):
        return {(j, k): y_shift(blocks[k], ycount - j) for j in range(1, ycount) for k in range(Z)}

    def assemble(own, others):
        wide = jnp.zeros((D, own[0].shape[1]), BF16)
        for j in range(ycount):
            for k in range(Z):
                block = own[k] if j == 0 else others[j, k]
                row = j * half + ((z_index - k) % Z) * part
                wide = lax.dynamic_update_slice_in_dim(wide, block, row, 0)
        return wide

    gate_weight, up_weight = gate_up_weight[0][:, :FF], gate_up_weight[0][:, FF:]
    down_z = over_z([columns(down_weight[0], k) for k in range(Z)])
    gu_z = over_z(
        [
            jnp.concatenate([columns(gate_weight, k), columns(up_weight, k)], axis=1)
            for k in range(Z)
        ]
    )
    down_y = over_y(down_z)
    gu_y = over_y(gu_z)
    wide_down = assemble(down_z, down_y)
    wide_gate_up = assemble(gu_z, gu_y)

    segment_row = segments[0]
    fill_order = slot_order[0]
    positions = jnp.arange(tok_rows)
    allowed = (positions[:, None] >= positions[None, :]) & (
        segment_row[:, None] == segment_row[None, :]
    )
    table_att = slot_table(att_routes, fill_order, experts)
    table_mlp = slot_table(mlp_routes, fill_order, experts)
    token_att = table_att[:, :tok_rows] + table_att[:, tok_rows:]
    token_mlp = table_mlp[:, :tok_rows] + table_mlp[:, tok_rows:]

    gain_one = small[0:1].astype(F32)
    gain_two = small[1:2].astype(F32)
    router_att = small[2 : 2 + experts]
    router_mlp = small[2 + experts : 2 + 2 * experts]
    inputs = y_major(tokens).astype(F32)
    grad_out = y_major(cotangent).astype(F32)
    scale_one = lax.rsqrt(jnp.mean(inputs * inputs, axis=1, keepdims=True) + EPSILON)
    normed_one = (inputs * scale_one * gain_one).astype(BF16)

    def to_experts(rows):
        slots = jnp.einsum("zts,ztd->zsd", tables, rows, preferred_element_type=F32).astype(BF16)
        return slots.reshape(Z, experts, capacity, D).transpose(1, 0, 2, 3)

    def to_tokens(rows):
        rows = rows.transpose(1, 0, 2, 3).reshape(Z, 2 * tok_rows, D)
        return jnp.einsum("zts,zsd->ztd", tables, rows, preferred_element_type=F32).astype(BF16)

    grads_z = lax.all_gather(
        jnp.concatenate([own_first(y_major(cotangent)), token_mlp.T], axis=1), "z", axis=0
    )
    tables = grads_z[:, :, D:]
    grad_rows = exchange(to_experts(grads_z[:, :, :D]), "expert").reshape(-1, D)
    att_slots_in = select_rows(token_att, normed_one).reshape(experts, capacity, D)
    send = jnp.stack(
        [
            jnp.concatenate([s, jnp.broadcast_to(n[None], (experts, tok_rows, half))], axis=1)
            for s, n in zip(halves(att_slots_in), halves(normed_one))
        ],
        axis=1,
    )
    got = exchange(send.reshape(experts * ycount, capacity + tok_rows, half), both)
    query_in = got[:, :capacity].reshape(experts * ycount * capacity, half)
    kv_in = got[:, capacity:].reshape(experts * ycount * tok_rows, half)
    own_y = [gu_y[j, k] for j, k in gu_y if k == 0] + [down_y[j, k] for j, k in gu_y if k == 0]
    query_in, kv_in = lax.optimization_barrier(
        (query_in, kv_in, down_z[2], gu_z[2], *own_y)
    )[:2]
    query_part = jnp.dot(query_in, wide_query, preferred_element_type=F32).astype(BF16)
    kv_out = jnp.dot(kv_in, wide_kv, preferred_element_type=F32).astype(BF16)
    back = jnp.concatenate(
        [
            query_part.reshape(experts * ycount, capacity, D),
            pack(kv_out.reshape(experts * ycount, tok_rows, kv_cols)),
        ],
        axis=1,
    )
    back = exchange(back, both).reshape(experts, ycount, 2 * capacity, D)
    summed = jnp.sum(back.astype(F32), axis=1).astype(BF16)
    query_slots = summed[:, :capacity].reshape(2 * tok_rows, D)
    kv_parts = unpack(summed[:, capacity:])
    keyvals = jnp.concatenate([kv_parts[e] for e in range(experts)], axis=-1)
    key_heads = keyvals[:, :D].reshape(tok_rows, HEADS, HEAD_DIM)
    value_heads = keyvals[:, D:].reshape(tok_rows, HEADS, HEAD_DIM)
    router_logits = lax.dot_general(
        normed_one, router_att, CONTRACT_LAST, preferred_element_type=F32
    )
    gate_att = chosen_gates(router_logits, att_routes, experts)
    query_pairs = spread_rows(table_att, query_slots)
    queries = query_pairs.reshape(2, tok_rows, HEADS, HEAD_DIM)
    mixed_heads, log_sums = attend_forward(queries, key_heads, value_heads, allowed)

    def to_rows(v):
        v = v.reshape(experts, 1, capacity, D)
        v = jnp.broadcast_to(v, (experts, ycount, capacity, D))
        return exchange(v.reshape(experts * ycount, capacity, D), both)

    def from_halves(v):
        v = exchange(v.reshape(experts * ycount, capacity, half), both)
        v = v.reshape(experts, ycount, capacity, half)
        return jnp.concatenate([v[:, y] for y in range(ycount)], axis=-1).reshape(2 * tok_rows, D)

    mixed_slots = after(
        select_rows(table_att, mixed_heads), down_z[1], down_z[3], *[down_y[j, 2] for j in js]
    )
    mixed_in = to_rows(mixed_slots).reshape(-1, D)
    projected = lax.dot_general(
        mixed_in, wide_output, CONTRACT_LAST, preferred_element_type=F32
    ).astype(BF16)
    att_slots = after(from_halves(projected), gu_z[1], *[gu_y[j, 2] for j in js])
    att_pairs = spread_rows(table_att, att_slots).astype(F32).reshape(2, tok_rows, D)
    hidden = inputs + gate_att[:, 0:1] * att_pairs[0] + gate_att[:, 1:2] * att_pairs[1]
    scale_two = lax.rsqrt(jnp.mean(hidden * hidden, axis=1, keepdims=True) + EPSILON)
    normed_two = (hidden * scale_two * gain_two).astype(BF16)
    mlp_logits = lax.dot_general(
        normed_two, router_mlp, CONTRACT_LAST, preferred_element_type=F32
    )
    gate_mlp = chosen_gates(mlp_logits, mlp_routes, experts)

    slot_gates = jnp.sum(
        table_mlp.astype(F32) * jnp.concatenate([gate_mlp[:, 0], gate_mlp[:, 1]])[None], axis=1
    )
    gate_cols = jnp.pad(
        jnp.concatenate(split3(slot_gates.reshape(2, tok_rows).T), axis=1), ((0, 0), (0, 122))
    )
    rows_z = lax.all_gather(
        jnp.concatenate([own_first(normed_two), gate_cols], axis=1), "z", axis=0
    )
    rows_z = after(
        rows_z, gu_z[3], grad_rows, *[down_y[j, k] for j in js for k in (1, 3)],
        *[gu_y[j, 1] for j in js],
    )
    gates_z = rows_z[:, :, D:]
    gates_z = jnp.concatenate([gates_z[:, :, 0:6:2], gates_z[:, :, 1:6:2]], axis=1)
    gates_z = jnp.pad(gates_z, ((0, 0), (0, 0), (0, 125)))
    gates_z = gates_z.reshape(Z, experts, capacity, 128).transpose(1, 0, 2, 3)
    got = exchange(
        jnp.concatenate([to_experts(rows_z[:, :, :D]), gates_z], axis=-1), "expert"
    ).reshape(-1, D + 128)
    free_grad = jnp.dot(grad_rows, wide_down, preferred_element_type=F32)
    got = after(got, free_grad)
    ffn_rows = got[:, :D]
    row_gates = jnp.sum(got[:, D : D + 3].astype(F32), axis=1, keepdims=True)
    gate_up = jnp.dot(ffn_rows, wide_gate_up, preferred_element_type=F32)
    gate_part = gate_up[:, :slice_ff]
    up_part = gate_up[:, slice_ff:]
    sigma = jax.nn.sigmoid(gate_part)
    activated = (gate_part * sigma * up_part).astype(BF16)
    act_grad = free_grad * row_gates
    gate_grad = act_grad * up_part * sigma * (1.0 + gate_part * (1.0 - sigma))
    up_grad = act_grad * gate_part * sigma
    gate_up_grad = jnp.concatenate([gate_grad, up_grad], axis=-1).astype(BF16)
    row_part = lax.dot_general(
        gate_up_grad, wide_gate_up, CONTRACT_LAST, preferred_element_type=F32
    ).astype(BF16)
    def outer(left_rows, right_rows):
        return lax.dot_general(left_rows, right_rows, CONTRACT_FIRST, preferred_element_type=F32)

    def block(v, k):
        return lax.dynamic_index_in_dim(v, (z_index + k) % Z, 0, keepdims=False)

    def grads_over_y(left, right):
        cols = right.shape[1]
        moved = {}
        for j in range(1, ycount):
            other = outer(left[:, j * half : (j + 1) * half], right).astype(BF16)
            other = other.reshape(Z, part, cols)
            for k in (1, 2, 3, 0):
                moved[j, k] = y_shift(block(other, k), j)
        return moved

    gated_rows = (row_gates * grad_rows.astype(F32)).astype(BF16)
    gu_moved = grads_over_y(ffn_rows, gate_up_grad)
    down_moved = grads_over_y(gated_rows, activated)
    slot_sums = jnp.sum(activated.astype(F32) * free_grad, axis=1, keepdims=True)
    slot_sums = jnp.pad(jnp.concatenate(split3(slot_sums), axis=1), ((0, 0), (0, 125)))
    back = exchange(
        jnp.concatenate([row_part, slot_sums], axis=1).reshape(
            experts, Z, capacity, D + 128
        ),
        "expert",
    )
    back = after(back, *[down_moved[j, k] for j in js for k in (1, 2)])
    sums = back[..., D : D + 3].transpose(1, 0, 2, 3).reshape(Z, 2 * tok_rows, 3)
    sums = jnp.concatenate([sums[:, :tok_rows], sums[:, tok_rows:]], axis=-1)
    sums = jnp.concatenate(
        [jnp.where(z_index == z, sums, jnp.zeros_like(sums)) for z in range(Z)], axis=-1
    )
    sums = jnp.pad(sums, ((0, 0), (0, 0), (0, 128 - 6 * Z)))
    row_back = back
    back = lax.psum_scatter(
        jnp.concatenate([to_tokens(back[..., :D]), sums], axis=-1).reshape(-1, D + 128),
        "z",
        scatter_dimension=0,
        tiled=True,
    )
    ffn_row_grads = own_first_back(back[:, :D]).astype(F32)
    sums = back[:, D : D + 6 * Z].astype(F32).reshape(tok_rows, Z, 2, 3)
    sums = jnp.sum(sums, axis=(1, 3)).T.reshape(2 * tok_rows, 1)
    gate_mlp_grad = jnp.sum(table_mlp.astype(F32) * sums, axis=0).reshape(2, tok_rows).T

    out_part = (
        row_gates
        * lax.dot_general(after(activated, row_back), wide_down, CONTRACT_LAST, preferred_element_type=F32)
    ).astype(BF16)
    out_part = to_tokens(exchange(out_part.reshape(experts, Z, capacity, D), "expert"))
    ffn_out = lax.psum_scatter(
        out_part.reshape(-1, D), "z", scatter_dimension=0, tiled=True
    )

    def grads_over_z(left, right, moved):
        own = outer(left[:, :half], right).reshape(Z, part, right.shape[1])
        got = {}
        for k in (1, 2, 3, 0):
            total = block(own, k)
            for j in range(1, ycount):
                total = total + moved[j, k].astype(F32)
            got[k] = total if k == 0 else z_shift(total.astype(BF16), k)
        return got

    def in_order(got):
        return [
            pick([got[(z - i) % Z].astype(F32) for z in range(Z)], z_index) for i in range(Z)
        ]

    gu_got = grads_over_z(ffn_rows, gate_up_grad, gu_moved)
    down_got = grads_over_z(gated_rows, activated, down_moved)
    gu_grads = in_order(gu_got)
    gate_up_weight_grad = jnp.concatenate(
        [g[:, :slice_ff] for g in gu_grads] + [g[:, slice_ff:] for g in gu_grads], axis=1
    )[None]
    down_weight_grad = jnp.concatenate(in_order(down_got), axis=1)[None]
    ffn_row_grads = after(
        ffn_row_grads,
        *[gu_moved[j, k] for j in js for k in (1, 2)],
        *[down_moved[j, k] for j in js for k in (3, 0)],
    )

    logit_mlp_grad = gate_logit_grad(gate_mlp, gate_mlp_grad, mlp_routes, experts)
    normed_two_grad = (
        ffn_row_grads
        + jnp.dot(logit_mlp_grad, router_mlp.astype(F32), precision=HIGHEST)
    )
    hidden_grad = grad_out + norm_back(hidden, scale_two, gain_two, normed_two_grad)
    gate_att_grad = jnp.sum(hidden_grad[None] * att_pairs, axis=2).T
    logit_att_grad = gate_logit_grad(gate_att, gate_att_grad, att_routes, experts)
    gated_hidden = jnp.concatenate(
        [gate_att[:, 0:1] * hidden_grad, gate_att[:, 1:2] * hidden_grad], axis=0
    ).astype(BF16)
    hidden_send = select_rows(table_att, gated_hidden).reshape(experts, capacity, D)
    hidden_in = exchange(
        jnp.stack(halves(hidden_send), axis=1).reshape(experts * ycount, capacity, half), both
    ).reshape(-1, half)
    hidden_in = after(hidden_in, *[down_got[k] for k in (1, 2, 3)], *[gu_moved[j, 3] for j in js])
    head_part = jnp.dot(hidden_in, wide_output, preferred_element_type=F32).astype(BF16)
    head_part = exchange(head_part.reshape(experts * ycount, capacity, D), both)
    head_part = after(head_part, gu_got[1], *[gu_moved[j, 0] for j in js])
    head_slots = jnp.sum(
        head_part.reshape(experts, ycount, capacity, D).astype(F32), axis=1
    ).astype(BF16)
    mixed_grad = spread_rows(table_att, head_slots.reshape(2 * tok_rows, D)).reshape(
        2, tok_rows, HEADS, HEAD_DIM
    )
    output_grad = lax.psum_scatter(
        outer(hidden_in, mixed_in).astype(BF16), "z", scatter_dimension=0, tiled=True
    ).astype(F32)[None]
    query_grad, key_grad, value_grad = attend_backward(
        queries, key_heads, value_heads, allowed, log_sums, mixed_grad
    )
    query_grad = after(query_grad, gu_got[2])
    keyval_row_grad = jnp.concatenate([key_grad, value_grad], axis=1).astype(BF16)
    query_send = select_rows(table_att, query_grad.astype(BF16)).reshape(experts, capacity, D)
    kv_send = pack(
        jnp.stack([keyval_row_grad[:, e * kv_cols : (e + 1) * kv_cols] for e in range(experts)])
    )
    send = jnp.concatenate([query_send, kv_send], axis=1).reshape(experts, 1, 2 * capacity, D)
    send = jnp.broadcast_to(send, (experts, ycount, 2 * capacity, D))
    got = exchange(send.reshape(experts * ycount, 2 * capacity, D), both)
    got = after(got, gu_got[3], output_grad)
    block_out = (hidden + own_first_back(after(ffn_out, got)).astype(F32)).astype(BF16)
    query_rows = got[:, :capacity].reshape(-1, D)
    kv_rows = unpack(got[:, capacity:]).reshape(-1, kv_cols)
    input_part = lax.dot_general(
        query_rows, wide_query, CONTRACT_LAST, preferred_element_type=F32
    ).astype(BF16)
    normed_part = lax.dot_general(
        kv_rows, wide_kv, CONTRACT_LAST, preferred_element_type=F32
    ).astype(BF16)
    back = jnp.concatenate(
        [
            input_part.reshape(experts * ycount, capacity, half),
            normed_part.reshape(experts * ycount, tok_rows, half),
        ],
        axis=1,
    )
    back = exchange(back, both).reshape(experts, ycount, capacity + tok_rows, half)
    back = jnp.concatenate([back[:, y] for y in range(ycount)], axis=-1)
    input_pairs = (
        spread_rows(table_att, back[:, :capacity].reshape(2 * tok_rows, D))
        .astype(F32)
        .reshape(2, tok_rows, D)
    )
    query_weight_grad = lax.psum_scatter(
        outer(query_in, query_rows).astype(BF16), "z", scatter_dimension=0, tiled=True
    ).astype(F32)[None]
    kv_grad_part = lax.psum_scatter(
        outer(kv_in, kv_rows).astype(BF16), "z", scatter_dimension=0, tiled=True
    )
    keyval_grad = lax.all_gather(kv_grad_part, "expert", axis=1, tiled=True).astype(F32)
    normed_one_grad = (
        input_pairs[0] + input_pairs[1] + jnp.sum(back[:, capacity:].astype(F32), axis=0)
    )
    normed_one_grad = normed_one_grad + jnp.dot(
        logit_att_grad, router_att.astype(F32), precision=HIGHEST
    )
    input_grad = natural(
        hidden_grad + norm_back(inputs, scale_one, gain_one, normed_one_grad)
    )

    small_grads = jnp.concatenate(
        [
            jnp.sum(normed_one_grad * inputs * scale_one, axis=0)[None],
            jnp.sum(normed_two_grad * hidden * scale_two, axis=0)[None],
            lax.dot_general(
                logit_att_grad, normed_one.astype(F32), CONTRACT_FIRST, precision=HIGHEST
            ),
            lax.dot_general(
                logit_mlp_grad, normed_two.astype(F32), CONTRACT_FIRST, precision=HIGHEST
            ),
        ],
        axis=0,
    )
    rows = small_grads.shape[0]
    small_grads = jnp.stack(
        [small_grads[:, i * part : (i + 1) * part] for i in range(Z * ycount)]
    )
    small_grads = jnp.sum(exchange(small_grads, ("y", "z")), axis=0)
    small_grads = lax.psum(small_grads, "expert").T
    gains_grad = small_grads[:, :2]
    router_grad = small_grads[:, 2:rows]
    return (
        natural(block_out),
        input_grad,
        gains_grad,
        keyval_grad,
        router_grad,
        query_weight_grad,
        output_grad,
        gate_up_weight_grad,
        down_weight_grad,
    )


def solution(mesh):
    experts, shards = mesh.shape["expert"], mesh.shape["shard"]
    grid = Mesh(mesh.devices.reshape(experts, Z, shards // Z), ("expert", "z", "y"))
    rows = P(("expert", "z", "y"), None)
    shared = P(("z", "y"), None)
    owned = P("expert", ("z", "y"), None)
    in_specs = (rows,) * 6 + (shared,) * 3 + (owned,) * 4
    out_specs = (rows,) * 2 + (shared,) * 3 + (owned,) * 4
    return jax.shard_map(
        per_device, mesh=grid, in_specs=in_specs, out_specs=out_specs, check_vma=False
    )
```

```python
import jax
import jax.numpy as jnp
from jax import lax
from jax.sharding import Mesh
from jax.sharding import PartitionSpec as P

D = 2048
HEADS = 16
HEAD_DIM = 128
FF = 5632
Z = 4

EPSILON = 1e-05
NEGATIVE = -1e30
HIGHEST = lax.Precision.HIGHEST
CONTRACT_FIRST = (((0,), (0,)), ((), ()))
CONTRACT_LAST = (((1,), (1,)), ((), ()))
BF16 = jnp.bfloat16
F32 = jnp.float32


def slot_table(routes, fill_order, experts):
    pair_count = 2 * routes.shape[0]
    capacity = pair_count // experts
    pair_index = jnp.arange(pair_count, dtype=jnp.int32)
    pair_expert = jnp.concatenate([routes[:, 0], routes[:, 1]]).astype(F32)
    reorder = (fill_order[:, None] == pair_index[None, :]).astype(F32)
    ordered = jnp.dot(reorder, pair_expert, precision=HIGHEST)
    onehot = (ordered[:, None] == jnp.arange(experts, dtype=F32)[None, :]).astype(F32)
    below_mask = (pair_index[:, None] > pair_index[None, :]).astype(F32)
    earlier = jnp.dot(below_mask, onehot, precision=HIGHEST)
    position = jnp.sum(earlier * onehot, axis=1)
    target = ordered * capacity + position
    placing = (
        (target[:, None] == pair_index.astype(F32)[None, :]) & (position < capacity)[:, None]
    ).astype(F32)
    return lax.dot_general(placing, reorder, CONTRACT_FIRST, precision=HIGHEST).astype(BF16)


def select_rows(table, pair_rows):
    return jnp.dot(table, pair_rows, preferred_element_type=F32).astype(BF16)


def spread_rows(table, slot_rows):
    return lax.dot_general(table, slot_rows, CONTRACT_FIRST, preferred_element_type=F32).astype(BF16)


def chosen_gates(logits, routes, experts):
    expert_ids = jnp.arange(experts, dtype=jnp.int32)[None, :]
    first_logit = jnp.sum(jnp.where(routes[:, 0:1] == expert_ids, logits, 0.0), axis=1)
    second_logit = jnp.sum(jnp.where(routes[:, 1:2] == expert_ids, logits, 0.0), axis=1)
    return jax.nn.softmax(jnp.stack([first_logit, second_logit], axis=1), axis=1)


def gate_logit_grad(gate_pair, gate_grad, routes, experts):
    expert_ids = jnp.arange(experts, dtype=jnp.int32)[None, :]
    chosen_grad = gate_pair * (gate_grad - jnp.sum(gate_pair * gate_grad, axis=1, keepdims=True))
    first_part = chosen_grad[:, 0:1] * (routes[:, 0:1] == expert_ids).astype(F32)
    return first_part + chosen_grad[:, 1:2] * (routes[:, 1:2] == expert_ids).astype(F32)


def norm_back(values, scale, gain_row, normed_grad):
    scaled = normed_grad * gain_row
    return scale * (
        scaled - values * scale * scale * jnp.mean(scaled * values, axis=1, keepdims=True)
    )


def attend_forward(queries, key_heads, value_heads, allowed):
    tok_rows = key_heads.shape[0]
    scores = jnp.einsum("kqhd,shd->khqs", queries, key_heads, preferred_element_type=F32) * (
        HEAD_DIM ** (-0.5)
    )
    masked = jnp.where(allowed[None, None], scores, NEGATIVE)
    row_max = jnp.max(masked, axis=-1, keepdims=True)
    exponent = jnp.exp(masked - row_max)
    totals = jnp.sum(exponent, axis=-1, keepdims=True)
    softmax_out = (exponent / totals).astype(BF16)
    mixed = jnp.einsum("khqs,shd->kqhd", softmax_out, value_heads, preferred_element_type=F32)
    mixed = mixed.astype(BF16).reshape(2 * tok_rows, HEADS * HEAD_DIM)
    return mixed, (row_max + jnp.log(totals))[..., 0]


def attend_backward(queries, key_heads, value_heads, allowed, log_sums, mixed_grad):
    tok_rows = key_heads.shape[0]
    scale_factor = HEAD_DIM ** (-0.5)
    scores = (
        jnp.einsum("kqhd,shd->khqs", queries, key_heads, preferred_element_type=F32) * scale_factor
    )
    softmax_out = jnp.where(allowed[None, None], jnp.exp(scores - log_sums[..., None]), 0.0)
    prob_grad = jnp.einsum("kqhd,shd->khqs", mixed_grad, value_heads, preferred_element_type=F32)
    score_grad = (
        softmax_out * (prob_grad - jnp.sum(softmax_out * prob_grad, axis=-1, keepdims=True))
    ).astype(BF16)
    query_grad = (
        jnp.einsum("khqs,shd->kqhd", score_grad, key_heads, preferred_element_type=F32)
        * scale_factor
    )
    key_grad = (
        jnp.einsum("khqs,kqhd->shd", score_grad, queries, preferred_element_type=F32) * scale_factor
    )
    value_grad = jnp.einsum(
        "khqs,kqhd->shd", softmax_out.astype(BF16), mixed_grad, preferred_element_type=F32
    )
    return (
        query_grad.reshape(2 * tok_rows, D),
        key_grad.reshape(tok_rows, D),
        value_grad.reshape(tok_rows, D),
    )


def pick(choices, index):
    result = choices[0]
    for i in range(1, len(choices)):
        result = jnp.where(index == i, choices[i], result)
    return result


def split3(v):
    high = lax.reduce_precision(v, exponent_bits=8, mantissa_bits=7)
    middle = lax.reduce_precision(v - high, exponent_bits=8, mantissa_bits=7)
    return [high.astype(BF16), middle.astype(BF16), (v - high - middle).astype(BF16)]


def after(value, *others):
    return lax.optimization_barrier((value, *others))[0]


def per_device(
    tokens,
    cotangent,
    segments,
    att_routes,
    mlp_routes,
    slot_order,
    norm_gains,
    kv_weight,
    router_weight,
    query_weight,
    output_weight,
    gate_up_weight,
    down_weight,
):
    tok_rows = tokens.shape[0]
    experts = lax.axis_size("expert") * query_weight.shape[0]
    ycount = lax.axis_size("y")
    capacity = 2 * tok_rows // experts
    part = norm_gains.shape[0]
    half = D // ycount
    kv_cols = 2 * D // experts
    slice_ff = FF // Z
    pieces = tok_rows // capacity
    y_index = lax.axis_index("y")
    z_index = lax.axis_index("z")
    e_index = lax.axis_index("expert")

    def y_major(v):
        return jnp.concatenate(
            [
                v[:, (z * ycount + y) * part : (z * ycount + y + 1) * part]
                for y in range(ycount)
                for z in range(Z)
            ],
            axis=1,
        )

    def natural(v):
        return jnp.concatenate(
            [
                v[:, (y * Z + z) * part : (y * Z + z + 1) * part]
                for z in range(Z)
                for y in range(ycount)
            ],
            axis=1,
        )

    def halves(v):
        return [v[..., y * half : (y + 1) * half] for y in range(ycount)]

    def own_first(v):
        h = halves(v)
        return jnp.concatenate(
            [pick([h[(i + k) % ycount] for i in range(ycount)], y_index) for k in range(ycount)],
            axis=-1,
        )

    def own_first_back(v):
        h = halves(v)
        return jnp.concatenate(
            [pick([h[(j - i) % ycount] for i in range(ycount)], y_index) for j in range(ycount)],
            axis=-1,
        )

    def exchange(v, axes):
        return lax.all_to_all(v, axes, split_axis=0, concat_axis=0, tiled=True)

    def pack(v):
        return jnp.concatenate(
            [v[..., i * capacity : (i + 1) * capacity, :] for i in range(pieces)], axis=-1
        )

    def unpack(v):
        return jnp.concatenate(
            [v[..., i * kv_cols : (i + 1) * kv_cols] for i in range(pieces)], axis=-2
        )

    both = ("expert", "y")
    js = range(1, ycount)

    shards = Z * ycount
    small = jnp.concatenate([norm_gains, router_weight], axis=1)
    small = jnp.pad(small, ((0, 0), (0, -small.shape[1] % 16))).T
    small = exchange(jnp.broadcast_to(small[None], (shards, *small.shape)), ("y", "z"))
    small = jnp.concatenate([small[i] for i in range(shards)], axis=1)
    kv_part = lax.dynamic_slice_in_dim(kv_weight, e_index * kv_cols, kv_cols, 1)
    wide_both = lax.all_gather(
        jnp.concatenate([query_weight[0], kv_part], axis=1), "z", axis=0, tiled=True
    )
    wide_query, wide_kv = wide_both[:, :D], wide_both[:, D:]
    wide_output = lax.all_gather(output_weight[0], "z", axis=0, tiled=True)

    def z_shift(v, k):
        return lax.ppermute(v, "z", [(i, (i + k) % Z) for i in range(Z)])

    def y_shift(v, k):
        return lax.ppermute(v, "y", [(i, (i + k) % ycount) for i in range(ycount)])

    def columns(weight, k):
        return lax.dynamic_slice_in_dim(weight, ((z_index + k) % Z) * slice_ff, slice_ff, 1)

    def over_z(blocks):
        return [blocks[0]] + [z_shift(blocks[k], k) for k in range(1, Z)]

    def over_y(blocks):
        return {(j, k): y_shift(blocks[k], ycount - j) for j in range(1, ycount) for k in range(Z)}

    def assemble(own, others):
        wide = jnp.zeros((D, own[0].shape[1]), BF16)
        for j in range(ycount):
            for k in range(Z):
                block = own[k] if j == 0 else others[j, k]
                row = j * half + ((z_index - k) % Z) * part
                wide = lax.dynamic_update_slice_in_dim(wide, block, row, 0)
        return wide

    gate_weight, up_weight = gate_up_weight[0][:, :FF], gate_up_weight[0][:, FF:]
    down_z = over_z([columns(down_weight[0], k) for k in range(Z)])
    gu_z = over_z(
        [
            jnp.concatenate([columns(gate_weight, k), columns(up_weight, k)], axis=1)
            for k in range(Z)
        ]
    )
    down_y = over_y(down_z)
    gu_y = over_y(gu_z)
    wide_down = assemble(down_z, down_y)
    wide_gate_up = assemble(gu_z, gu_y)

    segment_row = segments[0]
    fill_order = slot_order[0]
    positions = jnp.arange(tok_rows)
    allowed = (positions[:, None] >= positions[None, :]) & (
        segment_row[:, None] == segment_row[None, :]
    )
    table_att = slot_table(att_routes, fill_order, experts)
    table_mlp = slot_table(mlp_routes, fill_order, experts)
    token_att = table_att[:, :tok_rows] + table_att[:, tok_rows:]
    token_mlp = table_mlp[:, :tok_rows] + table_mlp[:, tok_rows:]

    gain_one = small[0:1].astype(F32)
    gain_two = small[1:2].astype(F32)
    router_att = small[2 : 2 + experts]
    router_mlp = small[2 + experts : 2 + 2 * experts]
    inputs = y_major(tokens).astype(F32)
    grad_out = y_major(cotangent).astype(F32)
    scale_one = lax.rsqrt(jnp.mean(inputs * inputs, axis=1, keepdims=True) + EPSILON)
    normed_one = (inputs * scale_one * gain_one).astype(BF16)

    def to_experts(rows):
        slots = jnp.einsum("zts,ztd->zsd", tables, rows, preferred_element_type=F32).astype(BF16)
        return slots.reshape(Z, experts, capacity, D).transpose(1, 0, 2, 3)

    def to_tokens(rows):
        rows = rows.transpose(1, 0, 2, 3).reshape(Z, 2 * tok_rows, D)
        return jnp.einsum("zts,zsd->ztd", tables, rows, preferred_element_type=F32).astype(BF16)

    grads_z = lax.all_gather(
        jnp.concatenate([own_first(y_major(cotangent)), token_mlp.T], axis=1), "z", axis=0
    )
    tables = grads_z[:, :, D:]
    grad_rows = exchange(to_experts(grads_z[:, :, :D]), "expert").reshape(-1, D)
    att_slots_in = select_rows(token_att, normed_one).reshape(experts, capacity, D)
    send = jnp.stack(
        [
            jnp.concatenate([s, jnp.broadcast_to(n[None], (experts, tok_rows, half))], axis=1)
            for s, n in zip(halves(att_slots_in), halves(normed_one))
        ],
        axis=1,
    )
    got = exchange(send.reshape(experts * ycount, capacity + tok_rows, half), both)
    query_in = got[:, :capacity].reshape(experts * ycount * capacity, half)
    kv_in = got[:, capacity:].reshape(experts * ycount * tok_rows, half)
    own_y = [gu_y[j, k] for j, k in gu_y if k == 0] + [down_y[j, k] for j, k in gu_y if k == 0]
    query_in, kv_in = lax.optimization_barrier(
        (query_in, kv_in, *own_y)
    )[:2]
    query_part = jnp.dot(query_in, wide_query, preferred_element_type=F32).astype(BF16)
    kv_out = jnp.dot(kv_in, wide_kv, preferred_element_type=F32).astype(BF16)
    back = jnp.concatenate(
        [
            query_part.reshape(experts * ycount, capacity, D),
            pack(kv_out.reshape(experts * ycount, tok_rows, kv_cols)),
        ],
        axis=1,
    )
    back = exchange(back, both).reshape(experts, ycount, 2 * capacity, D)
    summed = jnp.sum(back.astype(F32), axis=1).astype(BF16)
    query_slots = summed[:, :capacity].reshape(2 * tok_rows, D)
    kv_parts = unpack(summed[:, capacity:])
    keyvals = jnp.concatenate([kv_parts[e] for e in range(experts)], axis=-1)
    key_heads = keyvals[:, :D].reshape(tok_rows, HEADS, HEAD_DIM)
    value_heads = keyvals[:, D:].reshape(tok_rows, HEADS, HEAD_DIM)
    router_logits = lax.dot_general(
        normed_one, router_att, CONTRACT_LAST, preferred_element_type=F32
    )
    gate_att = chosen_gates(router_logits, att_routes, experts)
    query_pairs = spread_rows(table_att, query_slots)
    queries = query_pairs.reshape(2, tok_rows, HEADS, HEAD_DIM)
    mixed_heads, log_sums = attend_forward(queries, key_heads, value_heads, allowed)

    def to_rows(v):
        v = v.reshape(experts, 1, capacity, D)
        v = jnp.broadcast_to(v, (experts, ycount, capacity, D))
        return exchange(v.reshape(experts * ycount, capacity, D), both)

    def from_halves(v):
        v = exchange(v.reshape(experts * ycount, capacity, half), both)
        v = v.reshape(experts, ycount, capacity, half)
        return jnp.concatenate([v[:, y] for y in range(ycount)], axis=-1).reshape(2 * tok_rows, D)

    mixed_slots = after(
        select_rows(table_att, mixed_heads), wide_output, *down_z[1:], gu_z[2]
    )
    mixed_in = to_rows(mixed_slots).reshape(-1, D)
    projected = lax.dot_general(
        mixed_in, wide_output, CONTRACT_LAST, preferred_element_type=F32
    ).astype(BF16)
    att_slots = after(
        from_halves(projected), gu_z[1], grads_z, *[gu_y[j, 2] for j in js], *down_y.values()
    )
    att_pairs = spread_rows(table_att, att_slots).astype(F32).reshape(2, tok_rows, D)
    hidden = inputs + gate_att[:, 0:1] * att_pairs[0] + gate_att[:, 1:2] * att_pairs[1]
    scale_two = lax.rsqrt(jnp.mean(hidden * hidden, axis=1, keepdims=True) + EPSILON)
    normed_two = (hidden * scale_two * gain_two).astype(BF16)
    mlp_logits = lax.dot_general(
        normed_two, router_mlp, CONTRACT_LAST, preferred_element_type=F32
    )
    gate_mlp = chosen_gates(mlp_logits, mlp_routes, experts)

    slot_gates = jnp.sum(
        table_mlp.astype(F32) * jnp.concatenate([gate_mlp[:, 0], gate_mlp[:, 1]])[None], axis=1
    )
    gate_cols = jnp.pad(
        jnp.concatenate(split3(slot_gates.reshape(2, tok_rows).T), axis=1), ((0, 0), (0, 122))
    )
    rows_z = lax.all_gather(
        jnp.concatenate([own_first(normed_two), gate_cols], axis=1), "z", axis=0
    )
    rows_z = after(
        rows_z, gu_z[3], grad_rows, *[gu_y[j, 1] for j in js]
    )
    gates_z = rows_z[:, :, D:]
    gates_z = jnp.concatenate([gates_z[:, :, 0:6:2], gates_z[:, :, 1:6:2]], axis=1)
    gates_z = jnp.pad(gates_z, ((0, 0), (0, 0), (0, 125)))
    gates_z = gates_z.reshape(Z, experts, capacity, 128).transpose(1, 0, 2, 3)
    got = exchange(
        jnp.concatenate([to_experts(rows_z[:, :, :D]), gates_z], axis=-1), "expert"
    ).reshape(-1, D + 128)
    free_grad = jnp.dot(grad_rows, wide_down, preferred_element_type=F32)
    got = after(got, free_grad)
    ffn_rows = got[:, :D]
    row_gates = jnp.sum(got[:, D : D + 3].astype(F32), axis=1, keepdims=True)
    gate_up = jnp.dot(ffn_rows, wide_gate_up, preferred_element_type=F32)
    gate_part = gate_up[:, :slice_ff]
    up_part = gate_up[:, slice_ff:]
    sigma = jax.nn.sigmoid(gate_part)
    activated = (gate_part * sigma * up_part).astype(BF16)
    act_grad = free_grad * row_gates
    gate_grad = act_grad * up_part * sigma * (1.0 + gate_part * (1.0 - sigma))
    up_grad = act_grad * gate_part * sigma
    gate_up_grad = jnp.concatenate([gate_grad, up_grad], axis=-1).astype(BF16)
    row_part = lax.dot_general(
        gate_up_grad, wide_gate_up, CONTRACT_LAST, preferred_element_type=F32
    ).astype(BF16)
    def outer(left_rows, right_rows):
        return lax.dot_general(left_rows, right_rows, CONTRACT_FIRST, preferred_element_type=F32)

    def block(v, k):
        return lax.dynamic_index_in_dim(v, (z_index + k) % Z, 0, keepdims=False)

    def grads_over_y(left, right):
        cols = right.shape[1]
        moved = {}
        for j in range(1, ycount):
            other = outer(left[:, j * half : (j + 1) * half], right).astype(BF16)
            other = other.reshape(Z, part, cols)
            for k in (1, 2, 3, 0):
                moved[j, k] = y_shift(block(other, k), j)
        return moved

    gated_rows = (row_gates * grad_rows.astype(F32)).astype(BF16)
    gu_moved = grads_over_y(ffn_rows, gate_up_grad)
    down_moved = grads_over_y(gated_rows, activated)
    slot_sums = jnp.sum(activated.astype(F32) * free_grad, axis=1, keepdims=True)
    slot_sums = jnp.pad(jnp.concatenate(split3(slot_sums), axis=1), ((0, 0), (0, 125)))
    back = exchange(
        jnp.concatenate([row_part, slot_sums], axis=1).reshape(
            experts, Z, capacity, D + 128
        ),
        "expert",
    )
    back = after(back, *[gu_moved[j, 1] for j in js])
    sums = back[..., D : D + 3].transpose(1, 0, 2, 3).reshape(Z, 2 * tok_rows, 3)
    sums = jnp.concatenate([sums[:, :tok_rows], sums[:, tok_rows:]], axis=-1)
    sums = jnp.concatenate(
        [jnp.where(z_index == z, sums, jnp.zeros_like(sums)) for z in range(Z)], axis=-1
    )
    sums = jnp.pad(sums, ((0, 0), (0, 0), (0, 128 - 6 * Z)))
    row_back = back
    back = lax.psum_scatter(
        jnp.concatenate([to_tokens(back[..., :D]), sums], axis=-1).reshape(-1, D + 128),
        "z",
        scatter_dimension=0,
        tiled=True,
    )
    ffn_row_grads = own_first_back(back[:, :D]).astype(F32)
    sums = back[:, D : D + 6 * Z].astype(F32).reshape(tok_rows, Z, 2, 3)
    sums = jnp.sum(sums, axis=(1, 3)).T.reshape(2 * tok_rows, 1)
    gate_mlp_grad = jnp.sum(table_mlp.astype(F32) * sums, axis=0).reshape(2, tok_rows).T

    out_part = (
        row_gates
        * lax.dot_general(after(activated, row_back), wide_down, CONTRACT_LAST, preferred_element_type=F32)
    ).astype(BF16)
    out_part = to_tokens(exchange(out_part.reshape(experts, Z, capacity, D), "expert"))
    ffn_out = lax.psum_scatter(
        out_part.reshape(-1, D), "z", scatter_dimension=0, tiled=True
    )

    def grads_over_z(left, right, moved):
        own = outer(left[:, :half], right).reshape(Z, part, right.shape[1])
        got = {}
        for k in (1, 2, 3, 0):
            total = block(own, k)
            for j in range(1, ycount):
                total = total + moved[j, k].astype(F32)
            got[k] = total if k == 0 else z_shift(total.astype(BF16), k)
        return got

    def in_order(got):
        return [
            pick([got[(z - i) % Z].astype(F32) for z in range(Z)], z_index) for i in range(Z)
        ]

    gu_got = grads_over_z(ffn_rows, gate_up_grad, gu_moved)
    down_got = grads_over_z(gated_rows, activated, down_moved)
    gu_grads = in_order(gu_got)
    gate_up_weight_grad = jnp.concatenate(
        [g[:, :slice_ff] for g in gu_grads] + [g[:, slice_ff:] for g in gu_grads], axis=1
    )[None]
    down_weight_grad = jnp.concatenate(in_order(down_got), axis=1)[None]
    ffn_row_grads = after(
        ffn_row_grads, *[gu_moved[j, k] for j in js for k in (2, 3)], out_part
    )

    logit_mlp_grad = gate_logit_grad(gate_mlp, gate_mlp_grad, mlp_routes, experts)
    normed_two_grad = (
        ffn_row_grads
        + jnp.dot(logit_mlp_grad, router_mlp.astype(F32), precision=HIGHEST)
    )
    hidden_grad = grad_out + norm_back(hidden, scale_two, gain_two, normed_two_grad)
    gate_att_grad = jnp.sum(hidden_grad[None] * att_pairs, axis=2).T
    logit_att_grad = gate_logit_grad(gate_att, gate_att_grad, att_routes, experts)
    gated_hidden = jnp.concatenate(
        [gate_att[:, 0:1] * hidden_grad, gate_att[:, 1:2] * hidden_grad], axis=0
    ).astype(BF16)
    hidden_send = select_rows(table_att, gated_hidden).reshape(experts, capacity, D)
    hidden_in = exchange(
        jnp.stack(halves(hidden_send), axis=1).reshape(experts * ycount, capacity, half), both
    ).reshape(-1, half)
    hidden_in = after(
        hidden_in, gu_got[1], *[gu_moved[j, 0] for j in js], *[down_moved[j, 1] for j in js]
    )
    head_part = jnp.dot(hidden_in, wide_output, preferred_element_type=F32).astype(BF16)
    head_part = exchange(head_part.reshape(experts * ycount, capacity, D), both)
    head_part = after(
        head_part, gu_got[2], ffn_out, *[down_moved[j, k] for j in js for k in (2, 3)]
    )
    head_slots = jnp.sum(
        head_part.reshape(experts, ycount, capacity, D).astype(F32), axis=1
    ).astype(BF16)
    mixed_grad = spread_rows(table_att, head_slots.reshape(2 * tok_rows, D)).reshape(
        2, tok_rows, HEADS, HEAD_DIM
    )
    output_grad = lax.psum_scatter(
        outer(hidden_in, mixed_in).astype(BF16), "z", scatter_dimension=0, tiled=True
    ).astype(F32)[None]
    query_grad, key_grad, value_grad = attend_backward(
        queries, key_heads, value_heads, allowed, log_sums, mixed_grad
    )
    query_grad = after(query_grad, gu_got[3], *[down_moved[j, 0] for j in js])
    keyval_row_grad = jnp.concatenate([key_grad, value_grad], axis=1).astype(BF16)
    query_send = select_rows(table_att, query_grad.astype(BF16)).reshape(experts, capacity, D)
    kv_send = pack(
        jnp.stack([keyval_row_grad[:, e * kv_cols : (e + 1) * kv_cols] for e in range(experts)])
    )
    send = jnp.concatenate([query_send, kv_send], axis=1).reshape(experts, 1, 2 * capacity, D)
    send = jnp.broadcast_to(send, (experts, ycount, 2 * capacity, D))
    got = exchange(send.reshape(experts * ycount, 2 * capacity, D), both)
    got = after(got, output_grad, *[down_got[k] for k in (1, 2)])
    block_out = (hidden + own_first_back(after(ffn_out, got)).astype(F32)).astype(BF16)
    query_rows = got[:, :capacity].reshape(-1, D)
    kv_rows = unpack(got[:, capacity:]).reshape(-1, kv_cols)
    input_part = lax.dot_general(
        query_rows, wide_query, CONTRACT_LAST, preferred_element_type=F32
    ).astype(BF16)
    normed_part = lax.dot_general(
        kv_rows, wide_kv, CONTRACT_LAST, preferred_element_type=F32
    ).astype(BF16)
    back = jnp.concatenate(
        [
            input_part.reshape(experts * ycount, capacity, half),
            normed_part.reshape(experts * ycount, tok_rows, half),
        ],
        axis=1,
    )
    query_outer = outer(query_in, query_rows).astype(BF16)
    kv_outer = outer(kv_in, kv_rows).astype(BF16)
    back = after(back, query_outer, kv_outer)
    back = exchange(back, both).reshape(experts, ycount, capacity + tok_rows, half)
    back = jnp.concatenate([back[:, y] for y in range(ycount)], axis=-1)
    input_pairs = (
        spread_rows(table_att, back[:, :capacity].reshape(2 * tok_rows, D))
        .astype(F32)
        .reshape(2, tok_rows, D)
    )
    kv_grad_part = lax.psum_scatter(kv_outer, "z", scatter_dimension=0, tiled=True)
    query_weight_grad = lax.psum_scatter(
        query_outer, "z", scatter_dimension=0, tiled=True
    ).astype(F32)[None]
    kv_grads = exchange(
        jnp.broadcast_to(kv_grad_part[None], (experts, *kv_grad_part.shape)), "expert"
    )
    keyval_grad = jnp.concatenate([kv_grads[e] for e in range(experts)], axis=1).astype(F32)
    normed_one_grad = (
        input_pairs[0] + input_pairs[1] + jnp.sum(back[:, capacity:].astype(F32), axis=0)
    )
    normed_one_grad = normed_one_grad + jnp.dot(
        logit_att_grad, router_att.astype(F32), precision=HIGHEST
    )
    input_grad = natural(
        hidden_grad + norm_back(inputs, scale_one, gain_one, normed_one_grad)
    )

    small_grads = jnp.concatenate(
        [
            jnp.sum(normed_one_grad * inputs * scale_one, axis=0)[None],
            jnp.sum(normed_two_grad * hidden * scale_two, axis=0)[None],
            lax.dot_general(
                logit_att_grad, normed_one.astype(F32), CONTRACT_FIRST, precision=HIGHEST
            ),
            lax.dot_general(
                logit_mlp_grad, normed_two.astype(F32), CONTRACT_FIRST, precision=HIGHEST
            ),
        ],
        axis=0,
    )
    rows = small_grads.shape[0]
    small_grads = jnp.stack(
        [small_grads[:, i * part : (i + 1) * part] for i in range(Z * ycount)]
    )
    small_grads = jnp.sum(exchange(small_grads, ("y", "z")), axis=0)
    small_grads = lax.psum(small_grads, "expert").T
    gains_grad = small_grads[:, :2]
    router_grad = small_grads[:, 2:rows]
    return (
        natural(block_out),
        input_grad,
        gains_grad,
        keyval_grad,
        router_grad,
        query_weight_grad,
        output_grad,
        gate_up_weight_grad,
        down_weight_grad,
    )


def solution(mesh):
    experts, shards = mesh.shape["expert"], mesh.shape["shard"]
    grid = Mesh(mesh.devices.reshape(experts, Z, shards // Z), ("expert", "z", "y"))
    rows = P(("expert", "z", "y"), None)
    shared = P(("z", "y"), None)
    owned = P("expert", ("z", "y"), None)
    in_specs = (rows,) * 6 + (shared,) * 3 + (owned,) * 4
    out_specs = (rows,) * 2 + (shared,) * 3 + (owned,) * 4
    return jax.shard_map(
        per_device, mesh=grid, in_specs=in_specs, out_specs=out_specs, check_vma=False
    )
```

```python
import jax
import jax.numpy as jnp
from jax import lax
from jax.sharding import Mesh
from jax.sharding import PartitionSpec as P

D = 2048
HEADS = 16
HEAD_DIM = 128
FF = 5632
Z = 4

EPSILON = 1e-05
NEGATIVE = -1e30
HIGHEST = lax.Precision.HIGHEST
CONTRACT_FIRST = (((0,), (0,)), ((), ()))
CONTRACT_LAST = (((1,), (1,)), ((), ()))
BF16 = jnp.bfloat16
F32 = jnp.float32


def slot_table(routes, fill_order, experts):
    pair_count = 2 * routes.shape[0]
    capacity = pair_count // experts
    pair_index = jnp.arange(pair_count, dtype=jnp.int32)
    pair_expert = jnp.concatenate([routes[:, 0], routes[:, 1]]).astype(F32)
    reorder = (fill_order[:, None] == pair_index[None, :]).astype(F32)
    ordered = jnp.dot(reorder, pair_expert, precision=HIGHEST)
    onehot = (ordered[:, None] == jnp.arange(experts, dtype=F32)[None, :]).astype(F32)
    below_mask = (pair_index[:, None] > pair_index[None, :]).astype(F32)
    earlier = jnp.dot(below_mask, onehot, precision=HIGHEST)
    position = jnp.sum(earlier * onehot, axis=1)
    target = ordered * capacity + position
    placing = (
        (target[:, None] == pair_index.astype(F32)[None, :]) & (position < capacity)[:, None]
    ).astype(F32)
    return lax.dot_general(placing, reorder, CONTRACT_FIRST, precision=HIGHEST).astype(BF16)


def select_rows(table, pair_rows):
    return jnp.dot(table, pair_rows, preferred_element_type=F32).astype(BF16)


def spread_rows(table, slot_rows):
    return lax.dot_general(table, slot_rows, CONTRACT_FIRST, preferred_element_type=F32).astype(BF16)


def chosen_gates(logits, routes, experts):
    expert_ids = jnp.arange(experts, dtype=jnp.int32)[None, :]
    first_logit = jnp.sum(jnp.where(routes[:, 0:1] == expert_ids, logits, 0.0), axis=1)
    second_logit = jnp.sum(jnp.where(routes[:, 1:2] == expert_ids, logits, 0.0), axis=1)
    return jax.nn.softmax(jnp.stack([first_logit, second_logit], axis=1), axis=1)


def gate_logit_grad(gate_pair, gate_grad, routes, experts):
    expert_ids = jnp.arange(experts, dtype=jnp.int32)[None, :]
    chosen_grad = gate_pair * (gate_grad - jnp.sum(gate_pair * gate_grad, axis=1, keepdims=True))
    first_part = chosen_grad[:, 0:1] * (routes[:, 0:1] == expert_ids).astype(F32)
    return first_part + chosen_grad[:, 1:2] * (routes[:, 1:2] == expert_ids).astype(F32)


def norm_back(values, scale, gain_row, normed_grad):
    scaled = normed_grad * gain_row
    return scale * (
        scaled - values * scale * scale * jnp.mean(scaled * values, axis=1, keepdims=True)
    )


def attend_forward(queries, key_heads, value_heads, allowed):
    tok_rows = key_heads.shape[0]
    scores = jnp.einsum("kqhd,shd->khqs", queries, key_heads, preferred_element_type=F32) * (
        HEAD_DIM ** (-0.5)
    )
    masked = jnp.where(allowed[None, None], scores, NEGATIVE)
    row_max = jnp.max(masked, axis=-1, keepdims=True)
    exponent = jnp.exp(masked - row_max)
    totals = jnp.sum(exponent, axis=-1, keepdims=True)
    softmax_out = (exponent / totals).astype(BF16)
    mixed = jnp.einsum("khqs,shd->kqhd", softmax_out, value_heads, preferred_element_type=F32)
    mixed = mixed.astype(BF16).reshape(2 * tok_rows, HEADS * HEAD_DIM)
    return mixed, (row_max + jnp.log(totals))[..., 0]


def attend_backward(queries, key_heads, value_heads, allowed, log_sums, mixed_grad):
    tok_rows = key_heads.shape[0]
    scale_factor = HEAD_DIM ** (-0.5)
    scores = (
        jnp.einsum("kqhd,shd->khqs", queries, key_heads, preferred_element_type=F32) * scale_factor
    )
    softmax_out = jnp.where(allowed[None, None], jnp.exp(scores - log_sums[..., None]), 0.0)
    prob_grad = jnp.einsum("kqhd,shd->khqs", mixed_grad, value_heads, preferred_element_type=F32)
    score_grad = (
        softmax_out * (prob_grad - jnp.sum(softmax_out * prob_grad, axis=-1, keepdims=True))
    ).astype(BF16)
    query_grad = (
        jnp.einsum("khqs,shd->kqhd", score_grad, key_heads, preferred_element_type=F32)
        * scale_factor
    )
    key_grad = (
        jnp.einsum("khqs,kqhd->shd", score_grad, queries, preferred_element_type=F32) * scale_factor
    )
    value_grad = jnp.einsum(
        "khqs,kqhd->shd", softmax_out.astype(BF16), mixed_grad, preferred_element_type=F32
    )
    return (
        query_grad.reshape(2 * tok_rows, D),
        key_grad.reshape(tok_rows, D),
        value_grad.reshape(tok_rows, D),
    )


def pick(choices, index):
    result = choices[0]
    for i in range(1, len(choices)):
        result = jnp.where(index == i, choices[i], result)
    return result


def split3(v):
    high = lax.reduce_precision(v, exponent_bits=8, mantissa_bits=7)
    middle = lax.reduce_precision(v - high, exponent_bits=8, mantissa_bits=7)
    return [high.astype(BF16), middle.astype(BF16), (v - high - middle).astype(BF16)]


def after(value, *others):
    return lax.optimization_barrier((value, *others))[0]


def per_device(
    tokens,
    cotangent,
    segments,
    att_routes,
    mlp_routes,
    slot_order,
    norm_gains,
    kv_weight,
    router_weight,
    query_weight,
    output_weight,
    gate_up_weight,
    down_weight,
):
    tok_rows = tokens.shape[0]
    experts = lax.axis_size("expert") * query_weight.shape[0]
    ycount = lax.axis_size("y")
    capacity = 2 * tok_rows // experts
    part = norm_gains.shape[0]
    half = D // ycount
    kv_cols = 2 * D // experts
    slice_ff = FF // Z
    pieces = tok_rows // capacity
    y_index = lax.axis_index("y")
    z_index = lax.axis_index("z")
    e_index = lax.axis_index("expert")

    def y_major(v):
        return jnp.concatenate(
            [
                v[:, (z * ycount + y) * part : (z * ycount + y + 1) * part]
                for y in range(ycount)
                for z in range(Z)
            ],
            axis=1,
        )

    def natural(v):
        return jnp.concatenate(
            [
                v[:, (y * Z + z) * part : (y * Z + z + 1) * part]
                for z in range(Z)
                for y in range(ycount)
            ],
            axis=1,
        )

    def halves(v):
        return [v[..., y * half : (y + 1) * half] for y in range(ycount)]

    def own_first(v):
        h = halves(v)
        return jnp.concatenate(
            [pick([h[(i + k) % ycount] for i in range(ycount)], y_index) for k in range(ycount)],
            axis=-1,
        )

    def own_first_back(v):
        h = halves(v)
        return jnp.concatenate(
            [pick([h[(j - i) % ycount] for i in range(ycount)], y_index) for j in range(ycount)],
            axis=-1,
        )

    def exchange(v, axes):
        return lax.all_to_all(v, axes, split_axis=0, concat_axis=0, tiled=True)

    def pack(v):
        return jnp.concatenate(
            [v[..., i * capacity : (i + 1) * capacity, :] for i in range(pieces)], axis=-1
        )

    def unpack(v):
        return jnp.concatenate(
            [v[..., i * kv_cols : (i + 1) * kv_cols] for i in range(pieces)], axis=-2
        )

    both = ("expert", "y")
    js = range(1, ycount)

    shards = Z * ycount
    small = jnp.concatenate([norm_gains, router_weight], axis=1)
    small = jnp.pad(small, ((0, 0), (0, -small.shape[1] % 16))).T
    small = exchange(jnp.broadcast_to(small[None], (shards, *small.shape)), ("y", "z"))
    small = jnp.concatenate([small[i] for i in range(shards)], axis=1)
    kv_part = lax.dynamic_slice_in_dim(kv_weight, e_index * kv_cols, kv_cols, 1)
    wide_both = lax.all_gather(
        jnp.concatenate([query_weight[0], kv_part], axis=1), "z", axis=0, tiled=True
    )
    wide_query, wide_kv = wide_both[:, :D], wide_both[:, D:]
    wide_output = lax.all_gather(output_weight[0], "z", axis=0, tiled=True)

    def z_shift(v, k):
        return lax.ppermute(v, "z", [(i, (i + k) % Z) for i in range(Z)])

    def y_shift(v, k):
        return lax.ppermute(v, "y", [(i, (i + k) % ycount) for i in range(ycount)])

    def columns(weight, k):
        return lax.dynamic_slice_in_dim(weight, ((z_index + k) % Z) * slice_ff, slice_ff, 1)

    def over_z(blocks):
        return [blocks[0]] + [z_shift(blocks[k], k) for k in range(1, Z)]

    def over_y(blocks):
        return {(j, k): y_shift(blocks[k], ycount - j) for j in range(1, ycount) for k in range(Z)}

    def assemble(own, others):
        wide = jnp.zeros((D, own[0].shape[1]), BF16)
        for j in range(ycount):
            for k in range(Z):
                block = own[k] if j == 0 else others[j, k]
                row = j * half + ((z_index - k) % Z) * part
                wide = lax.dynamic_update_slice_in_dim(wide, block, row, 0)
        return wide

    gate_weight, up_weight = gate_up_weight[0][:, :FF], gate_up_weight[0][:, FF:]
    down_z = over_z([columns(down_weight[0], k) for k in range(Z)])
    gu_z = over_z(
        [
            jnp.concatenate([columns(gate_weight, k), columns(up_weight, k)], axis=1)
            for k in range(Z)
        ]
    )
    down_y = over_y(down_z)
    gu_y = over_y(gu_z)
    wide_down = assemble(down_z, down_y)
    wide_gate_up = assemble(gu_z, gu_y)

    segment_row = segments[0]
    fill_order = slot_order[0]
    positions = jnp.arange(tok_rows)
    allowed = (positions[:, None] >= positions[None, :]) & (
        segment_row[:, None] == segment_row[None, :]
    )
    table_att = slot_table(att_routes, fill_order, experts)
    table_mlp = slot_table(mlp_routes, fill_order, experts)
    token_att = table_att[:, :tok_rows] + table_att[:, tok_rows:]
    token_mlp = table_mlp[:, :tok_rows] + table_mlp[:, tok_rows:]

    gain_one = small[0:1].astype(F32)
    gain_two = small[1:2].astype(F32)
    router_att = small[2 : 2 + experts]
    router_mlp = small[2 + experts : 2 + 2 * experts]
    inputs = y_major(tokens).astype(F32)
    grad_out = y_major(cotangent).astype(F32)
    scale_one = lax.rsqrt(jnp.mean(inputs * inputs, axis=1, keepdims=True) + EPSILON)
    normed_one = (inputs * scale_one * gain_one).astype(BF16)

    def to_experts(rows):
        slots = jnp.einsum("zts,ztd->zsd", tables, rows, preferred_element_type=F32).astype(BF16)
        return slots.reshape(Z, experts, capacity, D).transpose(1, 0, 2, 3)

    def to_tokens(rows):
        rows = rows.transpose(1, 0, 2, 3).reshape(Z, 2 * tok_rows, D)
        return jnp.einsum("zts,zsd->ztd", tables, rows, preferred_element_type=F32).astype(BF16)

    grads_z = lax.all_gather(
        jnp.concatenate([own_first(y_major(cotangent)), token_mlp.T], axis=1), "z", axis=0
    )
    tables = grads_z[:, :, D:]
    grad_rows = exchange(to_experts(grads_z[:, :, :D]), "expert").reshape(-1, D)
    att_slots_in = select_rows(token_att, normed_one).reshape(experts, capacity, D)
    send = jnp.stack(
        [
            jnp.concatenate([s, jnp.broadcast_to(n[None], (experts, tok_rows, half))], axis=1)
            for s, n in zip(halves(att_slots_in), halves(normed_one))
        ],
        axis=1,
    )
    got = exchange(send.reshape(experts * ycount, capacity + tok_rows, half), both)
    query_in = got[:, :capacity].reshape(experts * ycount * capacity, half)
    kv_in = got[:, capacity:].reshape(experts * ycount * tok_rows, half)
    own_y = [gu_y[j, k] for j, k in gu_y if k == 0] + [down_y[j, k] for j, k in gu_y if k == 0]
    query_in, kv_in = lax.optimization_barrier(
        (query_in, kv_in, *own_y)
    )[:2]
    query_part = jnp.dot(query_in, wide_query, preferred_element_type=F32).astype(BF16)
    kv_out = jnp.dot(kv_in, wide_kv, preferred_element_type=F32).astype(BF16)
    back = jnp.concatenate(
        [
            query_part.reshape(experts * ycount, capacity, D),
            pack(kv_out.reshape(experts * ycount, tok_rows, kv_cols)),
        ],
        axis=1,
    )
    back = exchange(back, both).reshape(experts, ycount, 2 * capacity, D)
    back = after(back, grads_z)
    summed = jnp.sum(back.astype(F32), axis=1).astype(BF16)
    query_slots = summed[:, :capacity].reshape(2 * tok_rows, D)
    kv_parts = unpack(summed[:, capacity:])
    keyvals = jnp.concatenate([kv_parts[e] for e in range(experts)], axis=-1)
    key_heads = keyvals[:, :D].reshape(tok_rows, HEADS, HEAD_DIM)
    value_heads = keyvals[:, D:].reshape(tok_rows, HEADS, HEAD_DIM)
    router_logits = lax.dot_general(
        normed_one, router_att, CONTRACT_LAST, preferred_element_type=F32
    )
    gate_att = chosen_gates(router_logits, att_routes, experts)
    query_pairs = spread_rows(table_att, query_slots)
    queries = query_pairs.reshape(2, tok_rows, HEADS, HEAD_DIM)
    mixed_heads, log_sums = attend_forward(queries, key_heads, value_heads, allowed)

    def to_rows(v):
        v = v.reshape(experts, 1, capacity, D)
        v = jnp.broadcast_to(v, (experts, ycount, capacity, D))
        return exchange(v.reshape(experts * ycount, capacity, D), both)

    def from_halves(v):
        v = exchange(v.reshape(experts * ycount, capacity, half), both)
        v = v.reshape(experts, ycount, capacity, half)
        return jnp.concatenate([v[:, y] for y in range(ycount)], axis=-1).reshape(2 * tok_rows, D)

    mixed_slots = after(
        select_rows(table_att, mixed_heads), wide_output, grad_rows, *down_z[1:]
    )
    mixed_in = to_rows(mixed_slots).reshape(-1, D)
    mixed_in = after(mixed_in, *[down_y[j, k] for j in js for k in (1, 3)])
    projected = lax.dot_general(
        mixed_in, wide_output, CONTRACT_LAST, preferred_element_type=F32
    ).astype(BF16)
    att_slots = after(from_halves(projected), gu_z[2], *[down_y[j, 2] for j in js])
    att_pairs = spread_rows(table_att, att_slots).astype(F32).reshape(2, tok_rows, D)
    hidden = inputs + gate_att[:, 0:1] * att_pairs[0] + gate_att[:, 1:2] * att_pairs[1]
    scale_two = lax.rsqrt(jnp.mean(hidden * hidden, axis=1, keepdims=True) + EPSILON)
    normed_two = (hidden * scale_two * gain_two).astype(BF16)
    mlp_logits = lax.dot_general(
        normed_two, router_mlp, CONTRACT_LAST, preferred_element_type=F32
    )
    gate_mlp = chosen_gates(mlp_logits, mlp_routes, experts)

    slot_gates = jnp.sum(
        table_mlp.astype(F32) * jnp.concatenate([gate_mlp[:, 0], gate_mlp[:, 1]])[None], axis=1
    )
    gate_cols = jnp.pad(
        jnp.concatenate(split3(slot_gates.reshape(2, tok_rows).T), axis=1), ((0, 0), (0, 122))
    )
    rows_z = lax.all_gather(
        jnp.concatenate([own_first(normed_two), gate_cols], axis=1), "z", axis=0
    )
    rows_z = after(
        rows_z, gu_z[1], gu_z[3], *[gu_y[j, 2] for j in js]
    )
    gates_z = rows_z[:, :, D:]
    gates_z = jnp.concatenate([gates_z[:, :, 0:6:2], gates_z[:, :, 1:6:2]], axis=1)
    gates_z = jnp.pad(gates_z, ((0, 0), (0, 0), (0, 125)))
    gates_z = gates_z.reshape(Z, experts, capacity, 128).transpose(1, 0, 2, 3)
    got = exchange(
        jnp.concatenate([to_experts(rows_z[:, :, :D]), gates_z], axis=-1), "expert"
    ).reshape(-1, D + 128)
    free_grad = jnp.dot(grad_rows, wide_down, preferred_element_type=F32)
    got = after(got, free_grad)
    ffn_rows = got[:, :D]
    row_gates = jnp.sum(got[:, D : D + 3].astype(F32), axis=1, keepdims=True)
    gate_up = jnp.dot(ffn_rows, wide_gate_up, preferred_element_type=F32)
    gate_part = gate_up[:, :slice_ff]
    up_part = gate_up[:, slice_ff:]
    sigma = jax.nn.sigmoid(gate_part)
    activated = (gate_part * sigma * up_part).astype(BF16)
    act_grad = free_grad * row_gates
    gate_grad = act_grad * up_part * sigma * (1.0 + gate_part * (1.0 - sigma))
    up_grad = act_grad * gate_part * sigma
    gate_up_grad = jnp.concatenate([gate_grad, up_grad], axis=-1).astype(BF16)
    row_part = lax.dot_general(
        gate_up_grad, wide_gate_up, CONTRACT_LAST, preferred_element_type=F32
    ).astype(BF16)

    def outer(left_rows, right_rows):
        return lax.dot_general(left_rows, right_rows, CONTRACT_FIRST, preferred_element_type=F32)

    def block(v, k):
        return lax.dynamic_index_in_dim(v, (z_index + k) % Z, 0, keepdims=False)

    def peers(left, right):
        return [
            outer(left[:, j * half : (j + 1) * half], right)
            .astype(BF16)
            .reshape(Z, part, right.shape[1])
            for j in js
        ]

    def over_y_back(others, k):
        return [y_shift(block(other, k), j) for j, other in zip(js, others)]

    def add_up(own, moved):
        total = own
        for m in moved:
            total = total + m.astype(F32)
        return total

    def in_order(got):
        return [
            pick([got[(z - i) % Z].astype(F32) for z in range(Z)], z_index) for i in range(Z)
        ]

    gated_rows = (row_gates * grad_rows.astype(F32)).astype(BF16)
    gu_peers = peers(ffn_rows, gate_up_grad)
    gu_moved = {k: over_y_back(gu_peers, k) for k in (1, 2, 3)}
    slot_sums = jnp.sum(activated.astype(F32) * free_grad, axis=1, keepdims=True)
    slot_sums = jnp.pad(jnp.concatenate(split3(slot_sums), axis=1), ((0, 0), (0, 125)))
    back = exchange(
        jnp.concatenate([row_part, slot_sums], axis=1).reshape(
            experts, Z, capacity, D + 128
        ),
        "expert",
    )
    back = after(back, *gu_moved[1])
    sums = back[..., D : D + 3].transpose(1, 0, 2, 3).reshape(Z, 2 * tok_rows, 3)
    sums = jnp.concatenate([sums[:, :tok_rows], sums[:, tok_rows:]], axis=-1)
    sums = jnp.concatenate(
        [jnp.where(z_index == z, sums, jnp.zeros_like(sums)) for z in range(Z)], axis=-1
    )
    sums = jnp.pad(sums, ((0, 0), (0, 0), (0, 128 - 6 * Z)))
    row_back = back
    back = lax.psum_scatter(
        jnp.concatenate([to_tokens(back[..., :D]), sums], axis=-1).reshape(-1, D + 128),
        "z",
        scatter_dimension=0,
        tiled=True,
    )
    ffn_row_grads = own_first_back(back[:, :D]).astype(F32)
    sums = back[:, D : D + 6 * Z].astype(F32).reshape(tok_rows, Z, 2, 3)
    sums = jnp.sum(sums, axis=(1, 3)).T.reshape(2 * tok_rows, 1)
    gate_mlp_grad = jnp.sum(table_mlp.astype(F32) * sums, axis=0).reshape(2, tok_rows).T

    out_part = (
        row_gates
        * lax.dot_general(after(activated, row_back), wide_down, CONTRACT_LAST, preferred_element_type=F32)
    ).astype(BF16)
    out_part = to_tokens(exchange(out_part.reshape(experts, Z, capacity, D), "expert"))
    ffn_out = lax.psum_scatter(
        out_part.reshape(-1, D), "z", scatter_dimension=0, tiled=True
    )

    gu_own = outer(ffn_rows[:, :half], gate_up_grad).reshape(Z, part, 2 * slice_ff)
    gu_got = {
        k: z_shift(add_up(block(gu_own, k), gu_moved[k]).astype(BF16), k) for k in (1, 2, 3)
    }

    ffn_row_grads = after(ffn_row_grads, *gu_moved[2], out_part)
    late_rows = after(gated_rows, ffn_row_grads)
    down_peers = peers(late_rows, activated)
    down_moved = {k: over_y_back(down_peers, k) for k in (1, 2, 3)}
    down_own = outer(late_rows[:, :half], activated).reshape(Z, part, slice_ff)
    logit_mlp_grad = gate_logit_grad(gate_mlp, gate_mlp_grad, mlp_routes, experts)
    normed_two_grad = (
        ffn_row_grads
        + jnp.dot(logit_mlp_grad, router_mlp.astype(F32), precision=HIGHEST)
    )
    hidden_grad = grad_out + norm_back(hidden, scale_two, gain_two, normed_two_grad)
    gate_att_grad = jnp.sum(hidden_grad[None] * att_pairs, axis=2).T
    logit_att_grad = gate_logit_grad(gate_att, gate_att_grad, att_routes, experts)
    gated_hidden = jnp.concatenate(
        [gate_att[:, 0:1] * hidden_grad, gate_att[:, 1:2] * hidden_grad], axis=0
    ).astype(BF16)
    hidden_send = select_rows(table_att, gated_hidden).reshape(experts, capacity, D)
    hidden_in = exchange(
        jnp.stack(halves(hidden_send), axis=1).reshape(experts * ycount, capacity, half), both
    ).reshape(-1, half)
    hidden_in = after(hidden_in, *gu_moved[3])
    head_part = jnp.dot(hidden_in, wide_output, preferred_element_type=F32).astype(BF16)
    head_part = exchange(head_part.reshape(experts * ycount, capacity, D), both)
    head_part = after(head_part, gu_got[1], ffn_out, *[m for k in (1, 2) for m in down_moved[k]])
    head_slots = jnp.sum(
        head_part.reshape(experts, ycount, capacity, D).astype(F32), axis=1
    ).astype(BF16)
    mixed_grad = spread_rows(table_att, head_slots.reshape(2 * tok_rows, D)).reshape(
        2, tok_rows, HEADS, HEAD_DIM
    )
    output_grad = lax.psum_scatter(
        outer(hidden_in, mixed_in).astype(BF16), "z", scatter_dimension=0, tiled=True
    ).astype(F32)[None]
    query_grad, key_grad, value_grad = attend_backward(
        queries, key_heads, value_heads, allowed, log_sums, mixed_grad
    )
    query_grad = after(query_grad, gu_got[3], *down_moved[3])
    late_own, late_gu, late_down = lax.optimization_barrier(
        (down_own, gu_peers, down_peers, query_grad)
    )[:3]
    gu_moved[0] = over_y_back(late_gu, 0)
    down_moved[0] = over_y_back(late_down, 0)
    down_got = {
        k: z_shift(add_up(block(late_own, k), down_moved[k]).astype(BF16), k) for k in (1, 2, 3)
    }
    keyval_row_grad = jnp.concatenate([key_grad, value_grad], axis=1).astype(BF16)
    query_send = select_rows(table_att, query_grad.astype(BF16)).reshape(experts, capacity, D)
    kv_send = pack(
        jnp.stack([keyval_row_grad[:, e * kv_cols : (e + 1) * kv_cols] for e in range(experts)])
    )
    send = jnp.concatenate([query_send, kv_send], axis=1).reshape(experts, 1, 2 * capacity, D)
    send = jnp.broadcast_to(send, (experts, ycount, 2 * capacity, D))
    got = exchange(send.reshape(experts * ycount, 2 * capacity, D), both)
    got = after(got, output_grad, gu_got[2], *gu_moved[0])
    block_out = (hidden + own_first_back(after(ffn_out, got)).astype(F32)).astype(BF16)
    query_rows = got[:, :capacity].reshape(-1, D)
    kv_rows = unpack(got[:, capacity:]).reshape(-1, kv_cols)
    input_part = lax.dot_general(
        query_rows, wide_query, CONTRACT_LAST, preferred_element_type=F32
    ).astype(BF16)
    normed_part = lax.dot_general(
        kv_rows, wide_kv, CONTRACT_LAST, preferred_element_type=F32
    ).astype(BF16)
    back = jnp.concatenate(
        [
            input_part.reshape(experts * ycount, capacity, half),
            normed_part.reshape(experts * ycount, tok_rows, half),
        ],
        axis=1,
    )
    query_outer = outer(query_in, query_rows).astype(BF16)
    kv_outer = outer(kv_in, kv_rows).astype(BF16)
    back = after(back, query_outer, kv_outer)
    back = exchange(back, both).reshape(experts, ycount, capacity + tok_rows, half)
    back = after(back, *[down_got[k] for k in (1, 2, 3)], *down_moved[0])
    gu_got[0] = add_up(block(gu_own, 0), gu_moved[0])
    down_got[0] = add_up(block(late_own, 0), down_moved[0])
    gu_grads = in_order(gu_got)
    gate_up_weight_grad = jnp.concatenate(
        [g[:, :slice_ff] for g in gu_grads] + [g[:, slice_ff:] for g in gu_grads], axis=1
    )[None]
    down_weight_grad = jnp.concatenate(in_order(down_got), axis=1)[None]
    back = jnp.concatenate([back[:, y] for y in range(ycount)], axis=-1)
    input_pairs = (
        spread_rows(table_att, back[:, :capacity].reshape(2 * tok_rows, D))
        .astype(F32)
        .reshape(2, tok_rows, D)
    )
    kv_grad_part = lax.psum_scatter(kv_outer, "z", scatter_dimension=0, tiled=True)
    query_weight_grad = lax.psum_scatter(
        query_outer, "z", scatter_dimension=0, tiled=True
    ).astype(F32)[None]
    kv_grads = exchange(
        jnp.broadcast_to(kv_grad_part[None], (experts, *kv_grad_part.shape)), "expert"
    )
    keyval_grad = jnp.concatenate([kv_grads[e] for e in range(experts)], axis=1).astype(F32)
    normed_one_grad = (
        input_pairs[0] + input_pairs[1] + jnp.sum(back[:, capacity:].astype(F32), axis=0)
    )
    normed_one_grad = normed_one_grad + jnp.dot(
        logit_att_grad, router_att.astype(F32), precision=HIGHEST
    )
    input_grad = natural(
        hidden_grad + norm_back(inputs, scale_one, gain_one, normed_one_grad)
    )

    small_grads = jnp.concatenate(
        [
            jnp.sum(normed_one_grad * inputs * scale_one, axis=0)[None],
            jnp.sum(normed_two_grad * hidden * scale_two, axis=0)[None],
            lax.dot_general(
                logit_att_grad, normed_one.astype(F32), CONTRACT_FIRST, precision=HIGHEST
            ),
            lax.dot_general(
                logit_mlp_grad, normed_two.astype(F32), CONTRACT_FIRST, precision=HIGHEST
            ),
        ],
        axis=0,
    )
    rows = small_grads.shape[0]
    small_grads = jnp.stack(
        [small_grads[:, i * part : (i + 1) * part] for i in range(Z * ycount)]
    )
    small_grads = jnp.sum(exchange(small_grads, ("y", "z")), axis=0)
    small_grads = lax.psum(small_grads, "expert").T
    gains_grad = small_grads[:, :2]
    router_grad = small_grads[:, 2:rows]
    return (
        natural(block_out),
        input_grad,
        gains_grad,
        keyval_grad,
        router_grad,
        query_weight_grad,
        output_grad,
        gate_up_weight_grad,
        down_weight_grad,
    )


def solution(mesh):
    experts, shards = mesh.shape["expert"], mesh.shape["shard"]
    grid = Mesh(mesh.devices.reshape(experts, Z, shards // Z), ("expert", "z", "y"))
    rows = P(("expert", "z", "y"), None)
    shared = P(("z", "y"), None)
    owned = P("expert", ("z", "y"), None)
    in_specs = (rows,) * 6 + (shared,) * 3 + (owned,) * 4
    out_specs = (rows,) * 2 + (shared,) * 3 + (owned,) * 4
    return jax.shard_map(
        per_device, mesh=grid, in_specs=in_specs, out_specs=out_specs, check_vma=False
    )
```

```python
import jax
import jax.numpy as jnp
from jax import lax
from jax.sharding import Mesh
from jax.sharding import PartitionSpec as P

D = 2048
HEADS = 16
HEAD_DIM = 128
FF = 5632
Z = 4

EPSILON = 1e-05
NEGATIVE = -1e30
HIGHEST = lax.Precision.HIGHEST
CONTRACT_FIRST = (((0,), (0,)), ((), ()))
CONTRACT_LAST = (((1,), (1,)), ((), ()))
BF16 = jnp.bfloat16
F32 = jnp.float32


def slot_table(routes, fill_order, experts):
    pair_count = 2 * routes.shape[0]
    capacity = pair_count // experts
    pair_index = jnp.arange(pair_count, dtype=jnp.int32)
    pair_expert = jnp.concatenate([routes[:, 0], routes[:, 1]]).astype(F32)
    reorder = (fill_order[:, None] == pair_index[None, :]).astype(F32)
    ordered = jnp.dot(reorder, pair_expert, precision=HIGHEST)
    onehot = (ordered[:, None] == jnp.arange(experts, dtype=F32)[None, :]).astype(F32)
    below_mask = (pair_index[:, None] > pair_index[None, :]).astype(F32)
    earlier = jnp.dot(below_mask, onehot, precision=HIGHEST)
    position = jnp.sum(earlier * onehot, axis=1)
    target = ordered * capacity + position
    placing = (
        (target[:, None] == pair_index.astype(F32)[None, :]) & (position < capacity)[:, None]
    ).astype(F32)
    return lax.dot_general(placing, reorder, CONTRACT_FIRST, precision=HIGHEST).astype(BF16)


def select_rows(table, pair_rows):
    return jnp.dot(table, pair_rows, preferred_element_type=F32).astype(BF16)


def spread_rows(table, slot_rows):
    return lax.dot_general(table, slot_rows, CONTRACT_FIRST, preferred_element_type=F32).astype(BF16)


def chosen_gates(logits, routes, experts):
    expert_ids = jnp.arange(experts, dtype=jnp.int32)[None, :]
    first_logit = jnp.sum(jnp.where(routes[:, 0:1] == expert_ids, logits, 0.0), axis=1)
    second_logit = jnp.sum(jnp.where(routes[:, 1:2] == expert_ids, logits, 0.0), axis=1)
    return jax.nn.softmax(jnp.stack([first_logit, second_logit], axis=1), axis=1)


def gate_logit_grad(gate_pair, gate_grad, routes, experts):
    expert_ids = jnp.arange(experts, dtype=jnp.int32)[None, :]
    chosen_grad = gate_pair * (gate_grad - jnp.sum(gate_pair * gate_grad, axis=1, keepdims=True))
    first_part = chosen_grad[:, 0:1] * (routes[:, 0:1] == expert_ids).astype(F32)
    return first_part + chosen_grad[:, 1:2] * (routes[:, 1:2] == expert_ids).astype(F32)


def norm_back(values, scale, gain_row, normed_grad):
    scaled = normed_grad * gain_row
    return scale * (
        scaled - values * scale * scale * jnp.mean(scaled * values, axis=1, keepdims=True)
    )


def attend_forward(queries, key_heads, value_heads, allowed):
    tok_rows = key_heads.shape[0]
    scores = jnp.einsum("kqhd,shd->khqs", queries, key_heads, preferred_element_type=F32) * (
        HEAD_DIM ** (-0.5)
    )
    masked = jnp.where(allowed[None, None], scores, NEGATIVE)
    row_max = jnp.max(masked, axis=-1, keepdims=True)
    exponent = jnp.exp(masked - row_max)
    totals = jnp.sum(exponent, axis=-1, keepdims=True)
    softmax_out = (exponent / totals).astype(BF16)
    mixed = jnp.einsum("khqs,shd->kqhd", softmax_out, value_heads, preferred_element_type=F32)
    mixed = mixed.astype(BF16).reshape(2 * tok_rows, HEADS * HEAD_DIM)
    return mixed, (row_max + jnp.log(totals))[..., 0]


def attend_backward(queries, key_heads, value_heads, allowed, log_sums, mixed_grad):
    tok_rows = key_heads.shape[0]
    scale_factor = HEAD_DIM ** (-0.5)
    scores = (
        jnp.einsum("kqhd,shd->khqs", queries, key_heads, preferred_element_type=F32) * scale_factor
    )
    softmax_out = jnp.where(allowed[None, None], jnp.exp(scores - log_sums[..., None]), 0.0)
    prob_grad = jnp.einsum("kqhd,shd->khqs", mixed_grad, value_heads, preferred_element_type=F32)
    score_grad = (
        softmax_out * (prob_grad - jnp.sum(softmax_out * prob_grad, axis=-1, keepdims=True))
    ).astype(BF16)
    query_grad = (
        jnp.einsum("khqs,shd->kqhd", score_grad, key_heads, preferred_element_type=F32)
        * scale_factor
    )
    key_grad = (
        jnp.einsum("khqs,kqhd->shd", score_grad, queries, preferred_element_type=F32) * scale_factor
    )
    value_grad = jnp.einsum(
        "khqs,kqhd->shd", softmax_out.astype(BF16), mixed_grad, preferred_element_type=F32
    )
    return (
        query_grad.reshape(2 * tok_rows, D),
        key_grad.reshape(tok_rows, D),
        value_grad.reshape(tok_rows, D),
    )


def pick(choices, index):
    result = choices[0]
    for i in range(1, len(choices)):
        result = jnp.where(index == i, choices[i], result)
    return result


def split3(v):
    high = lax.reduce_precision(v, exponent_bits=8, mantissa_bits=7)
    middle = lax.reduce_precision(v - high, exponent_bits=8, mantissa_bits=7)
    return [high.astype(BF16), middle.astype(BF16), (v - high - middle).astype(BF16)]


def after(value, *others):
    return lax.optimization_barrier((value, *others))[0]


def per_device(
    tokens,
    cotangent,
    segments,
    att_routes,
    mlp_routes,
    slot_order,
    norm_gains,
    kv_weight,
    router_weight,
    query_weight,
    output_weight,
    gate_up_weight,
    down_weight,
):
    tok_rows = tokens.shape[0]
    experts = lax.axis_size("expert") * query_weight.shape[0]
    ycount = lax.axis_size("y")
    capacity = 2 * tok_rows // experts
    part = norm_gains.shape[0]
    half = D // ycount
    kv_cols = 2 * D // experts
    slice_ff = FF // Z
    pieces = tok_rows // capacity
    y_index = lax.axis_index("y")
    z_index = lax.axis_index("z")
    e_index = lax.axis_index("expert")

    def y_major(v):
        return jnp.concatenate(
            [
                v[:, (z * ycount + y) * part : (z * ycount + y + 1) * part]
                for y in range(ycount)
                for z in range(Z)
            ],
            axis=1,
        )

    def natural(v):
        return jnp.concatenate(
            [
                v[:, (y * Z + z) * part : (y * Z + z + 1) * part]
                for z in range(Z)
                for y in range(ycount)
            ],
            axis=1,
        )

    def halves(v):
        return [v[..., y * half : (y + 1) * half] for y in range(ycount)]

    def own_first(v):
        h = halves(v)
        return jnp.concatenate(
            [pick([h[(i + k) % ycount] for i in range(ycount)], y_index) for k in range(ycount)],
            axis=-1,
        )

    def own_first_back(v):
        h = halves(v)
        return jnp.concatenate(
            [pick([h[(j - i) % ycount] for i in range(ycount)], y_index) for j in range(ycount)],
            axis=-1,
        )

    def exchange(v, axes):
        return lax.all_to_all(v, axes, split_axis=0, concat_axis=0, tiled=True)

    def pack(v):
        return jnp.concatenate(
            [v[..., i * capacity : (i + 1) * capacity, :] for i in range(pieces)], axis=-1
        )

    def unpack(v):
        return jnp.concatenate(
            [v[..., i * kv_cols : (i + 1) * kv_cols] for i in range(pieces)], axis=-2
        )

    both = ("expert", "y")
    js = range(1, ycount)

    shards = Z * ycount
    small = jnp.concatenate([norm_gains, router_weight], axis=1)
    small = jnp.pad(small, ((0, 0), (0, -small.shape[1] % 16))).T
    small = exchange(jnp.broadcast_to(small[None], (shards, *small.shape)), ("y", "z"))
    small = jnp.concatenate([small[i] for i in range(shards)], axis=1)
    kv_part = lax.dynamic_slice_in_dim(kv_weight, e_index * kv_cols, kv_cols, 1)
    wide_both = lax.all_gather(
        jnp.concatenate([query_weight[0], kv_part], axis=1), "z", axis=0, tiled=True
    )
    wide_query, wide_kv = wide_both[:, :D], wide_both[:, D:]
    wide_output = lax.all_gather(output_weight[0], "z", axis=0, tiled=True)

    def z_shift(v, k):
        return lax.ppermute(v, "z", [(i, (i + k) % Z) for i in range(Z)])

    def y_shift(v, k):
        return lax.ppermute(v, "y", [(i, (i + k) % ycount) for i in range(ycount)])

    def columns(weight, k):
        return lax.dynamic_slice_in_dim(weight, ((z_index + k) % Z) * slice_ff, slice_ff, 1)

    def over_z(blocks):
        return [blocks[0]] + [z_shift(blocks[k], k) for k in range(1, Z)]

    def over_y(blocks):
        return {(j, k): y_shift(blocks[k], ycount - j) for j in range(1, ycount) for k in range(Z)}

    def assemble(own, others):
        wide = jnp.zeros((D, own[0].shape[1]), BF16)
        for j in range(ycount):
            for k in range(Z):
                block = own[k] if j == 0 else others[j, k]
                row = j * half + ((z_index - k) % Z) * part
                wide = lax.dynamic_update_slice_in_dim(wide, block, row, 0)
        return wide

    gate_weight, up_weight = gate_up_weight[0][:, :FF], gate_up_weight[0][:, FF:]
    gu_z = over_z(
        [
            jnp.concatenate([columns(gate_weight, k), columns(up_weight, k)], axis=1)
            for k in range(Z)
        ]
    )
    gu_y = over_y(gu_z)
    down_own_y = {j: y_shift(columns(down_weight[0], 0), ycount - j) for j in js}
    wide_gate_up = assemble(gu_z, gu_y)

    segment_row = segments[0]
    fill_order = slot_order[0]
    positions = jnp.arange(tok_rows)
    allowed = (positions[:, None] >= positions[None, :]) & (
        segment_row[:, None] == segment_row[None, :]
    )
    table_att = slot_table(att_routes, fill_order, experts)
    table_mlp = slot_table(mlp_routes, fill_order, experts)
    token_att = table_att[:, :tok_rows] + table_att[:, tok_rows:]
    token_mlp = table_mlp[:, :tok_rows] + table_mlp[:, tok_rows:]

    gain_one = small[0:1].astype(F32)
    gain_two = small[1:2].astype(F32)
    router_att = small[2 : 2 + experts]
    router_mlp = small[2 + experts : 2 + 2 * experts]
    inputs = y_major(tokens).astype(F32)
    grad_out = y_major(cotangent).astype(F32)
    scale_one = lax.rsqrt(jnp.mean(inputs * inputs, axis=1, keepdims=True) + EPSILON)
    normed_one = (inputs * scale_one * gain_one).astype(BF16)

    def to_experts(rows):
        slots = jnp.einsum("zts,ztd->zsd", tables, rows, preferred_element_type=F32).astype(BF16)
        return slots.reshape(Z, experts, capacity, D).transpose(1, 0, 2, 3)

    def to_tokens(rows):
        rows = rows.transpose(1, 0, 2, 3).reshape(Z, 2 * tok_rows, D)
        return jnp.einsum("zts,zsd->ztd", tables, rows, preferred_element_type=F32).astype(BF16)

    grads_z = lax.all_gather(
        jnp.concatenate([own_first(y_major(cotangent)), token_mlp.T], axis=1), "z", axis=0
    )
    tables = grads_z[:, :, D:]
    grad_rows = exchange(to_experts(grads_z[:, :, :D]), "expert").reshape(-1, D)
    att_slots_in = select_rows(token_att, normed_one).reshape(experts, capacity, D)
    send = jnp.stack(
        [
            jnp.concatenate([s, jnp.broadcast_to(n[None], (experts, tok_rows, half))], axis=1)
            for s, n in zip(halves(att_slots_in), halves(normed_one))
        ],
        axis=1,
    )
    got = exchange(send.reshape(experts * ycount, capacity + tok_rows, half), both)
    query_in = got[:, :capacity].reshape(experts * ycount * capacity, half)
    kv_in = got[:, capacity:].reshape(experts * ycount * tok_rows, half)
    own_y = [gu_y[j, 0] for j in js] + list(down_own_y.values())
    query_in, kv_in = lax.optimization_barrier(
        (query_in, kv_in, *own_y)
    )[:2]
    query_part = jnp.dot(query_in, wide_query, preferred_element_type=F32).astype(BF16)
    kv_out = jnp.dot(kv_in, wide_kv, preferred_element_type=F32).astype(BF16)
    back = jnp.concatenate(
        [
            query_part.reshape(experts * ycount, capacity, D),
            pack(kv_out.reshape(experts * ycount, tok_rows, kv_cols)),
        ],
        axis=1,
    )
    back = exchange(back, both).reshape(experts, ycount, 2 * capacity, D)
    back = after(back, grads_z)
    summed = jnp.sum(back.astype(F32), axis=1).astype(BF16)
    query_slots = summed[:, :capacity].reshape(2 * tok_rows, D)
    kv_parts = unpack(summed[:, capacity:])
    keyvals = jnp.concatenate([kv_parts[e] for e in range(experts)], axis=-1)
    key_heads = keyvals[:, :D].reshape(tok_rows, HEADS, HEAD_DIM)
    value_heads = keyvals[:, D:].reshape(tok_rows, HEADS, HEAD_DIM)
    router_logits = lax.dot_general(
        normed_one, router_att, CONTRACT_LAST, preferred_element_type=F32
    )
    gate_att = chosen_gates(router_logits, att_routes, experts)
    query_pairs = spread_rows(table_att, query_slots)
    queries = query_pairs.reshape(2, tok_rows, HEADS, HEAD_DIM)
    mixed_heads, log_sums = attend_forward(queries, key_heads, value_heads, allowed)

    def to_rows(v):
        v = v.reshape(experts, 1, capacity, D)
        v = jnp.broadcast_to(v, (experts, ycount, capacity, D))
        return exchange(v.reshape(experts * ycount, capacity, D), both)

    def from_halves(v):
        v = exchange(v.reshape(experts * ycount, capacity, half), both)
        v = v.reshape(experts, ycount, capacity, half)
        return jnp.concatenate([v[:, y] for y in range(ycount)], axis=-1).reshape(2 * tok_rows, D)

    mixed_slots = after(
        select_rows(table_att, mixed_heads), wide_output, grad_rows, gu_z[1]
    )
    mixed_in = to_rows(mixed_slots).reshape(-1, D)
    projected = lax.dot_general(
        mixed_in, wide_output, CONTRACT_LAST, preferred_element_type=F32
    ).astype(BF16)
    att_slots = after(from_halves(projected), gu_z[2], gu_z[3], *[gu_y[j, 1] for j in js])
    att_pairs = spread_rows(table_att, att_slots).astype(F32).reshape(2, tok_rows, D)
    hidden = inputs + gate_att[:, 0:1] * att_pairs[0] + gate_att[:, 1:2] * att_pairs[1]
    scale_two = lax.rsqrt(jnp.mean(hidden * hidden, axis=1, keepdims=True) + EPSILON)
    normed_two = (hidden * scale_two * gain_two).astype(BF16)
    mlp_logits = lax.dot_general(
        normed_two, router_mlp, CONTRACT_LAST, preferred_element_type=F32
    )
    gate_mlp = chosen_gates(mlp_logits, mlp_routes, experts)

    slot_gates = jnp.sum(
        table_mlp.astype(F32) * jnp.concatenate([gate_mlp[:, 0], gate_mlp[:, 1]])[None], axis=1
    )
    gate_cols = jnp.pad(
        jnp.concatenate(split3(slot_gates.reshape(2, tok_rows).T), axis=1), ((0, 0), (0, 122))
    )
    rows_z = lax.all_gather(
        jnp.concatenate([own_first(normed_two), gate_cols], axis=1), "z", axis=0
    )
    rows_z = after(rows_z, *[gu_y[j, k] for j in js for k in (2, 3)])
    late_down = after(down_weight[0], rows_z)
    down_z = over_z([columns(down_weight[0], 0)] + [columns(late_down, k) for k in range(1, Z)])
    down_y = {(j, k): y_shift(down_z[k], ycount - j) for j in js for k in range(1, Z)}
    wide_down = assemble(down_z, down_y | {(j, 0): down_own_y[j] for j in js})
    gates_z = rows_z[:, :, D:]
    gates_z = jnp.concatenate([gates_z[:, :, 0:6:2], gates_z[:, :, 1:6:2]], axis=1)
    gates_z = jnp.pad(gates_z, ((0, 0), (0, 0), (0, 125)))
    gates_z = gates_z.reshape(Z, experts, capacity, 128).transpose(1, 0, 2, 3)
    got = exchange(
        jnp.concatenate([to_experts(rows_z[:, :, :D]), gates_z], axis=-1), "expert"
    ).reshape(-1, D + 128)
    got = after(got, *down_z[1:], *[down_y[j, k] for j in js for k in (1, 3)])
    ffn_rows = got[:, :D]
    row_gates = jnp.sum(got[:, D : D + 3].astype(F32), axis=1, keepdims=True)
    def outer(left_rows, right_rows):
        return lax.dot_general(left_rows, right_rows, CONTRACT_FIRST, preferred_element_type=F32)

    def block(v, k):
        return lax.dynamic_index_in_dim(v, (z_index + k) % Z, 0, keepdims=False)

    def peers(left, right):
        return [
            outer(left[:, j * half : (j + 1) * half], right)
            .astype(BF16)
            .reshape(Z, part, right.shape[1])
            for j in js
        ]

    def over_y_back(others, k):
        return [y_shift(block(other, k), j) for j, other in zip(js, others)]

    def add_up(own, moved):
        total = own
        for m in moved:
            total = total + m.astype(F32)
        return total

    def in_order(got):
        return [
            pick([got[(z - i) % Z].astype(F32) for z in range(Z)], z_index) for i in range(Z)
        ]

    gate_up = jnp.dot(ffn_rows, wide_gate_up, preferred_element_type=F32)
    gate_part = gate_up[:, :slice_ff]
    up_part = gate_up[:, slice_ff:]
    sigma = jax.nn.sigmoid(gate_part)
    activated = (gate_part * sigma * up_part).astype(BF16)
    gated_rows = (row_gates * grad_rows.astype(F32)).astype(BF16)
    down_peers = peers(gated_rows, activated)
    down_own = outer(gated_rows[:, :half], activated).reshape(Z, part, slice_ff)
    down_moved = {k: over_y_back(down_peers, k) for k in (1, 2, 3)}
    down_got = {
        k: z_shift(add_up(block(down_own, k), down_moved[k]).astype(BF16), k) for k in (1, 2, 3)
    }
    free_grad = jnp.dot(
        after(grad_rows, down_peers, down_own), wide_down, preferred_element_type=F32
    )
    act_grad = free_grad * row_gates
    gate_grad = act_grad * up_part * sigma * (1.0 + gate_part * (1.0 - sigma))
    up_grad = act_grad * gate_part * sigma
    gate_up_grad = jnp.concatenate([gate_grad, up_grad], axis=-1).astype(BF16)
    row_part = lax.dot_general(
        gate_up_grad, wide_gate_up, CONTRACT_LAST, preferred_element_type=F32
    ).astype(BF16)

    row_part = after(row_part, *down_moved[1])
    gu_peers = peers(ffn_rows, gate_up_grad)
    gu_moved = {k: over_y_back(gu_peers, k) for k in (1, 2, 3)}
    slot_sums = jnp.sum(activated.astype(F32) * free_grad, axis=1, keepdims=True)
    slot_sums = jnp.pad(jnp.concatenate(split3(slot_sums), axis=1), ((0, 0), (0, 125)))
    back = exchange(
        jnp.concatenate([row_part, slot_sums], axis=1).reshape(
            experts, Z, capacity, D + 128
        ),
        "expert",
    )
    back = after(back, *gu_moved[1], *down_moved[2], *down_moved[3], down_got[1], down_got[3])
    sums = back[..., D : D + 3].transpose(1, 0, 2, 3).reshape(Z, 2 * tok_rows, 3)
    sums = jnp.concatenate([sums[:, :tok_rows], sums[:, tok_rows:]], axis=-1)
    sums = jnp.concatenate(
        [jnp.where(z_index == z, sums, jnp.zeros_like(sums)) for z in range(Z)], axis=-1
    )
    sums = jnp.pad(sums, ((0, 0), (0, 0), (0, 128 - 6 * Z)))
    row_back = back
    back = lax.psum_scatter(
        jnp.concatenate([to_tokens(back[..., :D]), sums], axis=-1).reshape(-1, D + 128),
        "z",
        scatter_dimension=0,
        tiled=True,
    )
    ffn_row_grads = own_first_back(back[:, :D]).astype(F32)
    sums = back[:, D : D + 6 * Z].astype(F32).reshape(tok_rows, Z, 2, 3)
    sums = jnp.sum(sums, axis=(1, 3)).T.reshape(2 * tok_rows, 1)
    gate_mlp_grad = jnp.sum(table_mlp.astype(F32) * sums, axis=0).reshape(2, tok_rows).T

    out_part = (
        row_gates
        * lax.dot_general(after(activated, row_back), wide_down, CONTRACT_LAST, preferred_element_type=F32)
    ).astype(BF16)
    out_part = to_tokens(exchange(out_part.reshape(experts, Z, capacity, D), "expert"))
    ffn_out = lax.psum_scatter(
        out_part.reshape(-1, D), "z", scatter_dimension=0, tiled=True
    )

    gu_own = outer(ffn_rows[:, :half], gate_up_grad).reshape(Z, part, 2 * slice_ff)
    gu_got = {
        k: z_shift(add_up(block(gu_own, k), gu_moved[k]).astype(BF16), k) for k in (1, 2, 3)
    }

    ffn_row_grads = after(ffn_row_grads, *gu_moved[2], out_part, down_got[2], gu_got[1])
    logit_mlp_grad = gate_logit_grad(gate_mlp, gate_mlp_grad, mlp_routes, experts)
    normed_two_grad = (
        ffn_row_grads
        + jnp.dot(logit_mlp_grad, router_mlp.astype(F32), precision=HIGHEST)
    )
    hidden_grad = grad_out + norm_back(hidden, scale_two, gain_two, normed_two_grad)
    gate_att_grad = jnp.sum(hidden_grad[None] * att_pairs, axis=2).T
    logit_att_grad = gate_logit_grad(gate_att, gate_att_grad, att_routes, experts)
    gated_hidden = jnp.concatenate(
        [gate_att[:, 0:1] * hidden_grad, gate_att[:, 1:2] * hidden_grad], axis=0
    ).astype(BF16)
    hidden_send = select_rows(table_att, gated_hidden).reshape(experts, capacity, D)
    hidden_in = exchange(
        jnp.stack(halves(hidden_send), axis=1).reshape(experts * ycount, capacity, half), both
    ).reshape(-1, half)
    hidden_in = after(hidden_in, *gu_moved[3])
    head_part = jnp.dot(hidden_in, wide_output, preferred_element_type=F32).astype(BF16)
    head_part = exchange(head_part.reshape(experts * ycount, capacity, D), both)
    head_part = after(head_part, gu_got[3])
    head_slots = jnp.sum(
        head_part.reshape(experts, ycount, capacity, D).astype(F32), axis=1
    ).astype(BF16)
    mixed_grad = spread_rows(table_att, head_slots.reshape(2 * tok_rows, D)).reshape(
        2, tok_rows, HEADS, HEAD_DIM
    )
    output_grad = lax.psum_scatter(
        outer(hidden_in, mixed_in).astype(BF16), "z", scatter_dimension=0, tiled=True
    ).astype(F32)[None]
    query_grad, key_grad, value_grad = attend_backward(
        queries, key_heads, value_heads, allowed, log_sums, mixed_grad
    )
    late_gu, late_down = lax.optimization_barrier((gu_peers, down_peers, head_part))[:2]
    gu_moved[0] = over_y_back(late_gu, 0)
    down_moved[0] = over_y_back(late_down, 0)
    keyval_row_grad = jnp.concatenate([key_grad, value_grad], axis=1).astype(BF16)
    query_send = select_rows(table_att, query_grad.astype(BF16)).reshape(experts, capacity, D)
    kv_send = pack(
        jnp.stack([keyval_row_grad[:, e * kv_cols : (e + 1) * kv_cols] for e in range(experts)])
    )
    send = jnp.concatenate([query_send, kv_send], axis=1).reshape(experts, 1, 2 * capacity, D)
    send = jnp.broadcast_to(send, (experts, ycount, 2 * capacity, D))
    got = exchange(send.reshape(experts * ycount, 2 * capacity, D), both)
    got = after(got, output_grad, gu_got[2], *gu_moved[0])
    block_out = (hidden + own_first_back(after(ffn_out, got)).astype(F32)).astype(BF16)
    query_rows = got[:, :capacity].reshape(-1, D)
    kv_rows = unpack(got[:, capacity:]).reshape(-1, kv_cols)
    input_part = lax.dot_general(
        query_rows, wide_query, CONTRACT_LAST, preferred_element_type=F32
    ).astype(BF16)
    normed_part = lax.dot_general(
        kv_rows, wide_kv, CONTRACT_LAST, preferred_element_type=F32
    ).astype(BF16)
    back = jnp.concatenate(
        [
            input_part.reshape(experts * ycount, capacity, half),
            normed_part.reshape(experts * ycount, tok_rows, half),
        ],
        axis=1,
    )
    query_outer = outer(query_in, query_rows).astype(BF16)
    kv_outer = outer(kv_in, kv_rows).astype(BF16)
    back = after(back, query_outer, kv_outer)
    back = exchange(back, both).reshape(experts, ycount, capacity + tok_rows, half)
    back = after(back, *down_moved[0], ffn_out)
    gu_got[0] = add_up(block(gu_own, 0), gu_moved[0])
    down_got[0] = add_up(block(down_own, 0), down_moved[0])
    gu_grads = in_order(gu_got)
    gate_up_weight_grad = jnp.concatenate(
        [g[:, :slice_ff] for g in gu_grads] + [g[:, slice_ff:] for g in gu_grads], axis=1
    )[None]
    down_weight_grad = jnp.concatenate(in_order(down_got), axis=1)[None]
    back = jnp.concatenate([back[:, y] for y in range(ycount)], axis=-1)
    input_pairs = (
        spread_rows(table_att, back[:, :capacity].reshape(2 * tok_rows, D))
        .astype(F32)
        .reshape(2, tok_rows, D)
    )
    kv_grad_part = lax.psum_scatter(kv_outer, "z", scatter_dimension=0, tiled=True)
    query_weight_grad = lax.psum_scatter(
        query_outer, "z", scatter_dimension=0, tiled=True
    ).astype(F32)[None]
    kv_grads = exchange(
        jnp.broadcast_to(kv_grad_part[None], (experts, *kv_grad_part.shape)), "expert"
    )
    keyval_grad = jnp.concatenate([kv_grads[e] for e in range(experts)], axis=1).astype(F32)
    normed_one_grad = (
        input_pairs[0] + input_pairs[1] + jnp.sum(back[:, capacity:].astype(F32), axis=0)
    )
    normed_one_grad = normed_one_grad + jnp.dot(
        logit_att_grad, router_att.astype(F32), precision=HIGHEST
    )
    input_grad = natural(
        hidden_grad + norm_back(inputs, scale_one, gain_one, normed_one_grad)
    )

    small_grads = jnp.concatenate(
        [
            jnp.sum(normed_one_grad * inputs * scale_one, axis=0)[None],
            jnp.sum(normed_two_grad * hidden * scale_two, axis=0)[None],
            lax.dot_general(
                logit_att_grad, normed_one.astype(F32), CONTRACT_FIRST, precision=HIGHEST
            ),
            lax.dot_general(
                logit_mlp_grad, normed_two.astype(F32), CONTRACT_FIRST, precision=HIGHEST
            ),
        ],
        axis=0,
    )
    rows = small_grads.shape[0]
    small_grads = jnp.stack(
        [small_grads[:, i * part : (i + 1) * part] for i in range(Z * ycount)]
    )
    small_grads = jnp.sum(exchange(small_grads, ("y", "z")), axis=0)
    small_grads = exchange(
        jnp.broadcast_to(small_grads[None], (experts, rows, part)), "expert"
    )
    small_grads = jnp.sum(small_grads, axis=0).T
    gains_grad = small_grads[:, :2]
    router_grad = small_grads[:, 2:rows]
    return (
        natural(block_out),
        input_grad,
        gains_grad,
        keyval_grad,
        router_grad,
        query_weight_grad,
        output_grad,
        gate_up_weight_grad,
        down_weight_grad,
    )


def solution(mesh):
    experts, shards = mesh.shape["expert"], mesh.shape["shard"]
    grid = Mesh(mesh.devices.reshape(experts, Z, shards // Z), ("expert", "z", "y"))
    rows = P(("expert", "z", "y"), None)
    shared = P(("z", "y"), None)
    owned = P("expert", ("z", "y"), None)
    in_specs = (rows,) * 6 + (shared,) * 3 + (owned,) * 4
    out_specs = (rows,) * 2 + (shared,) * 3 + (owned,) * 4
    return jax.shard_map(
        per_device, mesh=grid, in_specs=in_specs, out_specs=out_specs, check_vma=False
    )
```

```python
import jax
import jax.numpy as jnp
from jax import lax
from jax.sharding import Mesh
from jax.sharding import PartitionSpec as P

D = 2048
HEADS = 16
HEAD_DIM = 128
FF = 5632
Z = 4

EPSILON = 1e-05
NEGATIVE = -1e30
HIGHEST = lax.Precision.HIGHEST
CONTRACT_FIRST = (((0,), (0,)), ((), ()))
CONTRACT_LAST = (((1,), (1,)), ((), ()))
BF16 = jnp.bfloat16
F32 = jnp.float32

FROM = {
    "projected": ["gate_up_y3"],
    "row_slots": ["gate_up_grad_y0"],
    "hidden_rows": ["down_grad_z3"],
}
WAIT = {
    "projections": ["down_y0", "gate_up_y0"],
    "attended": ["down_z1", "down_z2", "gate_up_z2", "output_weight"],
    "projected": ["cotangent_rows", "down_y1", "down_y2", "down_y3", "down_z3", "gate_up_y2", "gate_up_z1"],
    "gathered_rows": ["cotangent_slots"],
    "expert_rows": ["gate_up_y1", "gate_up_z3"],
    "hidden_units": ["gate_up_grad_y3"],
    "row_grads": ["down_grad_y2", "output_slots"],
    "hidden_rows": ["down_grad_y0", "gate_up_grad_y0", "gate_up_grad_z1", "output_rows"],
    "head_slots": ["down_grad_y3"],
    "query_grads": ["down_grad_y1", "gate_up_grad_z3"],
    "query_rows": ["down_grad_z1"],
    "input_slots": ["down_grad_z3", "gate_up_grad_y1"],
    "small": ["down_grad_z2", "gate_up_grad_peers", "gate_up_grad_y2", "output_grad"],
}


def slot_table(routes, fill_order, experts):
    pair_count = 2 * routes.shape[0]
    capacity = pair_count // experts
    pair_index = jnp.arange(pair_count, dtype=jnp.int32)
    pair_expert = jnp.concatenate([routes[:, 0], routes[:, 1]]).astype(F32)
    reorder = (fill_order[:, None] == pair_index[None, :]).astype(F32)
    ordered = jnp.dot(reorder, pair_expert, precision=HIGHEST)
    onehot = (ordered[:, None] == jnp.arange(experts, dtype=F32)[None, :]).astype(F32)
    below_mask = (pair_index[:, None] > pair_index[None, :]).astype(F32)
    earlier = jnp.dot(below_mask, onehot, precision=HIGHEST)
    position = jnp.sum(earlier * onehot, axis=1)
    target = ordered * capacity + position
    placing = (
        (target[:, None] == pair_index.astype(F32)[None, :]) & (position < capacity)[:, None]
    ).astype(F32)
    return lax.dot_general(placing, reorder, CONTRACT_FIRST, precision=HIGHEST).astype(BF16)


def select_rows(table, pair_rows):
    return jnp.dot(table, pair_rows, preferred_element_type=F32).astype(BF16)


def spread_rows(table, slot_rows):
    return lax.dot_general(table, slot_rows, CONTRACT_FIRST, preferred_element_type=F32).astype(BF16)


def chosen_gates(logits, routes, experts):
    expert_ids = jnp.arange(experts, dtype=jnp.int32)[None, :]
    first_logit = jnp.sum(jnp.where(routes[:, 0:1] == expert_ids, logits, 0.0), axis=1)
    second_logit = jnp.sum(jnp.where(routes[:, 1:2] == expert_ids, logits, 0.0), axis=1)
    return jax.nn.softmax(jnp.stack([first_logit, second_logit], axis=1), axis=1)


def gate_logit_grad(gate_pair, gate_grad, routes, experts):
    expert_ids = jnp.arange(experts, dtype=jnp.int32)[None, :]
    chosen_grad = gate_pair * (gate_grad - jnp.sum(gate_pair * gate_grad, axis=1, keepdims=True))
    first_part = chosen_grad[:, 0:1] * (routes[:, 0:1] == expert_ids).astype(F32)
    return first_part + chosen_grad[:, 1:2] * (routes[:, 1:2] == expert_ids).astype(F32)


def norm_back(values, scale, gain_row, normed_grad):
    scaled = normed_grad * gain_row
    return scale * (
        scaled - values * scale * scale * jnp.mean(scaled * values, axis=1, keepdims=True)
    )


def attend_forward(queries, key_heads, value_heads, allowed):
    tok_rows = key_heads.shape[0]
    scores = jnp.einsum("kqhd,shd->khqs", queries, key_heads, preferred_element_type=F32) * (
        HEAD_DIM ** (-0.5)
    )
    masked = jnp.where(allowed[None, None], scores, NEGATIVE)
    row_max = jnp.max(masked, axis=-1, keepdims=True)
    exponent = jnp.exp(masked - row_max)
    totals = jnp.sum(exponent, axis=-1, keepdims=True)
    softmax_out = (exponent / totals).astype(BF16)
    mixed = jnp.einsum("khqs,shd->kqhd", softmax_out, value_heads, preferred_element_type=F32)
    mixed = mixed.astype(BF16).reshape(2 * tok_rows, HEADS * HEAD_DIM)
    return mixed, (row_max + jnp.log(totals))[..., 0]


def attend_backward(queries, key_heads, value_heads, allowed, log_sums, mixed_grad):
    tok_rows = key_heads.shape[0]
    scale_factor = HEAD_DIM ** (-0.5)
    scores = (
        jnp.einsum("kqhd,shd->khqs", queries, key_heads, preferred_element_type=F32) * scale_factor
    )
    softmax_out = jnp.where(allowed[None, None], jnp.exp(scores - log_sums[..., None]), 0.0)
    prob_grad = jnp.einsum("kqhd,shd->khqs", mixed_grad, value_heads, preferred_element_type=F32)
    score_grad = (
        softmax_out * (prob_grad - jnp.sum(softmax_out * prob_grad, axis=-1, keepdims=True))
    ).astype(BF16)
    query_grad = (
        jnp.einsum("khqs,shd->kqhd", score_grad, key_heads, preferred_element_type=F32)
        * scale_factor
    )
    key_grad = (
        jnp.einsum("khqs,kqhd->shd", score_grad, queries, preferred_element_type=F32) * scale_factor
    )
    value_grad = jnp.einsum(
        "khqs,kqhd->shd", softmax_out.astype(BF16), mixed_grad, preferred_element_type=F32
    )
    return (
        query_grad.reshape(2 * tok_rows, D),
        key_grad.reshape(tok_rows, D),
        value_grad.reshape(tok_rows, D),
    )


def pick(choices, index):
    result = choices[0]
    for i in range(1, len(choices)):
        result = jnp.where(index == i, choices[i], result)
    return result


def split3(v):
    high = lax.reduce_precision(v, exponent_bits=8, mantissa_bits=7)
    middle = lax.reduce_precision(v - high, exponent_bits=8, mantissa_bits=7)
    return [high.astype(BF16), middle.astype(BF16), (v - high - middle).astype(BF16)]


def after(value, *others):
    return lax.optimization_barrier((value, *others))[0]


def per_device(
    tokens,
    cotangent,
    segments,
    att_routes,
    mlp_routes,
    slot_order,
    norm_gains,
    kv_weight,
    router_weight,
    query_weight,
    output_weight,
    gate_up_weight,
    down_weight,
):
    tok_rows = tokens.shape[0]
    experts = lax.axis_size("expert") * query_weight.shape[0]
    ycount = lax.axis_size("y")
    capacity = 2 * tok_rows // experts
    part = norm_gains.shape[0]
    half = D // ycount
    kv_cols = 2 * D // experts
    slice_ff = FF // Z
    pieces = tok_rows // capacity
    y_index = lax.axis_index("y")
    z_index = lax.axis_index("z")
    e_index = lax.axis_index("expert")

    def y_major(v):
        return jnp.concatenate(
            [
                v[:, (z * ycount + y) * part : (z * ycount + y + 1) * part]
                for y in range(ycount)
                for z in range(Z)
            ],
            axis=1,
        )

    def natural(v):
        return jnp.concatenate(
            [
                v[:, (y * Z + z) * part : (y * Z + z + 1) * part]
                for z in range(Z)
                for y in range(ycount)
            ],
            axis=1,
        )

    def halves(v):
        return [v[..., y * half : (y + 1) * half] for y in range(ycount)]

    def own_first(v):
        h = halves(v)
        return jnp.concatenate(
            [pick([h[(i + k) % ycount] for i in range(ycount)], y_index) for k in range(ycount)],
            axis=-1,
        )

    def own_first_back(v):
        h = halves(v)
        return jnp.concatenate(
            [pick([h[(j - i) % ycount] for i in range(ycount)], y_index) for j in range(ycount)],
            axis=-1,
        )

    def exchange(v, axes):
        return lax.all_to_all(v, axes, split_axis=0, concat_axis=0, tiled=True)

    def pack(v):
        return jnp.concatenate(
            [v[..., i * capacity : (i + 1) * capacity, :] for i in range(pieces)], axis=-1
        )

    def unpack(v):
        return jnp.concatenate(
            [v[..., i * kv_cols : (i + 1) * kv_cols] for i in range(pieces)], axis=-2
        )

    both = ("expert", "y")
    js = range(1, ycount)

    shards = Z * ycount
    small = jnp.concatenate([norm_gains, router_weight], axis=1)
    small = jnp.pad(small, ((0, 0), (0, -small.shape[1] % 16))).T
    small = exchange(jnp.broadcast_to(small[None], (shards, *small.shape)), ("y", "z"))
    small = jnp.concatenate([small[i] for i in range(shards)], axis=1)
    kv_part = lax.dynamic_slice_in_dim(kv_weight, e_index * kv_cols, kv_cols, 1)
    wide_both = lax.all_gather(
        jnp.concatenate([query_weight[0], kv_part], axis=1), "z", axis=0, tiled=True
    )
    wide_query, wide_kv = wide_both[:, :D], wide_both[:, D:]
    wide_output = lax.all_gather(output_weight[0], "z", axis=0, tiled=True)

    def z_shift(v, k, name):
        with jax.named_scope(f"{name}_z{k}"):
            return lax.ppermute(v, "z", [(i, (i + k) % Z) for i in range(Z)])

    def y_shift(v, k, name):
        with jax.named_scope(name):
            return lax.ppermute(v, "y", [(i, (i + k) % ycount) for i in range(ycount)])

    gu_weight, dn_weight = gate_up_weight[0], down_weight[0]
    gate_weight, up_weight = gu_weight[:, :FF], gu_weight[:, FF:]
    moved = {}
    makers = {}

    def columns(weight, k):
        return lax.dynamic_slice_in_dim(weight, ((z_index + k) % Z) * slice_ff, slice_ff, 1)

    def weight_columns(part_name, k):
        if part_name == "down":
            return columns(dn_weight, k)
        return jnp.concatenate([columns(gate_weight, k), columns(up_weight, k)], axis=1)

    def fetch(name):
        if name not in moved:
            moved[name] = makers[name]()
        return moved[name]

    def step(name, value):
        value = lax.optimization_barrier(
            (value, [fetch(n) for n in WAIT.get(name, ()) if n in makers])
        )[0]
        for n in FROM.get(name, ()):
            if n not in moved:
                moved[n] = makers[n](value)
        return value

    def weight_makers(part_name):
        for k in range(Z):

            def over_z(*others, k=k):
                own = after(weight_columns(part_name, k), *others)
                return z_shift(own, k, part_name) if k else own

            def over_y(*others, k=k):
                own = after(fetch(f"{part_name}_z{k}"), *others)
                return [y_shift(own, ycount - j, f"{part_name}_y{k}") for j in js]

            makers[f"{part_name}_z{k}"] = over_z
            makers[f"{part_name}_y{k}"] = over_y

    def assemble(part_name):
        rows = [[fetch(f"{part_name}_z{k}") for k in range(Z)]]
        rows += [[fetch(f"{part_name}_y{k}")[j - 1] for k in range(Z)] for j in js]
        wide = jnp.zeros((D, rows[0][0].shape[1]), BF16)
        for j in range(ycount):
            for k in range(Z):
                row = j * half + ((z_index - k) % Z) * part
                wide = lax.dynamic_update_slice_in_dim(wide, rows[j][k], row, 0)
        return wide

    weight_makers("down")
    weight_makers("gate_up")
    step("start", ())

    segment_row = segments[0]
    fill_order = slot_order[0]
    positions = jnp.arange(tok_rows)
    allowed = (positions[:, None] >= positions[None, :]) & (
        segment_row[:, None] == segment_row[None, :]
    )
    table_att = slot_table(att_routes, fill_order, experts)
    table_mlp = slot_table(mlp_routes, fill_order, experts)
    token_att = table_att[:, :tok_rows] + table_att[:, tok_rows:]
    token_mlp = table_mlp[:, :tok_rows] + table_mlp[:, tok_rows:]

    gain_one = small[0:1].astype(F32)
    gain_two = small[1:2].astype(F32)
    router_att = small[2 : 2 + experts]
    router_mlp = small[2 + experts : 2 + 2 * experts]
    inputs = y_major(tokens).astype(F32)
    grad_out = y_major(cotangent).astype(F32)
    scale_one = lax.rsqrt(jnp.mean(inputs * inputs, axis=1, keepdims=True) + EPSILON)
    normed_one = (inputs * scale_one * gain_one).astype(BF16)

    def to_experts(rows):
        slots = jnp.einsum("zts,ztd->zsd", tables, rows, preferred_element_type=F32).astype(BF16)
        return slots.reshape(Z, experts, capacity, D).transpose(1, 0, 2, 3)

    def to_tokens(rows):
        rows = rows.transpose(1, 0, 2, 3).reshape(Z, 2 * tok_rows, D)
        return jnp.einsum("zts,zsd->ztd", tables, rows, preferred_element_type=F32).astype(BF16)

    grads_z = lax.all_gather(
        jnp.concatenate([own_first(y_major(cotangent)), token_mlp.T], axis=1), "z", axis=0
    )
    tables = grads_z[:, :, D:]
    grad_rows = exchange(to_experts(grads_z[:, :, :D]), "expert").reshape(-1, D)
    att_slots_in = select_rows(token_att, normed_one).reshape(experts, capacity, D)
    send = jnp.stack(
        [
            jnp.concatenate([s, jnp.broadcast_to(n[None], (experts, tok_rows, half))], axis=1)
            for s, n in zip(halves(att_slots_in), halves(normed_one))
        ],
        axis=1,
    )
    got = exchange(send.reshape(experts * ycount, capacity + tok_rows, half), both)
    query_in = got[:, :capacity].reshape(experts * ycount * capacity, half)
    kv_in = got[:, capacity:].reshape(experts * ycount * tok_rows, half)
    query_in, kv_in = step("projections", (query_in, kv_in))
    query_part = jnp.dot(query_in, wide_query, preferred_element_type=F32).astype(BF16)
    kv_out = jnp.dot(kv_in, wide_kv, preferred_element_type=F32).astype(BF16)
    back = jnp.concatenate(
        [
            query_part.reshape(experts * ycount, capacity, D),
            pack(kv_out.reshape(experts * ycount, tok_rows, kv_cols)),
        ],
        axis=1,
    )
    back = exchange(back, both).reshape(experts, ycount, 2 * capacity, D)
    makers["cotangent_rows"] = lambda: grads_z
    makers["cotangent_slots"] = lambda: grad_rows
    makers["output_weight"] = lambda: wide_output
    back = step("queries", back)
    summed = jnp.sum(back.astype(F32), axis=1).astype(BF16)
    query_slots = summed[:, :capacity].reshape(2 * tok_rows, D)
    kv_parts = unpack(summed[:, capacity:])
    keyvals = jnp.concatenate([kv_parts[e] for e in range(experts)], axis=-1)
    key_heads = keyvals[:, :D].reshape(tok_rows, HEADS, HEAD_DIM)
    value_heads = keyvals[:, D:].reshape(tok_rows, HEADS, HEAD_DIM)
    router_logits = lax.dot_general(
        normed_one, router_att, CONTRACT_LAST, preferred_element_type=F32
    )
    gate_att = chosen_gates(router_logits, att_routes, experts)
    query_pairs = spread_rows(table_att, query_slots)
    queries = query_pairs.reshape(2, tok_rows, HEADS, HEAD_DIM)
    mixed_heads, log_sums = attend_forward(queries, key_heads, value_heads, allowed)

    def to_rows(v):
        v = v.reshape(experts, 1, capacity, D)
        v = jnp.broadcast_to(v, (experts, ycount, capacity, D))
        return exchange(v.reshape(experts * ycount, capacity, D), both)

    def from_halves(v):
        v = exchange(v.reshape(experts * ycount, capacity, half), both)
        v = v.reshape(experts, ycount, capacity, half)
        return jnp.concatenate([v[:, y] for y in range(ycount)], axis=-1).reshape(2 * tok_rows, D)

    mixed_slots = step("attended", select_rows(table_att, mixed_heads))
    mixed_in = step("attended_rows", to_rows(mixed_slots).reshape(-1, D))
    projected = lax.dot_general(
        mixed_in, wide_output, CONTRACT_LAST, preferred_element_type=F32
    ).astype(BF16)
    att_slots = step("projected", from_halves(projected))
    att_pairs = spread_rows(table_att, att_slots).astype(F32).reshape(2, tok_rows, D)
    hidden = inputs + gate_att[:, 0:1] * att_pairs[0] + gate_att[:, 1:2] * att_pairs[1]
    scale_two = lax.rsqrt(jnp.mean(hidden * hidden, axis=1, keepdims=True) + EPSILON)
    normed_two = (hidden * scale_two * gain_two).astype(BF16)
    mlp_logits = lax.dot_general(
        normed_two, router_mlp, CONTRACT_LAST, preferred_element_type=F32
    )
    gate_mlp = chosen_gates(mlp_logits, mlp_routes, experts)

    slot_gates = jnp.sum(
        table_mlp.astype(F32) * jnp.concatenate([gate_mlp[:, 0], gate_mlp[:, 1]])[None], axis=1
    )
    gate_cols = jnp.pad(
        jnp.concatenate(split3(slot_gates.reshape(2, tok_rows).T), axis=1), ((0, 0), (0, 122))
    )
    rows_z = lax.all_gather(
        jnp.concatenate([own_first(normed_two), gate_cols], axis=1), "z", axis=0
    )
    rows_z = step("gathered_rows", rows_z)
    gates_z = rows_z[:, :, D:]
    gates_z = jnp.concatenate([gates_z[:, :, 0:6:2], gates_z[:, :, 1:6:2]], axis=1)
    gates_z = jnp.pad(gates_z, ((0, 0), (0, 0), (0, 125)))
    gates_z = gates_z.reshape(Z, experts, capacity, 128).transpose(1, 0, 2, 3)
    got = exchange(
        jnp.concatenate([to_experts(rows_z[:, :, :D]), gates_z], axis=-1), "expert"
    ).reshape(-1, D + 128)
    got = step("expert_rows", got)
    wide_down, wide_gate_up = assemble("down"), assemble("gate_up")
    free_grad = jnp.dot(grad_rows, wide_down, preferred_element_type=F32)
    got = after(got, free_grad)
    ffn_rows = got[:, :D]
    row_gates = jnp.sum(got[:, D : D + 3].astype(F32), axis=1, keepdims=True)
    gate_up = jnp.dot(ffn_rows, wide_gate_up, preferred_element_type=F32)
    gate_part = gate_up[:, :slice_ff]
    up_part = gate_up[:, slice_ff:]
    sigma = jax.nn.sigmoid(gate_part)
    activated = (gate_part * sigma * up_part).astype(BF16)
    act_grad = free_grad * row_gates
    gate_grad = act_grad * up_part * sigma * (1.0 + gate_part * (1.0 - sigma))
    up_grad = act_grad * gate_part * sigma
    gate_up_grad = jnp.concatenate([gate_grad, up_grad], axis=-1).astype(BF16)
    row_part = lax.dot_general(
        gate_up_grad, wide_gate_up, CONTRACT_LAST, preferred_element_type=F32
    ).astype(BF16)

    def outer(left_rows, right_rows):
        return lax.dot_general(left_rows, right_rows, CONTRACT_FIRST, preferred_element_type=F32)

    def block(v, k):
        return lax.dynamic_index_in_dim(v, (z_index + k) % Z, 0, keepdims=False)

    def peers(left, right):
        return [
            outer(left[:, j * half : (j + 1) * half], right)
            .astype(BF16)
            .reshape(Z, part, right.shape[1])
            for j in js
        ]

    def add_up(own, moved):
        total = own
        for m in moved:
            total = total + m.astype(F32)
        return total

    def grad_makers(part_name, left, right):
        others = peers(left, right)
        own = outer(left[:, :half], right).reshape(Z, part, right.shape[1])
        for k in range(Z):

            def over_y(*steps, k=k):
                return [
                    y_shift(after(block(other, k), *steps), j, f"{part_name}_y{k}")
                    for j, other in zip(js, others)
                ]

            def over_z(*steps, k=k):
                total = add_up(block(own, k), fetch(f"{part_name}_y{k}"))
                return z_shift(after(total.astype(BF16), *steps), k, part_name) if k else total

            makers[f"{part_name}_y{k}"] = over_y
            makers[f"{part_name}_z{k}"] = over_z
        makers[f"{part_name}_peers"] = lambda: others
        makers[f"{part_name}_own"] = lambda: own

    def in_order(got):
        return [
            pick([got[(z - i) % Z].astype(F32) for z in range(Z)], z_index) for i in range(Z)
        ]

    gated_rows = (row_gates * grad_rows.astype(F32)).astype(BF16)
    grad_makers("gate_up_grad", ffn_rows, gate_up_grad)
    grad_makers("down_grad", gated_rows, activated)
    row_part = step("hidden_units", row_part)
    slot_sums = jnp.sum(activated.astype(F32) * free_grad, axis=1, keepdims=True)
    slot_sums = jnp.pad(jnp.concatenate(split3(slot_sums), axis=1), ((0, 0), (0, 125)))
    back = exchange(
        jnp.concatenate([row_part, slot_sums], axis=1).reshape(
            experts, Z, capacity, D + 128
        ),
        "expert",
    )
    back = step("row_slots", back)
    sums = back[..., D : D + 3].transpose(1, 0, 2, 3).reshape(Z, 2 * tok_rows, 3)
    sums = jnp.concatenate([sums[:, :tok_rows], sums[:, tok_rows:]], axis=-1)
    sums = jnp.concatenate(
        [jnp.where(z_index == z, sums, jnp.zeros_like(sums)) for z in range(Z)], axis=-1
    )
    sums = jnp.pad(sums, ((0, 0), (0, 0), (0, 128 - 6 * Z)))
    row_back = back
    back = lax.psum_scatter(
        jnp.concatenate([to_tokens(back[..., :D]), sums], axis=-1).reshape(-1, D + 128),
        "z",
        scatter_dimension=0,
        tiled=True,
    )
    ffn_row_grads = own_first_back(back[:, :D]).astype(F32)
    sums = back[:, D : D + 6 * Z].astype(F32).reshape(tok_rows, Z, 2, 3)
    sums = jnp.sum(sums, axis=(1, 3)).T.reshape(2 * tok_rows, 1)
    gate_mlp_grad = jnp.sum(table_mlp.astype(F32) * sums, axis=0).reshape(2, tok_rows).T

    out_part = (
        row_gates
        * lax.dot_general(after(activated, row_back), wide_down, CONTRACT_LAST, preferred_element_type=F32)
    ).astype(BF16)
    out_part = to_tokens(exchange(out_part.reshape(experts, Z, capacity, D), "expert"))
    ffn_out = lax.psum_scatter(
        out_part.reshape(-1, D), "z", scatter_dimension=0, tiled=True
    )

    makers["output_slots"] = lambda: out_part
    makers["output_rows"] = lambda: ffn_out
    ffn_row_grads = step("row_grads", ffn_row_grads)
    logit_mlp_grad = gate_logit_grad(gate_mlp, gate_mlp_grad, mlp_routes, experts)
    normed_two_grad = (
        ffn_row_grads
        + jnp.dot(logit_mlp_grad, router_mlp.astype(F32), precision=HIGHEST)
    )
    hidden_grad = grad_out + norm_back(hidden, scale_two, gain_two, normed_two_grad)
    gate_att_grad = jnp.sum(hidden_grad[None] * att_pairs, axis=2).T
    logit_att_grad = gate_logit_grad(gate_att, gate_att_grad, att_routes, experts)
    gated_hidden = jnp.concatenate(
        [gate_att[:, 0:1] * hidden_grad, gate_att[:, 1:2] * hidden_grad], axis=0
    ).astype(BF16)
    hidden_send = select_rows(table_att, gated_hidden).reshape(experts, capacity, D)
    hidden_in = exchange(
        jnp.stack(halves(hidden_send), axis=1).reshape(experts * ycount, capacity, half), both
    ).reshape(-1, half)
    hidden_in = step("hidden_rows", hidden_in)
    head_part = jnp.dot(hidden_in, wide_output, preferred_element_type=F32).astype(BF16)
    head_part = exchange(head_part.reshape(experts * ycount, capacity, D), both)
    head_part = step("head_slots", head_part)
    head_slots = jnp.sum(
        head_part.reshape(experts, ycount, capacity, D).astype(F32), axis=1
    ).astype(BF16)
    mixed_grad = spread_rows(table_att, head_slots.reshape(2 * tok_rows, D)).reshape(
        2, tok_rows, HEADS, HEAD_DIM
    )
    makers["output_grad"] = lambda *others: lax.psum_scatter(
        outer(after(hidden_in, *others), mixed_in).astype(BF16),
        "z",
        scatter_dimension=0,
        tiled=True,
    )
    query_grad, key_grad, value_grad = attend_backward(
        queries, key_heads, value_heads, allowed, log_sums, mixed_grad
    )
    query_grad = step("query_grads", query_grad)
    keyval_row_grad = jnp.concatenate([key_grad, value_grad], axis=1).astype(BF16)
    query_send = select_rows(table_att, query_grad.astype(BF16)).reshape(experts, capacity, D)
    kv_send = pack(
        jnp.stack([keyval_row_grad[:, e * kv_cols : (e + 1) * kv_cols] for e in range(experts)])
    )
    send = jnp.concatenate([query_send, kv_send], axis=1).reshape(experts, 1, 2 * capacity, D)
    send = jnp.broadcast_to(send, (experts, ycount, 2 * capacity, D))
    got = exchange(send.reshape(experts * ycount, 2 * capacity, D), both)
    got = step("query_rows", got)
    block_out = (hidden + own_first_back(after(ffn_out, got)).astype(F32)).astype(BF16)
    query_rows = got[:, :capacity].reshape(-1, D)
    kv_rows = unpack(got[:, capacity:]).reshape(-1, kv_cols)
    input_part = lax.dot_general(
        query_rows, wide_query, CONTRACT_LAST, preferred_element_type=F32
    ).astype(BF16)
    normed_part = lax.dot_general(
        kv_rows, wide_kv, CONTRACT_LAST, preferred_element_type=F32
    ).astype(BF16)
    back = jnp.concatenate(
        [
            input_part.reshape(experts * ycount, capacity, half),
            normed_part.reshape(experts * ycount, tok_rows, half),
        ],
        axis=1,
    )
    query_outer = outer(query_in, query_rows).astype(BF16)
    kv_outer = outer(kv_in, kv_rows).astype(BF16)
    back = after(back, query_outer, kv_outer)
    back = exchange(back, both).reshape(experts, ycount, capacity + tok_rows, half)
    back = step("input_slots", back)
    gu_grads = in_order([fetch(f"gate_up_grad_z{k}") for k in range(Z)])
    down_grads = in_order([fetch(f"down_grad_z{k}") for k in range(Z)])
    gate_up_weight_grad = jnp.concatenate(
        [g[:, :slice_ff] for g in gu_grads] + [g[:, slice_ff:] for g in gu_grads], axis=1
    )[None]
    down_weight_grad = jnp.concatenate(down_grads, axis=1)[None]
    output_grad = fetch("output_grad").astype(F32)[None]
    back = jnp.concatenate([back[:, y] for y in range(ycount)], axis=-1)
    input_pairs = (
        spread_rows(table_att, back[:, :capacity].reshape(2 * tok_rows, D))
        .astype(F32)
        .reshape(2, tok_rows, D)
    )
    kv_grad_part = lax.psum_scatter(kv_outer, "z", scatter_dimension=0, tiled=True)
    query_weight_grad = lax.psum_scatter(
        query_outer, "z", scatter_dimension=0, tiled=True
    ).astype(F32)[None]
    kv_grads = exchange(
        jnp.broadcast_to(kv_grad_part[None], (experts, *kv_grad_part.shape)), "expert"
    )
    keyval_grad = jnp.concatenate([kv_grads[e] for e in range(experts)], axis=1).astype(F32)
    normed_one_grad = (
        input_pairs[0] + input_pairs[1] + jnp.sum(back[:, capacity:].astype(F32), axis=0)
    )
    normed_one_grad = normed_one_grad + jnp.dot(
        logit_att_grad, router_att.astype(F32), precision=HIGHEST
    )
    input_grad = natural(
        hidden_grad + norm_back(inputs, scale_one, gain_one, normed_one_grad)
    )

    small_grads = jnp.concatenate(
        [
            jnp.sum(normed_one_grad * inputs * scale_one, axis=0)[None],
            jnp.sum(normed_two_grad * hidden * scale_two, axis=0)[None],
            lax.dot_general(
                logit_att_grad, normed_one.astype(F32), CONTRACT_FIRST, precision=HIGHEST
            ),
            lax.dot_general(
                logit_mlp_grad, normed_two.astype(F32), CONTRACT_FIRST, precision=HIGHEST
            ),
        ],
        axis=0,
    )
    rows = small_grads.shape[0]
    small_grads = jnp.stack(
        [small_grads[:, i * part : (i + 1) * part] for i in range(Z * ycount)]
    )
    small_grads = step("small", exchange(small_grads, ("y", "z")))
    small_grads = jnp.sum(small_grads, axis=0)
    small_grads = exchange(
        jnp.broadcast_to(small_grads[None], (experts, rows, part)), "expert"
    )
    small_grads = jnp.sum(small_grads, axis=0).T
    gains_grad = small_grads[:, :2]
    router_grad = small_grads[:, 2:rows]
    return (
        natural(block_out),
        input_grad,
        gains_grad,
        keyval_grad,
        router_grad,
        query_weight_grad,
        output_grad,
        gate_up_weight_grad,
        down_weight_grad,
    )


def solution(mesh):
    experts, shards = mesh.shape["expert"], mesh.shape["shard"]
    grid = Mesh(mesh.devices.reshape(experts, Z, shards // Z), ("expert", "z", "y"))
    rows = P(("expert", "z", "y"), None)
    shared = P(("z", "y"), None)
    owned = P("expert", ("z", "y"), None)
    in_specs = (rows,) * 6 + (shared,) * 3 + (owned,) * 4
    out_specs = (rows,) * 2 + (shared,) * 3 + (owned,) * 4
    return jax.shard_map(
        per_device, mesh=grid, in_specs=in_specs, out_specs=out_specs, check_vma=False
    )
```

```python
import jax
import jax.numpy as jnp
from jax import lax
from jax.sharding import Mesh
from jax.sharding import PartitionSpec as P

D = 2048
HEADS = 16
HEAD_DIM = 128
FF = 5632
Z = 4

EPSILON = 1e-05
NEGATIVE = -1e30
HIGHEST = lax.Precision.HIGHEST
CONTRACT_FIRST = (((0,), (0,)), ((), ()))
CONTRACT_LAST = (((1,), (1,)), ((), ()))
BF16 = jnp.bfloat16
F32 = jnp.float32

FROM = {
    "projections": ["down_z1", "gate_up_y0", "gate_up_z2"],
    "queries": ["gate_up_y2"],
    "attended": ["down_y1"],
    "row_slots": ["down_grad_y1"],
    "row_grads": ["down_grad_y3"],
    "query_grads": ["down_grad_y0", "down_grad_z2", "down_grad_z3", "gate_up_grad_y0"],
    "query_rows": ["down_grad_z1"],
}
WAIT = {
    "projections": ["down_y2"],
    "queries": ["cotangent_rows", "gate_up_y0"],
    "attended": ["cotangent_slots", "down_z1", "down_z2", "down_z3"],
    "attended_rows": ["down_y0", "down_y1", "down_y3", "output_weight"],
    "projected": ["gate_up_y1", "gate_up_z2"],
    "expert_rows": ["gate_up_y2", "gate_up_z1", "gate_up_z3"],
    "hidden_units": ["gate_up_grad_y2"],
    "row_grads": ["output_slots"],
    "hidden_rows": ["gate_up_grad_y3", "gate_up_grad_z1"],
    "head_slots": ["down_grad_y2"],
    "query_grads": ["down_grad_y1", "down_grad_y3", "gate_up_grad_z2", "gate_up_grad_z3", "output_rows"],
    "query_rows": ["gate_up_grad_y0"],
    "input_slots": ["down_grad_y0", "down_grad_z1", "down_grad_z3", "output_grad"],
    "small": ["down_grad_z2"],
}
CHUNKS = 2


def slot_table(routes, fill_order, experts):
    pair_count = 2 * routes.shape[0]
    capacity = pair_count // experts
    pair_index = jnp.arange(pair_count, dtype=jnp.int32)
    pair_expert = jnp.concatenate([routes[:, 0], routes[:, 1]]).astype(F32)
    reorder = (fill_order[:, None] == pair_index[None, :]).astype(F32)
    ordered = jnp.dot(reorder, pair_expert, precision=HIGHEST)
    onehot = (ordered[:, None] == jnp.arange(experts, dtype=F32)[None, :]).astype(F32)
    below_mask = (pair_index[:, None] > pair_index[None, :]).astype(F32)
    earlier = jnp.dot(below_mask, onehot, precision=HIGHEST)
    position = jnp.sum(earlier * onehot, axis=1)
    target = ordered * capacity + position
    placing = (
        (target[:, None] == pair_index.astype(F32)[None, :]) & (position < capacity)[:, None]
    ).astype(F32)
    return lax.dot_general(placing, reorder, CONTRACT_FIRST, precision=HIGHEST).astype(BF16)


def select_rows(table, pair_rows):
    return jnp.dot(table, pair_rows, preferred_element_type=F32).astype(BF16)


def spread_rows(table, slot_rows):
    return lax.dot_general(table, slot_rows, CONTRACT_FIRST, preferred_element_type=F32).astype(BF16)


def chosen_gates(logits, routes, experts):
    expert_ids = jnp.arange(experts, dtype=jnp.int32)[None, :]
    first_logit = jnp.sum(jnp.where(routes[:, 0:1] == expert_ids, logits, 0.0), axis=1)
    second_logit = jnp.sum(jnp.where(routes[:, 1:2] == expert_ids, logits, 0.0), axis=1)
    return jax.nn.softmax(jnp.stack([first_logit, second_logit], axis=1), axis=1)


def gate_logit_grad(gate_pair, gate_grad, routes, experts):
    expert_ids = jnp.arange(experts, dtype=jnp.int32)[None, :]
    chosen_grad = gate_pair * (gate_grad - jnp.sum(gate_pair * gate_grad, axis=1, keepdims=True))
    first_part = chosen_grad[:, 0:1] * (routes[:, 0:1] == expert_ids).astype(F32)
    return first_part + chosen_grad[:, 1:2] * (routes[:, 1:2] == expert_ids).astype(F32)


def norm_back(values, scale, gain_row, normed_grad):
    scaled = normed_grad * gain_row
    return scale * (
        scaled - values * scale * scale * jnp.mean(scaled * values, axis=1, keepdims=True)
    )


def attend_forward(queries, key_heads, value_heads, allowed):
    tok_rows = key_heads.shape[0]
    scores = jnp.einsum("kqhd,shd->khqs", queries, key_heads, preferred_element_type=F32) * (
        HEAD_DIM ** (-0.5)
    )
    masked = jnp.where(allowed[None, None], scores, NEGATIVE)
    row_max = jnp.max(masked, axis=-1, keepdims=True)
    exponent = jnp.exp(masked - row_max)
    totals = jnp.sum(exponent, axis=-1, keepdims=True)
    softmax_out = (exponent / totals).astype(BF16)
    mixed = jnp.einsum("khqs,shd->kqhd", softmax_out, value_heads, preferred_element_type=F32)
    mixed = mixed.astype(BF16).reshape(2 * tok_rows, HEADS * HEAD_DIM)
    return mixed, (row_max + jnp.log(totals))[..., 0]


def attend_backward(queries, key_heads, value_heads, allowed, log_sums, mixed_grad):
    tok_rows = key_heads.shape[0]
    scale_factor = HEAD_DIM ** (-0.5)
    scores = (
        jnp.einsum("kqhd,shd->khqs", queries, key_heads, preferred_element_type=F32) * scale_factor
    )
    softmax_out = jnp.where(allowed[None, None], jnp.exp(scores - log_sums[..., None]), 0.0)
    prob_grad = jnp.einsum("kqhd,shd->khqs", mixed_grad, value_heads, preferred_element_type=F32)
    score_grad = (
        softmax_out * (prob_grad - jnp.sum(softmax_out * prob_grad, axis=-1, keepdims=True))
    ).astype(BF16)
    query_grad = (
        jnp.einsum("khqs,shd->kqhd", score_grad, key_heads, preferred_element_type=F32)
        * scale_factor
    )
    key_grad = (
        jnp.einsum("khqs,kqhd->shd", score_grad, queries, preferred_element_type=F32) * scale_factor
    )
    value_grad = jnp.einsum(
        "khqs,kqhd->shd", softmax_out.astype(BF16), mixed_grad, preferred_element_type=F32
    )
    return (
        query_grad.reshape(2 * tok_rows, D),
        key_grad.reshape(tok_rows, D),
        value_grad.reshape(tok_rows, D),
    )


def pick(choices, index):
    result = choices[0]
    for i in range(1, len(choices)):
        result = jnp.where(index == i, choices[i], result)
    return result


def split3(v):
    high = lax.reduce_precision(v, exponent_bits=8, mantissa_bits=7)
    middle = lax.reduce_precision(v - high, exponent_bits=8, mantissa_bits=7)
    return [high.astype(BF16), middle.astype(BF16), (v - high - middle).astype(BF16)]


def after(value, *others):
    return lax.optimization_barrier((value, *others))[0]


def per_device(
    tokens,
    cotangent,
    segments,
    att_routes,
    mlp_routes,
    slot_order,
    norm_gains,
    kv_weight,
    router_weight,
    query_weight,
    output_weight,
    gate_up_weight,
    down_weight,
):
    tok_rows = tokens.shape[0]
    experts = lax.axis_size("expert") * query_weight.shape[0]
    ycount = lax.axis_size("y")
    capacity = 2 * tok_rows // experts
    part = norm_gains.shape[0]
    half = D // ycount
    kv_cols = 2 * D // experts
    slice_ff = FF // Z
    pieces = tok_rows // capacity
    y_index = lax.axis_index("y")
    z_index = lax.axis_index("z")
    e_index = lax.axis_index("expert")

    def y_major(v):
        return jnp.concatenate(
            [
                v[:, (z * ycount + y) * part : (z * ycount + y + 1) * part]
                for y in range(ycount)
                for z in range(Z)
            ],
            axis=1,
        )

    def natural(v):
        return jnp.concatenate(
            [
                v[:, (y * Z + z) * part : (y * Z + z + 1) * part]
                for z in range(Z)
                for y in range(ycount)
            ],
            axis=1,
        )

    def halves(v):
        return [v[..., y * half : (y + 1) * half] for y in range(ycount)]

    def own_first(v):
        h = halves(v)
        return jnp.concatenate(
            [pick([h[(i + k) % ycount] for i in range(ycount)], y_index) for k in range(ycount)],
            axis=-1,
        )

    def own_first_back(v):
        h = halves(v)
        return jnp.concatenate(
            [pick([h[(j - i) % ycount] for i in range(ycount)], y_index) for j in range(ycount)],
            axis=-1,
        )

    def exchange(v, axes):
        return lax.all_to_all(v, axes, split_axis=0, concat_axis=0, tiled=True)

    def pack(v):
        return jnp.concatenate(
            [v[..., i * capacity : (i + 1) * capacity, :] for i in range(pieces)], axis=-1
        )

    def unpack(v):
        return jnp.concatenate(
            [v[..., i * kv_cols : (i + 1) * kv_cols] for i in range(pieces)], axis=-2
        )

    both = ("expert", "y")
    js = range(1, ycount)

    shards = Z * ycount
    small = jnp.concatenate([norm_gains, router_weight], axis=1)
    small = jnp.pad(small, ((0, 0), (0, -small.shape[1] % 16))).T
    small = exchange(jnp.broadcast_to(small[None], (shards, *small.shape)), ("y", "z"))
    small = jnp.concatenate([small[i] for i in range(shards)], axis=1)
    kv_part = lax.dynamic_slice_in_dim(kv_weight, e_index * kv_cols, kv_cols, 1)
    wide_both = lax.all_gather(
        jnp.concatenate([query_weight[0], kv_part], axis=1), "z", axis=0, tiled=True
    )
    wide_query, wide_kv = wide_both[:, :D], wide_both[:, D:]
    wide_output = lax.all_gather(output_weight[0], "z", axis=0, tiled=True)

    def z_shift(v, k, name):
        with jax.named_scope(f"{name}_z{k}"):
            return lax.ppermute(v, "z", [(i, (i + k) % Z) for i in range(Z)])

    def y_shift(v, k, name):
        with jax.named_scope(name):
            return lax.ppermute(v, "y", [(i, (i + k) % ycount) for i in range(ycount)])

    gu_weight, dn_weight = gate_up_weight[0], down_weight[0]
    gate_weight, up_weight = gu_weight[:, :FF], gu_weight[:, FF:]
    moved = {}
    makers = {}

    def columns(weight, k):
        return lax.dynamic_slice_in_dim(weight, ((z_index + k) % Z) * slice_ff, slice_ff, 1)

    def weight_columns(part_name, k):
        if part_name == "down":
            return columns(dn_weight, k)
        return jnp.concatenate([columns(gate_weight, k), columns(up_weight, k)], axis=1)

    def fetch(name):
        if name not in moved:
            moved[name] = makers[name]()
        return moved[name]

    def step(name, value):
        value = lax.optimization_barrier(
            (value, [fetch(n) for n in WAIT.get(name, ()) if n in makers])
        )[0]
        for n in FROM.get(name, ()):
            if n not in moved:
                moved[n] = makers[n](value)
        return value

    def weight_makers(part_name):
        for k in range(Z):

            def over_z(*others, k=k):
                own = after(weight_columns(part_name, k), *others)
                return z_shift(own, k, part_name) if k else own

            def over_y(*others, k=k):
                own = after(fetch(f"{part_name}_z{k}"), *others)
                return [y_shift(own, ycount - j, f"{part_name}_y{k}") for j in js]

            makers[f"{part_name}_z{k}"] = over_z
            makers[f"{part_name}_y{k}"] = over_y

    def assemble(part_name):
        rows = [[fetch(f"{part_name}_z{k}") for k in range(Z)]]
        rows += [[fetch(f"{part_name}_y{k}")[j - 1] for k in range(Z)] for j in js]
        wide = jnp.zeros((D, rows[0][0].shape[1]), BF16)
        for j in range(ycount):
            for k in range(Z):
                row = j * half + ((z_index - k) % Z) * part
                wide = lax.dynamic_update_slice_in_dim(wide, rows[j][k], row, 0)
        return wide

    weight_makers("down")
    weight_makers("gate_up")
    step("start", ())

    segment_row = segments[0]
    fill_order = slot_order[0]
    positions = jnp.arange(tok_rows)
    allowed = (positions[:, None] >= positions[None, :]) & (
        segment_row[:, None] == segment_row[None, :]
    )
    table_att = slot_table(att_routes, fill_order, experts)
    table_mlp = slot_table(mlp_routes, fill_order, experts)
    token_att = table_att[:, :tok_rows] + table_att[:, tok_rows:]
    token_mlp = table_mlp[:, :tok_rows] + table_mlp[:, tok_rows:]

    gain_one = small[0:1].astype(F32)
    gain_two = small[1:2].astype(F32)
    router_att = small[2 : 2 + experts]
    router_mlp = small[2 + experts : 2 + 2 * experts]
    inputs = y_major(tokens).astype(F32)
    grad_out = y_major(cotangent).astype(F32)
    scale_one = lax.rsqrt(jnp.mean(inputs * inputs, axis=1, keepdims=True) + EPSILON)
    normed_one = (inputs * scale_one * gain_one).astype(BF16)

    def to_experts(rows):
        slots = jnp.einsum("zts,ztd->zsd", tables, rows, preferred_element_type=F32).astype(BF16)
        return slots.reshape(Z, experts, capacity, D).transpose(1, 0, 2, 3)

    def to_tokens(rows):
        rows = rows.transpose(1, 0, 2, 3).reshape(Z, 2 * tok_rows, D)
        return jnp.einsum("zts,zsd->ztd", tables, rows, preferred_element_type=F32).astype(BF16)

    grads_z = lax.all_gather(
        jnp.concatenate([own_first(y_major(cotangent)), token_mlp.T], axis=1), "z", axis=0
    )
    tables = grads_z[:, :, D:]
    sub = capacity // CHUNKS
    grad_slots = exchange(to_experts(grads_z[:, :, :D]), "expert")
    grad_rows = jnp.concatenate(
        [grad_slots[:, :, c * sub : (c + 1) * sub].reshape(-1, D) for c in range(CHUNKS)], axis=0
    )
    att_slots_in = select_rows(token_att, normed_one).reshape(experts, capacity, D)
    send = jnp.stack(
        [
            jnp.concatenate([s, jnp.broadcast_to(n[None], (experts, tok_rows, half))], axis=1)
            for s, n in zip(halves(att_slots_in), halves(normed_one))
        ],
        axis=1,
    )
    got = exchange(send.reshape(experts * ycount, capacity + tok_rows, half), both)
    query_in = got[:, :capacity].reshape(experts * ycount * capacity, half)
    kv_in = got[:, capacity:].reshape(experts * ycount * tok_rows, half)
    query_in, kv_in = step("projections", (query_in, kv_in))
    query_part = jnp.dot(query_in, wide_query, preferred_element_type=F32).astype(BF16)
    kv_out = jnp.dot(kv_in, wide_kv, preferred_element_type=F32).astype(BF16)
    back = jnp.concatenate(
        [
            query_part.reshape(experts * ycount, capacity, D),
            pack(kv_out.reshape(experts * ycount, tok_rows, kv_cols)),
        ],
        axis=1,
    )
    back = exchange(back, both).reshape(experts, ycount, 2 * capacity, D)
    makers["cotangent_rows"] = lambda: grads_z
    makers["cotangent_slots"] = lambda: grad_rows
    makers["output_weight"] = lambda: wide_output
    back = step("queries", back)
    summed = jnp.sum(back.astype(F32), axis=1).astype(BF16)
    query_slots = summed[:, :capacity].reshape(2 * tok_rows, D)
    kv_parts = unpack(summed[:, capacity:])
    keyvals = jnp.concatenate([kv_parts[e] for e in range(experts)], axis=-1)
    key_heads = keyvals[:, :D].reshape(tok_rows, HEADS, HEAD_DIM)
    value_heads = keyvals[:, D:].reshape(tok_rows, HEADS, HEAD_DIM)
    router_logits = lax.dot_general(
        normed_one, router_att, CONTRACT_LAST, preferred_element_type=F32
    )
    gate_att = chosen_gates(router_logits, att_routes, experts)
    query_pairs = spread_rows(table_att, query_slots)
    queries = query_pairs.reshape(2, tok_rows, HEADS, HEAD_DIM)
    mixed_heads, log_sums = attend_forward(queries, key_heads, value_heads, allowed)

    def to_rows(v):
        v = v.reshape(experts, 1, capacity, D)
        v = jnp.broadcast_to(v, (experts, ycount, capacity, D))
        return exchange(v.reshape(experts * ycount, capacity, D), both)

    def from_halves(v):
        v = exchange(v.reshape(experts * ycount, capacity, half), both)
        v = v.reshape(experts, ycount, capacity, half)
        return jnp.concatenate([v[:, y] for y in range(ycount)], axis=-1).reshape(2 * tok_rows, D)

    mixed_slots = step("attended", select_rows(table_att, mixed_heads))
    mixed_in = step("attended_rows", to_rows(mixed_slots).reshape(-1, D))
    projected = lax.dot_general(
        mixed_in, wide_output, CONTRACT_LAST, preferred_element_type=F32
    ).astype(BF16)
    att_slots = step("projected", from_halves(projected))
    att_pairs = spread_rows(table_att, att_slots).astype(F32).reshape(2, tok_rows, D)
    hidden = inputs + gate_att[:, 0:1] * att_pairs[0] + gate_att[:, 1:2] * att_pairs[1]
    scale_two = lax.rsqrt(jnp.mean(hidden * hidden, axis=1, keepdims=True) + EPSILON)
    normed_two = (hidden * scale_two * gain_two).astype(BF16)
    mlp_logits = lax.dot_general(
        normed_two, router_mlp, CONTRACT_LAST, preferred_element_type=F32
    )
    gate_mlp = chosen_gates(mlp_logits, mlp_routes, experts)

    slot_gates = jnp.sum(
        table_mlp.astype(F32) * jnp.concatenate([gate_mlp[:, 0], gate_mlp[:, 1]])[None], axis=1
    )
    gate_cols = jnp.pad(
        jnp.concatenate(split3(slot_gates.reshape(2, tok_rows).T), axis=1), ((0, 0), (0, 122))
    )
    rows_z = lax.all_gather(
        jnp.concatenate([own_first(normed_two), gate_cols], axis=1), "z", axis=0
    )
    rows_z = step("gathered_rows", rows_z)
    gates_z = rows_z[:, :, D:]
    gates_z = jnp.concatenate([gates_z[:, :, 0:6:2], gates_z[:, :, 1:6:2]], axis=1)
    gates_z = jnp.pad(gates_z, ((0, 0), (0, 0), (0, 125)))
    gates_z = gates_z.reshape(Z, experts, capacity, 128).transpose(1, 0, 2, 3)
    send = jnp.concatenate([to_experts(rows_z[:, :, :D]), gates_z], axis=-1)
    got = [
        exchange(send[:, :, c * sub : (c + 1) * sub], "expert").reshape(-1, D + 128)
        for c in range(CHUNKS)
    ]
    got[0] = step("expert_rows", got[0])
    wide_down, wide_gate_up = assemble("down"), assemble("gate_up")
    free_grad = jnp.dot(grad_rows, wide_down, preferred_element_type=F32)
    got[0] = after(got[0], free_grad)
    chunk_rows = grad_rows.shape[0] // CHUNKS

    def hidden_units(c):
        rows = got[c][:, :D]
        gates = jnp.sum(got[c][:, D : D + 3].astype(F32), axis=1, keepdims=True)
        free = free_grad[c * chunk_rows : (c + 1) * chunk_rows]
        gate_up = jnp.dot(rows, wide_gate_up, preferred_element_type=F32)
        gate_part = gate_up[:, :slice_ff]
        up_part = gate_up[:, slice_ff:]
        sigma = jax.nn.sigmoid(gate_part)
        activated = (gate_part * sigma * up_part).astype(BF16)
        act_grad = free * gates
        gate_grad = act_grad * up_part * sigma * (1.0 + gate_part * (1.0 - sigma))
        up_grad = act_grad * gate_part * sigma
        gate_up_grad = jnp.concatenate([gate_grad, up_grad], axis=-1).astype(BF16)
        row_part = lax.dot_general(
            gate_up_grad, wide_gate_up, CONTRACT_LAST, preferred_element_type=F32
        ).astype(BF16)
        sums = jnp.sum(activated.astype(F32) * free, axis=1, keepdims=True)
        sums = jnp.pad(jnp.concatenate(split3(sums), axis=1), ((0, 0), (0, 125)))
        row_part = jnp.concatenate([row_part, sums], axis=1)
        return rows, gates, activated, gate_up_grad, row_part

    units = [hidden_units(c) for c in range(CHUNKS)]
    ffn_rows, row_gates, activated, gate_up_grad = (
        jnp.concatenate(v, axis=0) for v in list(zip(*units))[:4]
    )

    def outer(left_rows, right_rows):
        return lax.dot_general(left_rows, right_rows, CONTRACT_FIRST, preferred_element_type=F32)

    def block(v, k):
        return lax.dynamic_index_in_dim(v, (z_index + k) % Z, 0, keepdims=False)

    def peers(left, right):
        return [
            outer(left[:, j * half : (j + 1) * half], right)
            .astype(BF16)
            .reshape(Z, part, right.shape[1])
            for j in js
        ]

    def add_up(own, moved):
        total = own
        for m in moved:
            total = total + m.astype(F32)
        return total

    def grad_makers(part_name, left, right):
        others = peers(left, right)
        own = outer(left[:, :half], right).reshape(Z, part, right.shape[1])
        for k in range(Z):

            def over_y(*steps, k=k):
                return [
                    y_shift(after(block(other, k), *steps), j, f"{part_name}_y{k}")
                    for j, other in zip(js, others)
                ]

            def over_z(*steps, k=k):
                total = add_up(block(own, k), fetch(f"{part_name}_y{k}"))
                return z_shift(after(total.astype(BF16), *steps), k, part_name) if k else total

            makers[f"{part_name}_y{k}"] = over_y
            makers[f"{part_name}_z{k}"] = over_z
        makers[f"{part_name}_peers"] = lambda: others
        makers[f"{part_name}_own"] = lambda: own

    def in_order(got):
        return [
            pick([got[(z - i) % Z].astype(F32) for z in range(Z)], z_index) for i in range(Z)
        ]

    gated_rows = (row_gates * grad_rows.astype(F32)).astype(BF16)
    grad_makers("gate_up_grad", ffn_rows, gate_up_grad)
    grad_makers("down_grad", gated_rows, activated)
    last_part = step("hidden_units", units[-1][4])
    back = jnp.concatenate(
        [
            exchange(v.reshape(experts, Z, sub, D + 128), "expert")
            for v in [u[4] for u in units[:-1]] + [last_part]
        ],
        axis=2,
    )
    back = step("row_slots", back)
    sums = back[..., D : D + 3].transpose(1, 0, 2, 3).reshape(Z, 2 * tok_rows, 3)
    sums = jnp.concatenate([sums[:, :tok_rows], sums[:, tok_rows:]], axis=-1)
    sums = jnp.concatenate(
        [jnp.where(z_index == z, sums, jnp.zeros_like(sums)) for z in range(Z)], axis=-1
    )
    sums = jnp.pad(sums, ((0, 0), (0, 0), (0, 128 - 6 * Z)))
    row_back = back
    back = lax.psum_scatter(
        jnp.concatenate([to_tokens(back[..., :D]), sums], axis=-1).reshape(-1, D + 128),
        "z",
        scatter_dimension=0,
        tiled=True,
    )
    ffn_row_grads = own_first_back(back[:, :D]).astype(F32)
    sums = back[:, D : D + 6 * Z].astype(F32).reshape(tok_rows, Z, 2, 3)
    sums = jnp.sum(sums, axis=(1, 3)).T.reshape(2 * tok_rows, 1)
    gate_mlp_grad = jnp.sum(table_mlp.astype(F32) * sums, axis=0).reshape(2, tok_rows).T

    def output_slots(*others):
        out_part = (
            row_gates
            * lax.dot_general(
                after(activated, row_back, *others),
                wide_down,
                CONTRACT_LAST,
                preferred_element_type=F32,
            )
        ).astype(BF16)
        out_part = out_part.reshape(CHUNKS, experts, Z, sub, D).transpose(1, 2, 0, 3, 4)
        return to_tokens(exchange(out_part.reshape(experts, Z, capacity, D), "expert"))

    makers["output_slots"] = output_slots
    makers["output_rows"] = lambda: lax.psum_scatter(
        fetch("output_slots").reshape(-1, D), "z", scatter_dimension=0, tiled=True
    )
    ffn_row_grads = step("row_grads", ffn_row_grads)
    logit_mlp_grad = gate_logit_grad(gate_mlp, gate_mlp_grad, mlp_routes, experts)
    normed_two_grad = (
        ffn_row_grads
        + jnp.dot(logit_mlp_grad, router_mlp.astype(F32), precision=HIGHEST)
    )
    hidden_grad = grad_out + norm_back(hidden, scale_two, gain_two, normed_two_grad)
    gate_att_grad = jnp.sum(hidden_grad[None] * att_pairs, axis=2).T
    logit_att_grad = gate_logit_grad(gate_att, gate_att_grad, att_routes, experts)
    gated_hidden = jnp.concatenate(
        [gate_att[:, 0:1] * hidden_grad, gate_att[:, 1:2] * hidden_grad], axis=0
    ).astype(BF16)
    hidden_send = select_rows(table_att, gated_hidden).reshape(experts, capacity, D)
    hidden_in = exchange(
        jnp.stack(halves(hidden_send), axis=1).reshape(experts * ycount, capacity, half), both
    ).reshape(-1, half)
    hidden_in = step("hidden_rows", hidden_in)
    head_part = jnp.dot(hidden_in, wide_output, preferred_element_type=F32).astype(BF16)
    head_part = exchange(head_part.reshape(experts * ycount, capacity, D), both)
    head_part = step("head_slots", head_part)
    head_slots = jnp.sum(
        head_part.reshape(experts, ycount, capacity, D).astype(F32), axis=1
    ).astype(BF16)
    mixed_grad = spread_rows(table_att, head_slots.reshape(2 * tok_rows, D)).reshape(
        2, tok_rows, HEADS, HEAD_DIM
    )
    makers["output_grad"] = lambda *others: lax.psum_scatter(
        outer(after(hidden_in, *others), mixed_in).astype(BF16),
        "z",
        scatter_dimension=0,
        tiled=True,
    )
    query_grad, key_grad, value_grad = attend_backward(
        queries, key_heads, value_heads, allowed, log_sums, mixed_grad
    )
    query_grad = step("query_grads", query_grad)
    keyval_row_grad = jnp.concatenate([key_grad, value_grad], axis=1).astype(BF16)
    query_send = select_rows(table_att, query_grad.astype(BF16)).reshape(experts, capacity, D)
    kv_send = pack(
        jnp.stack([keyval_row_grad[:, e * kv_cols : (e + 1) * kv_cols] for e in range(experts)])
    )
    send = jnp.concatenate([query_send, kv_send], axis=1).reshape(experts, 1, 2 * capacity, D)
    send = jnp.broadcast_to(send, (experts, ycount, 2 * capacity, D))
    got = exchange(send.reshape(experts * ycount, 2 * capacity, D), both)
    got = step("query_rows", got)
    block_out = (hidden + own_first_back(after(fetch("output_rows"), got)).astype(F32)).astype(BF16)
    query_rows = got[:, :capacity].reshape(-1, D)
    kv_rows = unpack(got[:, capacity:]).reshape(-1, kv_cols)
    input_part = lax.dot_general(
        query_rows, wide_query, CONTRACT_LAST, preferred_element_type=F32
    ).astype(BF16)
    normed_part = lax.dot_general(
        kv_rows, wide_kv, CONTRACT_LAST, preferred_element_type=F32
    ).astype(BF16)
    back = jnp.concatenate(
        [
            input_part.reshape(experts * ycount, capacity, half),
            normed_part.reshape(experts * ycount, tok_rows, half),
        ],
        axis=1,
    )
    query_outer = outer(query_in, query_rows).astype(BF16)
    kv_outer = outer(kv_in, kv_rows).astype(BF16)
    back = after(back, query_outer, kv_outer)
    back = exchange(back, both).reshape(experts, ycount, capacity + tok_rows, half)
    back = step("input_slots", back)
    gu_grads = in_order([fetch(f"gate_up_grad_z{k}") for k in range(Z)])
    down_grads = in_order([fetch(f"down_grad_z{k}") for k in range(Z)])
    gate_up_weight_grad = jnp.concatenate(
        [g[:, :slice_ff] for g in gu_grads] + [g[:, slice_ff:] for g in gu_grads], axis=1
    )[None]
    down_weight_grad = jnp.concatenate(down_grads, axis=1)[None]
    output_grad = fetch("output_grad").astype(F32)[None]
    back = jnp.concatenate([back[:, y] for y in range(ycount)], axis=-1)
    input_pairs = (
        spread_rows(table_att, back[:, :capacity].reshape(2 * tok_rows, D))
        .astype(F32)
        .reshape(2, tok_rows, D)
    )
    kv_grad_part = lax.psum_scatter(kv_outer, "z", scatter_dimension=0, tiled=True)
    query_weight_grad = lax.psum_scatter(
        query_outer, "z", scatter_dimension=0, tiled=True
    ).astype(F32)[None]
    kv_grads = exchange(
        jnp.broadcast_to(kv_grad_part[None], (experts, *kv_grad_part.shape)), "expert"
    )
    keyval_grad = jnp.concatenate([kv_grads[e] for e in range(experts)], axis=1).astype(F32)
    normed_one_grad = (
        input_pairs[0] + input_pairs[1] + jnp.sum(back[:, capacity:].astype(F32), axis=0)
    )
    normed_one_grad = normed_one_grad + jnp.dot(
        logit_att_grad, router_att.astype(F32), precision=HIGHEST
    )
    input_grad = natural(
        hidden_grad + norm_back(inputs, scale_one, gain_one, normed_one_grad)
    )

    small_grads = jnp.concatenate(
        [
            jnp.sum(normed_one_grad * inputs * scale_one, axis=0)[None],
            jnp.sum(normed_two_grad * hidden * scale_two, axis=0)[None],
            lax.dot_general(
                logit_att_grad, normed_one.astype(F32), CONTRACT_FIRST, precision=HIGHEST
            ),
            lax.dot_general(
                logit_mlp_grad, normed_two.astype(F32), CONTRACT_FIRST, precision=HIGHEST
            ),
        ],
        axis=0,
    )
    rows = small_grads.shape[0]
    small_grads = jnp.stack(
        [small_grads[:, i * part : (i + 1) * part] for i in range(Z * ycount)]
    )
    small_grads = step("small", exchange(small_grads, ("y", "z")))
    small_grads = jnp.sum(small_grads, axis=0)
    small_grads = exchange(
        jnp.broadcast_to(small_grads[None], (experts, rows, part)), "expert"
    )
    small_grads = jnp.sum(small_grads, axis=0).T
    gains_grad = small_grads[:, :2]
    router_grad = small_grads[:, 2:rows]
    return (
        natural(block_out),
        input_grad,
        gains_grad,
        keyval_grad,
        router_grad,
        query_weight_grad,
        output_grad,
        gate_up_weight_grad,
        down_weight_grad,
    )


def solution(mesh):
    experts, shards = mesh.shape["expert"], mesh.shape["shard"]
    grid = Mesh(mesh.devices.reshape(experts, Z, shards // Z), ("expert", "z", "y"))
    rows = P(("expert", "z", "y"), None)
    shared = P(("z", "y"), None)
    owned = P("expert", ("z", "y"), None)
    in_specs = (rows,) * 6 + (shared,) * 3 + (owned,) * 4
    out_specs = (rows,) * 2 + (shared,) * 3 + (owned,) * 4
    return jax.shard_map(
        per_device, mesh=grid, in_specs=in_specs, out_specs=out_specs, check_vma=False
    )
```

```python
import jax
import jax.numpy as jnp
from jax import lax
from jax.sharding import Mesh
from jax.sharding import PartitionSpec as P

D = 2048
HEADS = 16
HEAD_DIM = 128
FF = 5632
Z = 4

EPSILON = 1e-05
NEGATIVE = -1e30
HIGHEST = lax.Precision.HIGHEST
CONTRACT_FIRST = (((0,), (0,)), ((), ()))
CONTRACT_LAST = (((1,), (1,)), ((), ()))
BF16 = jnp.bfloat16
F32 = jnp.float32

FROM = {
    "projections": ["down_z1", "gate_up_y0", "gate_up_z2"],
    "attended": ["down_y1"],
    "row_slots": ["down_grad_y1"],
    "row_grads": ["down_grad_y3"],
    "query_grads": ["down_grad_y0", "down_grad_z2", "down_grad_z3", "gate_up_grad_y0"],
    "query_rows": ["down_grad_z1"],
}
WAIT = {
    "projections": ["down_y2"],
    "queries": ["cotangent_rows", "gate_up_y0"],
    "attended": ["cotangent_slots", "down_y0", "down_z1", "down_z2", "down_z3"],
    "attended_rows": ["down_y1", "down_y3", "output_weight"],
    "projected": ["gate_up_y1", "gate_up_z2"],
    "expert_rows": ["gate_up_y2", "gate_up_z1", "gate_up_z3"],
    "hidden_units": ["gate_up_grad_y2"],
    "row_grads": ["gate_up_grad_z1", "output_slots"],
    "hidden_rows": ["gate_up_grad_y3"],
    "head_slots": ["down_grad_y1", "down_grad_y2"],
    "query_grads": ["gate_up_grad_z2", "gate_up_grad_z3", "output_rows"],
    "query_rows": ["gate_up_grad_y0"],
    "input_slots": ["down_grad_y0", "down_grad_z1", "output_grad"],
    "small": ["down_grad_y3", "down_grad_z2", "down_grad_z3"],
}
CHUNKS = 2


def slot_table(routes, fill_order, experts):
    pair_count = 2 * routes.shape[0]
    capacity = pair_count // experts
    pair_index = jnp.arange(pair_count, dtype=jnp.int32)
    pair_expert = jnp.concatenate([routes[:, 0], routes[:, 1]]).astype(F32)
    reorder = (fill_order[:, None] == pair_index[None, :]).astype(F32)
    ordered = jnp.dot(reorder, pair_expert, precision=HIGHEST)
    onehot = (ordered[:, None] == jnp.arange(experts, dtype=F32)[None, :]).astype(F32)
    below_mask = (pair_index[:, None] > pair_index[None, :]).astype(F32)
    earlier = jnp.dot(below_mask, onehot, precision=HIGHEST)
    position = jnp.sum(earlier * onehot, axis=1)
    target = ordered * capacity + position
    placing = (
        (target[:, None] == pair_index.astype(F32)[None, :]) & (position < capacity)[:, None]
    ).astype(F32)
    return lax.dot_general(placing, reorder, CONTRACT_FIRST, precision=HIGHEST).astype(BF16)


def select_rows(table, pair_rows):
    return jnp.dot(table, pair_rows, preferred_element_type=F32).astype(BF16)


def spread_rows(table, slot_rows):
    return lax.dot_general(table, slot_rows, CONTRACT_FIRST, preferred_element_type=F32).astype(BF16)


def chosen_gates(logits, routes, experts):
    expert_ids = jnp.arange(experts, dtype=jnp.int32)[None, :]
    first_logit = jnp.sum(jnp.where(routes[:, 0:1] == expert_ids, logits, 0.0), axis=1)
    second_logit = jnp.sum(jnp.where(routes[:, 1:2] == expert_ids, logits, 0.0), axis=1)
    return jax.nn.softmax(jnp.stack([first_logit, second_logit], axis=1), axis=1)


def gate_logit_grad(gate_pair, gate_grad, routes, experts):
    expert_ids = jnp.arange(experts, dtype=jnp.int32)[None, :]
    chosen_grad = gate_pair * (gate_grad - jnp.sum(gate_pair * gate_grad, axis=1, keepdims=True))
    first_part = chosen_grad[:, 0:1] * (routes[:, 0:1] == expert_ids).astype(F32)
    return first_part + chosen_grad[:, 1:2] * (routes[:, 1:2] == expert_ids).astype(F32)


def norm_back(values, scale, gain_row, normed_grad):
    scaled = normed_grad * gain_row
    return scale * (
        scaled - values * scale * scale * jnp.mean(scaled * values, axis=1, keepdims=True)
    )


def attend_forward(queries, key_heads, value_heads, allowed):
    tok_rows = key_heads.shape[0]
    scores = jnp.einsum("kqhd,shd->khqs", queries, key_heads, preferred_element_type=F32) * (
        HEAD_DIM ** (-0.5)
    )
    masked = jnp.where(allowed[None, None], scores, NEGATIVE)
    row_max = jnp.max(masked, axis=-1, keepdims=True)
    exponent = jnp.exp(masked - row_max)
    totals = jnp.sum(exponent, axis=-1, keepdims=True)
    softmax_out = (exponent / totals).astype(BF16)
    mixed = jnp.einsum("khqs,shd->kqhd", softmax_out, value_heads, preferred_element_type=F32)
    mixed = mixed.astype(BF16).reshape(2 * tok_rows, HEADS * HEAD_DIM)
    return mixed, (row_max + jnp.log(totals))[..., 0]


def attend_backward(queries, key_heads, value_heads, allowed, log_sums, mixed_grad):
    tok_rows = key_heads.shape[0]
    scale_factor = HEAD_DIM ** (-0.5)
    scores = (
        jnp.einsum("kqhd,shd->khqs", queries, key_heads, preferred_element_type=F32) * scale_factor
    )
    softmax_out = jnp.where(allowed[None, None], jnp.exp(scores - log_sums[..., None]), 0.0)
    prob_grad = jnp.einsum("kqhd,shd->khqs", mixed_grad, value_heads, preferred_element_type=F32)
    score_grad = (
        softmax_out * (prob_grad - jnp.sum(softmax_out * prob_grad, axis=-1, keepdims=True))
    ).astype(BF16)
    query_grad = (
        jnp.einsum("khqs,shd->kqhd", score_grad, key_heads, preferred_element_type=F32)
        * scale_factor
    )
    key_grad = (
        jnp.einsum("khqs,kqhd->shd", score_grad, queries, preferred_element_type=F32) * scale_factor
    )
    value_grad = jnp.einsum(
        "khqs,kqhd->shd", softmax_out.astype(BF16), mixed_grad, preferred_element_type=F32
    )
    return (
        query_grad.reshape(2 * tok_rows, D),
        key_grad.reshape(tok_rows, D),
        value_grad.reshape(tok_rows, D),
    )


def pick(choices, index):
    result = choices[0]
    for i in range(1, len(choices)):
        result = jnp.where(index == i, choices[i], result)
    return result


def split3(v):
    high = lax.reduce_precision(v, exponent_bits=8, mantissa_bits=7)
    middle = lax.reduce_precision(v - high, exponent_bits=8, mantissa_bits=7)
    return [high.astype(BF16), middle.astype(BF16), (v - high - middle).astype(BF16)]


def after(value, *others):
    return lax.optimization_barrier((value, *others))[0]


def per_device(
    tokens,
    cotangent,
    segments,
    att_routes,
    mlp_routes,
    slot_order,
    norm_gains,
    kv_weight,
    router_weight,
    query_weight,
    output_weight,
    gate_up_weight,
    down_weight,
):
    tok_rows = tokens.shape[0]
    experts = lax.axis_size("expert") * query_weight.shape[0]
    ycount = lax.axis_size("y")
    capacity = 2 * tok_rows // experts
    part = norm_gains.shape[0]
    half = D // ycount
    kv_cols = 2 * D // experts
    slice_ff = FF // Z
    pieces = tok_rows // capacity
    y_index = lax.axis_index("y")
    z_index = lax.axis_index("z")
    e_index = lax.axis_index("expert")

    def y_major(v):
        return jnp.concatenate(
            [
                v[:, (z * ycount + y) * part : (z * ycount + y + 1) * part]
                for y in range(ycount)
                for z in range(Z)
            ],
            axis=1,
        )

    def natural(v):
        return jnp.concatenate(
            [
                v[:, (y * Z + z) * part : (y * Z + z + 1) * part]
                for z in range(Z)
                for y in range(ycount)
            ],
            axis=1,
        )

    def halves(v):
        return [v[..., y * half : (y + 1) * half] for y in range(ycount)]

    def own_first(v):
        h = halves(v)
        return jnp.concatenate(
            [pick([h[(i + k) % ycount] for i in range(ycount)], y_index) for k in range(ycount)],
            axis=-1,
        )

    def own_first_back(v):
        h = halves(v)
        return jnp.concatenate(
            [pick([h[(j - i) % ycount] for i in range(ycount)], y_index) for j in range(ycount)],
            axis=-1,
        )

    def exchange(v, axes):
        return lax.all_to_all(v, axes, split_axis=0, concat_axis=0, tiled=True)

    def pack(v):
        return jnp.concatenate(
            [v[..., i * capacity : (i + 1) * capacity, :] for i in range(pieces)], axis=-1
        )

    def unpack(v):
        return jnp.concatenate(
            [v[..., i * kv_cols : (i + 1) * kv_cols] for i in range(pieces)], axis=-2
        )

    both = ("expert", "y")
    js = range(1, ycount)

    shards = Z * ycount
    small = jnp.concatenate([norm_gains, router_weight], axis=1)
    small = jnp.pad(small, ((0, 0), (0, -small.shape[1] % 16))).T
    small = exchange(jnp.broadcast_to(small[None], (shards, *small.shape)), ("y", "z"))
    small = jnp.concatenate([small[i] for i in range(shards)], axis=1)
    kv_part = lax.dynamic_slice_in_dim(kv_weight, e_index * kv_cols, kv_cols, 1)
    wide_both = lax.all_gather(
        jnp.concatenate([query_weight[0], kv_part], axis=1), "z", axis=0, tiled=True
    )
    wide_query, wide_kv = wide_both[:, :D], wide_both[:, D:]
    wide_output = lax.all_gather(output_weight[0], "z", axis=0, tiled=True)

    def z_shift(v, k, name):
        with jax.named_scope(f"{name}_z{k}"):
            return lax.ppermute(v, "z", [(i, (i + k) % Z) for i in range(Z)])

    def y_shift(v, k, name):
        with jax.named_scope(name):
            return lax.ppermute(v, "y", [(i, (i + k) % ycount) for i in range(ycount)])

    gu_weight, dn_weight = gate_up_weight[0], down_weight[0]
    gate_weight, up_weight = gu_weight[:, :FF], gu_weight[:, FF:]
    moved = {}
    makers = {}

    def columns(weight, k):
        return lax.dynamic_slice_in_dim(weight, ((z_index + k) % Z) * slice_ff, slice_ff, 1)

    def weight_columns(part_name, k):
        if part_name == "down":
            return columns(dn_weight, k)
        return jnp.concatenate([columns(gate_weight, k), columns(up_weight, k)], axis=1)

    def fetch(name):
        if name not in moved:
            moved[name] = makers[name]()
        return moved[name]

    def step(name, value):
        value = lax.optimization_barrier(
            (value, [fetch(n) for n in WAIT.get(name, ()) if n in makers])
        )[0]
        for n in FROM.get(name, ()):
            if n not in moved:
                moved[n] = makers[n](value)
        return value

    def weight_makers(part_name):
        for k in range(Z):

            def over_z(*others, k=k):
                own = after(weight_columns(part_name, k), *others)
                return z_shift(own, k, part_name) if k else own

            def over_y(*others, k=k):
                own = after(fetch(f"{part_name}_z{k}"), *others)
                return [y_shift(own, ycount - j, f"{part_name}_y{k}") for j in js]

            makers[f"{part_name}_z{k}"] = over_z
            makers[f"{part_name}_y{k}"] = over_y

    def assemble(part_name):
        rows = [[fetch(f"{part_name}_z{k}") for k in range(Z)]]
        rows += [[fetch(f"{part_name}_y{k}")[j - 1] for k in range(Z)] for j in js]
        wide = jnp.zeros((D, rows[0][0].shape[1]), BF16)
        for j in range(ycount):
            for k in range(Z):
                row = j * half + ((z_index - k) % Z) * part
                wide = lax.dynamic_update_slice_in_dim(wide, rows[j][k], row, 0)
        return wide

    weight_makers("down")
    weight_makers("gate_up")
    step("start", ())

    segment_row = segments[0]
    fill_order = slot_order[0]
    positions = jnp.arange(tok_rows)
    allowed = (positions[:, None] >= positions[None, :]) & (
        segment_row[:, None] == segment_row[None, :]
    )
    table_att = slot_table(att_routes, fill_order, experts)
    table_mlp = slot_table(mlp_routes, fill_order, experts)
    token_att = table_att[:, :tok_rows] + table_att[:, tok_rows:]
    token_mlp = table_mlp[:, :tok_rows] + table_mlp[:, tok_rows:]

    gain_one = small[0:1].astype(F32)
    gain_two = small[1:2].astype(F32)
    router_att = small[2 : 2 + experts]
    router_mlp = small[2 + experts : 2 + 2 * experts]
    inputs = y_major(tokens).astype(F32)
    grad_out = y_major(cotangent).astype(F32)
    scale_one = lax.rsqrt(jnp.mean(inputs * inputs, axis=1, keepdims=True) + EPSILON)
    normed_one = (inputs * scale_one * gain_one).astype(BF16)

    def to_experts(rows):
        slots = jnp.einsum("zts,ztd->zsd", tables, rows, preferred_element_type=F32).astype(BF16)
        return slots.reshape(Z, experts, capacity, D).transpose(1, 0, 2, 3)

    def to_tokens(rows):
        rows = rows.transpose(1, 0, 2, 3).reshape(Z, 2 * tok_rows, D)
        return jnp.einsum("zts,zsd->ztd", tables, rows, preferred_element_type=F32).astype(BF16)

    grads_z = lax.all_gather(
        jnp.concatenate([own_first(y_major(cotangent)), token_mlp.T], axis=1), "z", axis=0
    )
    tables = grads_z[:, :, D:]
    sub = capacity // CHUNKS
    grad_slots = exchange(to_experts(grads_z[:, :, :D]), "expert")
    grad_rows = jnp.concatenate(
        [grad_slots[:, :, c * sub : (c + 1) * sub].reshape(-1, D) for c in range(CHUNKS)], axis=0
    )
    att_slots_in = select_rows(token_att, normed_one).reshape(experts, capacity, D)
    send = jnp.stack(
        [
            jnp.concatenate([s, jnp.broadcast_to(n[None], (experts, tok_rows, half))], axis=1)
            for s, n in zip(halves(att_slots_in), halves(normed_one))
        ],
        axis=1,
    )
    got = exchange(send.reshape(experts * ycount, capacity + tok_rows, half), both)
    query_in = got[:, :capacity].reshape(experts * ycount * capacity, half)
    kv_in = got[:, capacity:].reshape(experts * ycount * tok_rows, half)
    query_in, kv_in = step("projections", (query_in, kv_in))
    query_part = jnp.dot(query_in, wide_query, preferred_element_type=F32).astype(BF16)
    kv_out = jnp.dot(kv_in, wide_kv, preferred_element_type=F32).astype(BF16)
    back = jnp.concatenate(
        [
            query_part.reshape(experts * ycount, capacity, D),
            pack(kv_out.reshape(experts * ycount, tok_rows, kv_cols)),
        ],
        axis=1,
    )
    back = exchange(back, both).reshape(experts, ycount, 2 * capacity, D)
    makers["cotangent_rows"] = lambda: grads_z
    makers["cotangent_slots"] = lambda: grad_rows
    makers["output_weight"] = lambda: wide_output
    back = step("queries", back)
    summed = jnp.sum(back.astype(F32), axis=1).astype(BF16)
    query_slots = summed[:, :capacity].reshape(2 * tok_rows, D)
    kv_parts = unpack(summed[:, capacity:])
    keyvals = jnp.concatenate([kv_parts[e] for e in range(experts)], axis=-1)
    key_heads = keyvals[:, :D].reshape(tok_rows, HEADS, HEAD_DIM)
    value_heads = keyvals[:, D:].reshape(tok_rows, HEADS, HEAD_DIM)
    router_logits = lax.dot_general(
        normed_one, router_att, CONTRACT_LAST, preferred_element_type=F32
    )
    gate_att = chosen_gates(router_logits, att_routes, experts)
    query_pairs = spread_rows(table_att, query_slots)
    queries = query_pairs.reshape(2, tok_rows, HEADS, HEAD_DIM)
    mixed_heads, log_sums = attend_forward(queries, key_heads, value_heads, allowed)

    def to_rows(v):
        v = v.reshape(experts, 1, capacity, D)
        v = jnp.broadcast_to(v, (experts, ycount, capacity, D))
        return exchange(v.reshape(experts * ycount, capacity, D), both)

    def from_halves(v):
        v = exchange(v.reshape(experts * ycount, capacity, half), both)
        v = v.reshape(experts, ycount, capacity, half)
        return jnp.concatenate([v[:, y] for y in range(ycount)], axis=-1).reshape(2 * tok_rows, D)

    mixed_slots = step("attended", select_rows(table_att, mixed_heads))
    mixed_in = step("attended_rows", to_rows(mixed_slots).reshape(-1, D))
    projected = lax.dot_general(
        mixed_in, wide_output, CONTRACT_LAST, preferred_element_type=F32
    ).astype(BF16)
    att_slots = step("projected", from_halves(projected))
    att_pairs = spread_rows(table_att, att_slots).astype(F32).reshape(2, tok_rows, D)
    hidden = inputs + gate_att[:, 0:1] * att_pairs[0] + gate_att[:, 1:2] * att_pairs[1]
    scale_two = lax.rsqrt(jnp.mean(hidden * hidden, axis=1, keepdims=True) + EPSILON)
    normed_two = (hidden * scale_two * gain_two).astype(BF16)
    mlp_logits = lax.dot_general(
        normed_two, router_mlp, CONTRACT_LAST, preferred_element_type=F32
    )
    gate_mlp = chosen_gates(mlp_logits, mlp_routes, experts)

    slot_gates = jnp.sum(
        table_mlp.astype(F32) * jnp.concatenate([gate_mlp[:, 0], gate_mlp[:, 1]])[None], axis=1
    )
    gate_cols = jnp.pad(
        jnp.concatenate(split3(slot_gates.reshape(2, tok_rows).T), axis=1), ((0, 0), (0, 122))
    )
    rows_z = lax.all_gather(
        jnp.concatenate([own_first(normed_two), gate_cols], axis=1), "z", axis=0
    )
    rows_z = step("gathered_rows", rows_z)
    gates_z = rows_z[:, :, D:]
    gates_z = jnp.concatenate([gates_z[:, :, 0:6:2], gates_z[:, :, 1:6:2]], axis=1)
    gates_z = jnp.pad(gates_z, ((0, 0), (0, 0), (0, 125)))
    gates_z = gates_z.reshape(Z, experts, capacity, 128).transpose(1, 0, 2, 3)
    send = jnp.concatenate([to_experts(rows_z[:, :, :D]), gates_z], axis=-1)
    got = [
        exchange(send[:, :, c * sub : (c + 1) * sub], "expert").reshape(-1, D + 128)
        for c in range(CHUNKS)
    ]
    got[0] = step("expert_rows", got[0])
    wide_down, wide_gate_up = assemble("down"), assemble("gate_up")
    free_grad = jnp.dot(grad_rows, wide_down, preferred_element_type=F32)
    got[0] = after(got[0], free_grad)
    chunk_rows = grad_rows.shape[0] // CHUNKS

    def hidden_units(c):
        rows = got[c][:, :D]
        gates = jnp.sum(got[c][:, D : D + 3].astype(F32), axis=1, keepdims=True)
        free = free_grad[c * chunk_rows : (c + 1) * chunk_rows]
        gate_up = jnp.dot(rows, wide_gate_up, preferred_element_type=F32)
        gate_part = gate_up[:, :slice_ff]
        up_part = gate_up[:, slice_ff:]
        sigma = jax.nn.sigmoid(gate_part)
        activated = (gate_part * sigma * up_part).astype(BF16)
        act_grad = free * gates
        gate_grad = act_grad * up_part * sigma * (1.0 + gate_part * (1.0 - sigma))
        up_grad = act_grad * gate_part * sigma
        gate_up_grad = jnp.concatenate([gate_grad, up_grad], axis=-1).astype(BF16)
        row_part = lax.dot_general(
            gate_up_grad, wide_gate_up, CONTRACT_LAST, preferred_element_type=F32
        ).astype(BF16)
        sums = jnp.sum(activated.astype(F32) * free, axis=1, keepdims=True)
        sums = jnp.pad(jnp.concatenate(split3(sums), axis=1), ((0, 0), (0, 125)))
        row_part = jnp.concatenate([row_part, sums], axis=1)
        return rows, gates, activated, gate_up_grad, row_part

    units = [hidden_units(c) for c in range(CHUNKS)]
    ffn_rows, row_gates, activated, gate_up_grad = (
        jnp.concatenate(v, axis=0) for v in list(zip(*units))[:4]
    )

    def outer(left_rows, right_rows):
        return lax.dot_general(left_rows, right_rows, CONTRACT_FIRST, preferred_element_type=F32)

    def block(v, k):
        return lax.dynamic_index_in_dim(v, (z_index + k) % Z, 0, keepdims=False)

    def peers(left, right):
        return [
            outer(left[:, j * half : (j + 1) * half], right)
            .astype(BF16)
            .reshape(Z, part, right.shape[1])
            for j in js
        ]

    def add_up(own, moved):
        total = own
        for m in moved:
            total = total + m.astype(F32)
        return total

    def grad_makers(part_name, left, right):
        others = peers(left, right)
        own = outer(left[:, :half], right).reshape(Z, part, right.shape[1])
        for k in range(Z):

            def over_y(*steps, k=k):
                return [
                    y_shift(after(block(other, k), *steps), j, f"{part_name}_y{k}")
                    for j, other in zip(js, others)
                ]

            def over_z(*steps, k=k):
                total = add_up(block(own, k), fetch(f"{part_name}_y{k}"))
                return z_shift(after(total.astype(BF16), *steps), k, part_name) if k else total

            makers[f"{part_name}_y{k}"] = over_y
            makers[f"{part_name}_z{k}"] = over_z
        makers[f"{part_name}_peers"] = lambda: others
        makers[f"{part_name}_own"] = lambda: own

    def in_order(got):
        return [
            pick([got[(z - i) % Z].astype(F32) for z in range(Z)], z_index) for i in range(Z)
        ]

    gated_rows = (row_gates * grad_rows.astype(F32)).astype(BF16)
    grad_makers("gate_up_grad", ffn_rows, gate_up_grad)
    grad_makers("down_grad", gated_rows, activated)
    last_part = step("hidden_units", units[-1][4])
    back = jnp.concatenate(
        [
            exchange(v.reshape(experts, Z, sub, D + 128), "expert")
            for v in [u[4] for u in units[:-1]] + [last_part]
        ],
        axis=2,
    )
    back = step("row_slots", back)
    sums = back[..., D : D + 3].transpose(1, 0, 2, 3).reshape(Z, 2 * tok_rows, 3)
    sums = jnp.concatenate([sums[:, :tok_rows], sums[:, tok_rows:]], axis=-1)
    sums = jnp.concatenate(
        [jnp.where(z_index == z, sums, jnp.zeros_like(sums)) for z in range(Z)], axis=-1
    )
    sums = jnp.pad(sums, ((0, 0), (0, 0), (0, 128 - 6 * Z)))
    row_back = back
    back = lax.psum_scatter(
        jnp.concatenate([to_tokens(back[..., :D]), sums], axis=-1).reshape(-1, D + 128),
        "z",
        scatter_dimension=0,
        tiled=True,
    )
    ffn_row_grads = own_first_back(back[:, :D]).astype(F32)
    sums = back[:, D : D + 6 * Z].astype(F32).reshape(tok_rows, Z, 2, 3)
    sums = jnp.sum(sums, axis=(1, 3)).T.reshape(2 * tok_rows, 1)
    gate_mlp_grad = jnp.sum(table_mlp.astype(F32) * sums, axis=0).reshape(2, tok_rows).T

    def output_slots(*others):
        out_part = (
            row_gates
            * lax.dot_general(
                after(activated, row_back, *others),
                wide_down,
                CONTRACT_LAST,
                preferred_element_type=F32,
            )
        ).astype(BF16)
        out_part = out_part.reshape(CHUNKS, experts, Z, sub, D).transpose(1, 2, 0, 3, 4)
        return to_tokens(exchange(out_part.reshape(experts, Z, capacity, D), "expert"))

    makers["output_slots"] = output_slots
    makers["output_rows"] = lambda: lax.psum_scatter(
        fetch("output_slots").reshape(-1, D), "z", scatter_dimension=0, tiled=True
    )
    ffn_row_grads = step("row_grads", ffn_row_grads)
    logit_mlp_grad = gate_logit_grad(gate_mlp, gate_mlp_grad, mlp_routes, experts)
    normed_two_grad = (
        ffn_row_grads
        + jnp.dot(logit_mlp_grad, router_mlp.astype(F32), precision=HIGHEST)
    )
    hidden_grad = grad_out + norm_back(hidden, scale_two, gain_two, normed_two_grad)
    gate_att_grad = jnp.sum(hidden_grad[None] * att_pairs, axis=2).T
    logit_att_grad = gate_logit_grad(gate_att, gate_att_grad, att_routes, experts)
    gated_hidden = jnp.concatenate(
        [gate_att[:, 0:1] * hidden_grad, gate_att[:, 1:2] * hidden_grad], axis=0
    ).astype(BF16)
    hidden_send = select_rows(table_att, gated_hidden).reshape(experts, capacity, D)
    hidden_in = exchange(
        jnp.stack(halves(hidden_send), axis=1).reshape(experts * ycount, capacity, half), both
    ).reshape(-1, half)
    hidden_in = step("hidden_rows", hidden_in)
    head_part = jnp.dot(hidden_in, wide_output, preferred_element_type=F32).astype(BF16)
    head_part = exchange(head_part.reshape(experts * ycount, capacity, D), both)
    head_part = step("head_slots", head_part)
    head_slots = jnp.sum(
        head_part.reshape(experts, ycount, capacity, D).astype(F32), axis=1
    ).astype(BF16)
    mixed_grad = spread_rows(table_att, head_slots.reshape(2 * tok_rows, D)).reshape(
        2, tok_rows, HEADS, HEAD_DIM
    )
    makers["output_grad"] = lambda *others: lax.psum_scatter(
        outer(after(hidden_in, *others), mixed_in).astype(BF16),
        "z",
        scatter_dimension=0,
        tiled=True,
    )
    query_grad, key_grad, value_grad = attend_backward(
        queries, key_heads, value_heads, allowed, log_sums, mixed_grad
    )
    query_grad = step("query_grads", query_grad)
    keyval_row_grad = jnp.concatenate([key_grad, value_grad], axis=1).astype(BF16)
    query_send = select_rows(table_att, query_grad.astype(BF16)).reshape(experts, capacity, D)
    kv_send = pack(
        jnp.stack([keyval_row_grad[:, e * kv_cols : (e + 1) * kv_cols] for e in range(experts)])
    )
    send = jnp.concatenate([query_send, kv_send], axis=1).reshape(experts, 1, 2 * capacity, D)
    send = jnp.broadcast_to(send, (experts, ycount, 2 * capacity, D))
    got = exchange(send.reshape(experts * ycount, 2 * capacity, D), both)
    got = step("query_rows", got)
    block_out = (hidden + own_first_back(after(fetch("output_rows"), got)).astype(F32)).astype(BF16)
    query_rows = got[:, :capacity].reshape(-1, D)
    kv_rows = unpack(got[:, capacity:]).reshape(-1, kv_cols)
    input_part = lax.dot_general(
        query_rows, wide_query, CONTRACT_LAST, preferred_element_type=F32
    ).astype(BF16)
    normed_part = lax.dot_general(
        kv_rows, wide_kv, CONTRACT_LAST, preferred_element_type=F32
    ).astype(BF16)
    back = jnp.concatenate(
        [
            input_part.reshape(experts * ycount, capacity, half),
            normed_part.reshape(experts * ycount, tok_rows, half),
        ],
        axis=1,
    )
    query_outer = outer(query_in, query_rows).astype(BF16)
    kv_outer = outer(kv_in, kv_rows).astype(BF16)
    back = after(back, query_outer, kv_outer)
    back = exchange(back, both).reshape(experts, ycount, capacity + tok_rows, half)
    back = step("input_slots", back)
    gu_grads = in_order([fetch(f"gate_up_grad_z{k}") for k in range(Z)])
    down_grads = in_order([fetch(f"down_grad_z{k}") for k in range(Z)])
    gate_up_weight_grad = jnp.concatenate(
        [g[:, :slice_ff] for g in gu_grads] + [g[:, slice_ff:] for g in gu_grads], axis=1
    )[None]
    down_weight_grad = jnp.concatenate(down_grads, axis=1)[None]
    output_grad = fetch("output_grad").astype(F32)[None]
    back = jnp.concatenate([back[:, y] for y in range(ycount)], axis=-1)
    input_pairs = (
        spread_rows(table_att, back[:, :capacity].reshape(2 * tok_rows, D))
        .astype(F32)
        .reshape(2, tok_rows, D)
    )
    kv_grad_part = lax.psum_scatter(kv_outer, "z", scatter_dimension=0, tiled=True)
    query_weight_grad = lax.psum_scatter(
        query_outer, "z", scatter_dimension=0, tiled=True
    ).astype(F32)[None]
    kv_grads = exchange(
        jnp.broadcast_to(kv_grad_part[None], (experts, *kv_grad_part.shape)), "expert"
    )
    keyval_grad = jnp.concatenate([kv_grads[e] for e in range(experts)], axis=1).astype(F32)
    normed_one_grad = (
        input_pairs[0] + input_pairs[1] + jnp.sum(back[:, capacity:].astype(F32), axis=0)
    )
    normed_one_grad = normed_one_grad + jnp.dot(
        logit_att_grad, router_att.astype(F32), precision=HIGHEST
    )
    input_grad = natural(
        hidden_grad + norm_back(inputs, scale_one, gain_one, normed_one_grad)
    )

    small_grads = jnp.concatenate(
        [
            jnp.sum(normed_one_grad * inputs * scale_one, axis=0)[None],
            jnp.sum(normed_two_grad * hidden * scale_two, axis=0)[None],
            lax.dot_general(
                logit_att_grad, normed_one.astype(F32), CONTRACT_FIRST, precision=HIGHEST
            ),
            lax.dot_general(
                logit_mlp_grad, normed_two.astype(F32), CONTRACT_FIRST, precision=HIGHEST
            ),
        ],
        axis=0,
    )
    rows = small_grads.shape[0]
    small_grads = jnp.stack(
        [small_grads[:, i * part : (i + 1) * part] for i in range(Z * ycount)]
    )
    small_grads = step("small", exchange(small_grads, ("y", "z")))
    small_grads = jnp.sum(small_grads, axis=0)
    small_grads = exchange(
        jnp.broadcast_to(small_grads[None], (experts, rows, part)), "expert"
    )
    small_grads = jnp.sum(small_grads, axis=0).T
    gains_grad = small_grads[:, :2]
    router_grad = small_grads[:, 2:rows]
    return (
        natural(block_out),
        input_grad,
        gains_grad,
        keyval_grad,
        router_grad,
        query_weight_grad,
        output_grad,
        gate_up_weight_grad,
        down_weight_grad,
    )


def solution(mesh):
    experts, shards = mesh.shape["expert"], mesh.shape["shard"]
    grid = Mesh(mesh.devices.reshape(experts, Z, shards // Z), ("expert", "z", "y"))
    rows = P(("expert", "z", "y"), None)
    shared = P(("z", "y"), None)
    owned = P("expert", ("z", "y"), None)
    in_specs = (rows,) * 6 + (shared,) * 3 + (owned,) * 4
    out_specs = (rows,) * 2 + (shared,) * 3 + (owned,) * 4
    return jax.shard_map(
        per_device, mesh=grid, in_specs=in_specs, out_specs=out_specs, check_vma=False
    )
```

```python
import jax
import jax.numpy as jnp
from jax import lax
from jax.sharding import Mesh
from jax.sharding import PartitionSpec as P

D = 2048
HEADS = 16
HEAD_DIM = 128
FF = 5632
Z = 4

EPSILON = 1e-05
NEGATIVE = -1e30
HIGHEST = lax.Precision.HIGHEST
CONTRACT_FIRST = (((0,), (0,)), ((), ()))
CONTRACT_LAST = (((1,), (1,)), ((), ()))
BF16 = jnp.bfloat16
F32 = jnp.float32

FROM = {
    "projections": ["down_z1", "gate_up_y0", "gate_up_z2"],
    "queries": ["gate_up_y2"],
    "attended": ["down_y1"],
    "row_slots": ["down_grad_y1"],
    "row_grads": ["down_grad_y3"],
    "query_grads": ["down_grad_y0", "down_grad_z2", "down_grad_z3", "gate_up_grad_y0"],
    "query_rows": ["down_grad_z1"],
}
WAIT = {
    "projections": ["down_y2"],
    "queries": ["cotangent_rows"],
    "attended": ["cotangent_slots", "down_z1", "down_z2", "down_z3", "gate_up_y0"],
    "attended_rows": ["down_y0", "down_y1", "down_y3", "output_weight"],
    "projected": ["gate_up_y1", "gate_up_z2"],
    "expert_rows": ["gate_up_y2", "gate_up_z1", "gate_up_z3"],
    "hidden_units": ["gate_up_grad_y2"],
    "row_grads": ["output_slots"],
    "hidden_rows": ["gate_up_grad_y3", "gate_up_grad_z1"],
    "head_slots": ["down_grad_y2"],
    "query_grads": ["down_grad_y0", "down_grad_y1", "gate_up_grad_z2", "output_rows"],
    "query_rows": ["gate_up_grad_y0"],
    "input_slots": ["down_grad_z1", "down_grad_z3", "gate_up_grad_z3", "output_grad"],
    "small": ["down_grad_z2"],
}
CHUNKS = 2


def slot_table(routes, fill_order, experts):
    pair_count = 2 * routes.shape[0]
    capacity = pair_count // experts
    pair_index = jnp.arange(pair_count, dtype=jnp.int32)
    pair_expert = jnp.concatenate([routes[:, 0], routes[:, 1]]).astype(F32)
    reorder = (fill_order[:, None] == pair_index[None, :]).astype(F32)
    ordered = jnp.dot(reorder, pair_expert, precision=HIGHEST)
    onehot = (ordered[:, None] == jnp.arange(experts, dtype=F32)[None, :]).astype(F32)
    below_mask = (pair_index[:, None] > pair_index[None, :]).astype(F32)
    earlier = jnp.dot(below_mask, onehot, precision=HIGHEST)
    position = jnp.sum(earlier * onehot, axis=1)
    target = ordered * capacity + position
    placing = (
        (target[:, None] == pair_index.astype(F32)[None, :]) & (position < capacity)[:, None]
    ).astype(F32)
    return lax.dot_general(placing, reorder, CONTRACT_FIRST, precision=HIGHEST).astype(BF16)


def select_rows(table, pair_rows):
    return jnp.dot(table, pair_rows, preferred_element_type=F32).astype(BF16)


def spread_rows(table, slot_rows):
    return lax.dot_general(table, slot_rows, CONTRACT_FIRST, preferred_element_type=F32).astype(BF16)


def chosen_gates(logits, routes, experts):
    expert_ids = jnp.arange(experts, dtype=jnp.int32)[None, :]
    first_logit = jnp.sum(jnp.where(routes[:, 0:1] == expert_ids, logits, 0.0), axis=1)
    second_logit = jnp.sum(jnp.where(routes[:, 1:2] == expert_ids, logits, 0.0), axis=1)
    return jax.nn.softmax(jnp.stack([first_logit, second_logit], axis=1), axis=1)


def gate_logit_grad(gate_pair, gate_grad, routes, experts):
    expert_ids = jnp.arange(experts, dtype=jnp.int32)[None, :]
    chosen_grad = gate_pair * (gate_grad - jnp.sum(gate_pair * gate_grad, axis=1, keepdims=True))
    first_part = chosen_grad[:, 0:1] * (routes[:, 0:1] == expert_ids).astype(F32)
    return first_part + chosen_grad[:, 1:2] * (routes[:, 1:2] == expert_ids).astype(F32)


def norm_back(values, scale, gain_row, normed_grad):
    scaled = normed_grad * gain_row
    return scale * (
        scaled - values * scale * scale * jnp.mean(scaled * values, axis=1, keepdims=True)
    )


def attend_forward(queries, key_heads, value_heads, allowed):
    tok_rows = key_heads.shape[0]
    scores = jnp.einsum("kqhd,shd->khqs", queries, key_heads, preferred_element_type=F32) * (
        HEAD_DIM ** (-0.5)
    )
    masked = jnp.where(allowed[None, None], scores, NEGATIVE)
    row_max = jnp.max(masked, axis=-1, keepdims=True)
    exponent = jnp.exp(masked - row_max)
    totals = jnp.sum(exponent, axis=-1, keepdims=True)
    softmax_out = (exponent / totals).astype(BF16)
    mixed = jnp.einsum("khqs,shd->kqhd", softmax_out, value_heads, preferred_element_type=F32)
    mixed = mixed.astype(BF16).reshape(2 * tok_rows, HEADS * HEAD_DIM)
    return mixed, (row_max + jnp.log(totals))[..., 0]


def attend_backward(queries, key_heads, value_heads, allowed, log_sums, mixed_grad):
    tok_rows = key_heads.shape[0]
    scale_factor = HEAD_DIM ** (-0.5)
    scores = (
        jnp.einsum("kqhd,shd->khqs", queries, key_heads, preferred_element_type=F32) * scale_factor
    )
    softmax_out = jnp.where(allowed[None, None], jnp.exp(scores - log_sums[..., None]), 0.0)
    prob_grad = jnp.einsum("kqhd,shd->khqs", mixed_grad, value_heads, preferred_element_type=F32)
    score_grad = (
        softmax_out * (prob_grad - jnp.sum(softmax_out * prob_grad, axis=-1, keepdims=True))
    ).astype(BF16)
    query_grad = (
        jnp.einsum("khqs,shd->kqhd", score_grad, key_heads, preferred_element_type=F32)
        * scale_factor
    )
    key_grad = (
        jnp.einsum("khqs,kqhd->shd", score_grad, queries, preferred_element_type=F32) * scale_factor
    )
    value_grad = jnp.einsum(
        "khqs,kqhd->shd", softmax_out.astype(BF16), mixed_grad, preferred_element_type=F32
    )
    return (
        query_grad.reshape(2 * tok_rows, D),
        key_grad.reshape(tok_rows, D),
        value_grad.reshape(tok_rows, D),
    )


def pick(choices, index):
    result = choices[0]
    for i in range(1, len(choices)):
        result = jnp.where(index == i, choices[i], result)
    return result


def split3(v):
    high = lax.reduce_precision(v, exponent_bits=8, mantissa_bits=7)
    middle = lax.reduce_precision(v - high, exponent_bits=8, mantissa_bits=7)
    return [high.astype(BF16), middle.astype(BF16), (v - high - middle).astype(BF16)]


def after(value, *others):
    return lax.optimization_barrier((value, *others))[0]


def per_device(
    tokens,
    cotangent,
    segments,
    att_routes,
    mlp_routes,
    slot_order,
    norm_gains,
    kv_weight,
    router_weight,
    query_weight,
    output_weight,
    gate_up_weight,
    down_weight,
):
    tok_rows = tokens.shape[0]
    experts = lax.axis_size("expert") * query_weight.shape[0]
    ycount = lax.axis_size("y")
    capacity = 2 * tok_rows // experts
    part = norm_gains.shape[0]
    half = D // ycount
    kv_cols = 2 * D // experts
    slice_ff = FF // Z
    pieces = tok_rows // capacity
    y_index = lax.axis_index("y")
    z_index = lax.axis_index("z")
    e_index = lax.axis_index("expert")

    def y_major(v):
        return jnp.concatenate(
            [
                v[:, (z * ycount + y) * part : (z * ycount + y + 1) * part]
                for y in range(ycount)
                for z in range(Z)
            ],
            axis=1,
        )

    def natural(v):
        return jnp.concatenate(
            [
                v[:, (y * Z + z) * part : (y * Z + z + 1) * part]
                for z in range(Z)
                for y in range(ycount)
            ],
            axis=1,
        )

    def halves(v):
        return [v[..., y * half : (y + 1) * half] for y in range(ycount)]

    def own_first(v):
        h = halves(v)
        return jnp.concatenate(
            [pick([h[(i + k) % ycount] for i in range(ycount)], y_index) for k in range(ycount)],
            axis=-1,
        )

    def own_first_back(v):
        h = halves(v)
        return jnp.concatenate(
            [pick([h[(j - i) % ycount] for i in range(ycount)], y_index) for j in range(ycount)],
            axis=-1,
        )

    def exchange(v, axes):
        return lax.all_to_all(v, axes, split_axis=0, concat_axis=0, tiled=True)

    def pack(v):
        return jnp.concatenate(
            [v[..., i * capacity : (i + 1) * capacity, :] for i in range(pieces)], axis=-1
        )

    def unpack(v):
        return jnp.concatenate(
            [v[..., i * kv_cols : (i + 1) * kv_cols] for i in range(pieces)], axis=-2
        )

    both = ("expert", "y")
    js = range(1, ycount)

    shards = Z * ycount
    small = jnp.concatenate([norm_gains, router_weight], axis=1)
    small = jnp.pad(small, ((0, 0), (0, -small.shape[1] % 16))).T
    small = exchange(jnp.broadcast_to(small[None], (shards, *small.shape)), ("y", "z"))
    small = jnp.concatenate([small[i] for i in range(shards)], axis=1)
    kv_part = lax.dynamic_slice_in_dim(kv_weight, e_index * kv_cols, kv_cols, 1)
    wide_both = lax.all_gather(
        jnp.concatenate([query_weight[0], kv_part], axis=1), "z", axis=0, tiled=True
    )
    wide_query, wide_kv = wide_both[:, :D], wide_both[:, D:]
    wide_output = lax.all_gather(output_weight[0], "z", axis=0, tiled=True)

    def z_shift(v, k, name):
        with jax.named_scope(f"{name}_z{k}"):
            return lax.ppermute(v, "z", [(i, (i + k) % Z) for i in range(Z)])

    def y_shift(v, k, name):
        with jax.named_scope(name):
            return lax.ppermute(v, "y", [(i, (i + k) % ycount) for i in range(ycount)])

    gu_weight, dn_weight = gate_up_weight[0], down_weight[0]
    gate_weight, up_weight = gu_weight[:, :FF], gu_weight[:, FF:]
    moved = {}
    makers = {}

    def columns(weight, k):
        return lax.dynamic_slice_in_dim(weight, ((z_index + k) % Z) * slice_ff, slice_ff, 1)

    def weight_columns(part_name, k):
        if part_name == "down":
            return columns(dn_weight, k)
        return jnp.concatenate([columns(gate_weight, k), columns(up_weight, k)], axis=1)

    def fetch(name):
        if name not in moved:
            moved[name] = makers[name]()
        return moved[name]

    def step(name, value):
        value = lax.optimization_barrier(
            (value, [fetch(n) for n in WAIT.get(name, ()) if n in makers])
        )[0]
        for n in FROM.get(name, ()):
            if n not in moved:
                moved[n] = makers[n](value)
        return value

    def weight_makers(part_name):
        for k in range(Z):

            def over_z(*others, k=k):
                own = after(weight_columns(part_name, k), *others)
                return z_shift(own, k, part_name) if k else own

            def over_y(*others, k=k):
                own = after(fetch(f"{part_name}_z{k}"), *others)
                return [y_shift(own, ycount - j, f"{part_name}_y{k}") for j in js]

            makers[f"{part_name}_z{k}"] = over_z
            makers[f"{part_name}_y{k}"] = over_y

    def assemble(part_name):
        rows = [[fetch(f"{part_name}_z{k}") for k in range(Z)]]
        rows += [[fetch(f"{part_name}_y{k}")[j - 1] for k in range(Z)] for j in js]
        wide = jnp.zeros((D, rows[0][0].shape[1]), BF16)
        for j in range(ycount):
            for k in range(Z):
                row = j * half + ((z_index - k) % Z) * part
                wide = lax.dynamic_update_slice_in_dim(wide, rows[j][k], row, 0)
        return wide

    weight_makers("down")
    weight_makers("gate_up")
    step("start", ())

    segment_row = segments[0]
    fill_order = slot_order[0]
    positions = jnp.arange(tok_rows)
    allowed = (positions[:, None] >= positions[None, :]) & (
        segment_row[:, None] == segment_row[None, :]
    )
    table_att = slot_table(att_routes, fill_order, experts)
    table_mlp = slot_table(mlp_routes, fill_order, experts)
    token_att = table_att[:, :tok_rows] + table_att[:, tok_rows:]
    token_mlp = table_mlp[:, :tok_rows] + table_mlp[:, tok_rows:]

    gain_one = small[0:1].astype(F32)
    gain_two = small[1:2].astype(F32)
    router_att = small[2 : 2 + experts]
    router_mlp = small[2 + experts : 2 + 2 * experts]
    inputs = y_major(tokens).astype(F32)
    grad_out = y_major(cotangent).astype(F32)
    scale_one = lax.rsqrt(jnp.mean(inputs * inputs, axis=1, keepdims=True) + EPSILON)
    normed_one = (inputs * scale_one * gain_one).astype(BF16)

    def to_experts(rows):
        slots = jnp.einsum("zts,ztd->zsd", tables, rows, preferred_element_type=F32).astype(BF16)
        return slots.reshape(Z, experts, capacity, D).transpose(1, 0, 2, 3)

    def to_tokens(rows):
        rows = rows.transpose(1, 0, 2, 3).reshape(Z, 2 * tok_rows, D)
        return jnp.einsum("zts,zsd->ztd", tables, rows, preferred_element_type=F32).astype(BF16)

    grads_z = lax.all_gather(
        jnp.concatenate([own_first(y_major(cotangent)), token_mlp.T], axis=1), "z", axis=0
    )
    tables = grads_z[:, :, D:]
    sub = capacity // CHUNKS
    grad_slots = exchange(to_experts(grads_z[:, :, :D]), "expert")
    grad_rows = jnp.concatenate(
        [grad_slots[:, :, c * sub : (c + 1) * sub].reshape(-1, D) for c in range(CHUNKS)], axis=0
    )
    att_slots_in = select_rows(token_att, normed_one).reshape(experts, capacity, D)
    send = jnp.stack(
        [
            jnp.concatenate([s, jnp.broadcast_to(n[None], (experts, tok_rows, half))], axis=1)
            for s, n in zip(halves(att_slots_in), halves(normed_one))
        ],
        axis=1,
    )
    got = exchange(send.reshape(experts * ycount, capacity + tok_rows, half), both)
    query_in = got[:, :capacity].reshape(experts * ycount * capacity, half)
    kv_in = got[:, capacity:].reshape(experts * ycount * tok_rows, half)
    query_in, kv_in = step("projections", (query_in, kv_in))
    query_part = jnp.dot(query_in, wide_query, preferred_element_type=F32).astype(BF16)
    kv_out = jnp.dot(kv_in, wide_kv, preferred_element_type=F32).astype(BF16)
    back = jnp.concatenate(
        [
            query_part.reshape(experts * ycount, capacity, D),
            pack(kv_out.reshape(experts * ycount, tok_rows, kv_cols)),
        ],
        axis=1,
    )
    back = exchange(back, both).reshape(experts, ycount, 2 * capacity, D)
    makers["cotangent_rows"] = lambda: grads_z
    makers["cotangent_slots"] = lambda: grad_rows
    makers["output_weight"] = lambda: wide_output
    back = step("queries", back)
    summed = jnp.sum(back.astype(F32), axis=1).astype(BF16)
    query_slots = summed[:, :capacity].reshape(2 * tok_rows, D)
    kv_parts = unpack(summed[:, capacity:])
    keyvals = jnp.concatenate([kv_parts[e] for e in range(experts)], axis=-1)
    key_heads = keyvals[:, :D].reshape(tok_rows, HEADS, HEAD_DIM)
    value_heads = keyvals[:, D:].reshape(tok_rows, HEADS, HEAD_DIM)
    router_logits = lax.dot_general(
        normed_one, router_att, CONTRACT_LAST, preferred_element_type=F32
    )
    gate_att = chosen_gates(router_logits, att_routes, experts)
    query_pairs = spread_rows(table_att, query_slots)
    queries = query_pairs.reshape(2, tok_rows, HEADS, HEAD_DIM)
    mixed_heads, log_sums = attend_forward(queries, key_heads, value_heads, allowed)

    def to_rows(v):
        v = v.reshape(experts, 1, capacity, D)
        v = jnp.broadcast_to(v, (experts, ycount, capacity, D))
        return exchange(v.reshape(experts * ycount, capacity, D), both)

    def from_halves(v):
        v = exchange(v.reshape(experts * ycount, capacity, half), both)
        v = v.reshape(experts, ycount, capacity, half)
        return jnp.concatenate([v[:, y] for y in range(ycount)], axis=-1).reshape(2 * tok_rows, D)

    mixed_slots = step("attended", select_rows(table_att, mixed_heads))
    mixed_in = step("attended_rows", to_rows(mixed_slots).reshape(-1, D))
    projected = lax.dot_general(
        mixed_in, wide_output, CONTRACT_LAST, preferred_element_type=F32
    ).astype(BF16)
    att_slots = step("projected", from_halves(projected))
    att_pairs = spread_rows(table_att, att_slots).astype(F32).reshape(2, tok_rows, D)
    hidden = inputs + gate_att[:, 0:1] * att_pairs[0] + gate_att[:, 1:2] * att_pairs[1]
    scale_two = lax.rsqrt(jnp.mean(hidden * hidden, axis=1, keepdims=True) + EPSILON)
    normed_two = (hidden * scale_two * gain_two).astype(BF16)
    mlp_logits = lax.dot_general(
        normed_two, router_mlp, CONTRACT_LAST, preferred_element_type=F32
    )
    gate_mlp = chosen_gates(mlp_logits, mlp_routes, experts)

    slot_gates = jnp.sum(
        table_mlp.astype(F32) * jnp.concatenate([gate_mlp[:, 0], gate_mlp[:, 1]])[None], axis=1
    )
    gate_cols = jnp.pad(
        jnp.concatenate(split3(slot_gates.reshape(2, tok_rows).T), axis=1), ((0, 0), (0, 122))
    )
    rows_z = lax.all_gather(
        jnp.concatenate([own_first(normed_two), gate_cols], axis=1), "z", axis=0
    )
    rows_z = step("gathered_rows", rows_z)
    gates_z = rows_z[:, :, D:]
    gates_z = jnp.concatenate([gates_z[:, :, 0:6:2], gates_z[:, :, 1:6:2]], axis=1)
    gates_z = jnp.pad(gates_z, ((0, 0), (0, 0), (0, 125)))
    gates_z = gates_z.reshape(Z, experts, capacity, 128).transpose(1, 0, 2, 3)
    send = jnp.concatenate([to_experts(rows_z[:, :, :D]), gates_z], axis=-1)
    got = [
        exchange(send[:, :, c * sub : (c + 1) * sub], "expert").reshape(-1, D + 128)
        for c in range(CHUNKS)
    ]
    got[0] = step("expert_rows", got[0])
    wide_down, wide_gate_up = assemble("down"), assemble("gate_up")
    free_grad = jnp.dot(grad_rows, wide_down, preferred_element_type=F32)
    got[0] = after(got[0], free_grad)
    chunk_rows = grad_rows.shape[0] // CHUNKS

    def hidden_units(c):
        rows = got[c][:, :D]
        gates = jnp.sum(got[c][:, D : D + 3].astype(F32), axis=1, keepdims=True)
        free = free_grad[c * chunk_rows : (c + 1) * chunk_rows]
        gate_up = jnp.dot(rows, wide_gate_up, preferred_element_type=F32)
        gate_part = gate_up[:, :slice_ff]
        up_part = gate_up[:, slice_ff:]
        sigma = jax.nn.sigmoid(gate_part)
        activated = (gate_part * sigma * up_part).astype(BF16)
        act_grad = free * gates
        gate_grad = act_grad * up_part * sigma * (1.0 + gate_part * (1.0 - sigma))
        up_grad = act_grad * gate_part * sigma
        gate_up_grad = jnp.concatenate([gate_grad, up_grad], axis=-1).astype(BF16)
        row_part = lax.dot_general(
            gate_up_grad, wide_gate_up, CONTRACT_LAST, preferred_element_type=F32
        ).astype(BF16)
        sums = jnp.sum(activated.astype(F32) * free, axis=1, keepdims=True)
        sums = jnp.pad(jnp.concatenate(split3(sums), axis=1), ((0, 0), (0, 125)))
        row_part = jnp.concatenate([row_part, sums], axis=1)
        return rows, gates, activated, gate_up_grad, row_part

    units = [hidden_units(c) for c in range(CHUNKS)]
    ffn_rows, row_gates, activated, gate_up_grad = (
        jnp.concatenate(v, axis=0) for v in list(zip(*units))[:4]
    )

    def outer(left_rows, right_rows):
        return lax.dot_general(left_rows, right_rows, CONTRACT_FIRST, preferred_element_type=F32)

    def block(v, k):
        return lax.dynamic_index_in_dim(v, (z_index + k) % Z, 0, keepdims=False)

    def peers(left, right):
        return [
            outer(left[:, j * half : (j + 1) * half], right)
            .astype(BF16)
            .reshape(Z, part, right.shape[1])
            for j in js
        ]

    def add_up(own, moved):
        total = own
        for m in moved:
            total = total + m.astype(F32)
        return total

    def grad_makers(part_name, left, right):
        others = peers(left, right)
        own = outer(left[:, :half], right).reshape(Z, part, right.shape[1])
        for k in range(Z):

            def over_y(*steps, k=k):
                return [
                    y_shift(after(block(other, k), *steps), j, f"{part_name}_y{k}")
                    for j, other in zip(js, others)
                ]

            def over_z(*steps, k=k):
                total = add_up(block(own, k), fetch(f"{part_name}_y{k}"))
                return z_shift(after(total.astype(BF16), *steps), k, part_name) if k else total

            makers[f"{part_name}_y{k}"] = over_y
            makers[f"{part_name}_z{k}"] = over_z
        makers[f"{part_name}_peers"] = lambda: others
        makers[f"{part_name}_own"] = lambda: own

    def in_order(got):
        return [
            pick([got[(z - i) % Z].astype(F32) for z in range(Z)], z_index) for i in range(Z)
        ]

    gated_rows = (row_gates * grad_rows.astype(F32)).astype(BF16)
    grad_makers("gate_up_grad", ffn_rows, gate_up_grad)
    grad_makers("down_grad", gated_rows, activated)
    last_part = step("hidden_units", units[-1][4])
    back = jnp.concatenate(
        [
            exchange(v.reshape(experts, Z, sub, D + 128), "expert")
            for v in [u[4] for u in units[:-1]] + [last_part]
        ],
        axis=2,
    )
    back = step("row_slots", back)
    sums = back[..., D : D + 3].transpose(1, 0, 2, 3).reshape(Z, 2 * tok_rows, 3)
    sums = jnp.concatenate([sums[:, :tok_rows], sums[:, tok_rows:]], axis=-1)
    sums = jnp.concatenate(
        [jnp.where(z_index == z, sums, jnp.zeros_like(sums)) for z in range(Z)], axis=-1
    )
    sums = jnp.pad(sums, ((0, 0), (0, 0), (0, 128 - 6 * Z)))
    row_back = back
    back = lax.psum_scatter(
        jnp.concatenate([to_tokens(back[..., :D]), sums], axis=-1).reshape(-1, D + 128),
        "z",
        scatter_dimension=0,
        tiled=True,
    )
    ffn_row_grads = own_first_back(back[:, :D]).astype(F32)
    sums = back[:, D : D + 6 * Z].astype(F32).reshape(tok_rows, Z, 2, 3)
    sums = jnp.sum(sums, axis=(1, 3)).T.reshape(2 * tok_rows, 1)
    gate_mlp_grad = jnp.sum(table_mlp.astype(F32) * sums, axis=0).reshape(2, tok_rows).T

    def output_slots(*others):
        out_part = (
            row_gates
            * lax.dot_general(
                after(activated, row_back, *others),
                wide_down,
                CONTRACT_LAST,
                preferred_element_type=F32,
            )
        ).astype(BF16)
        out_part = out_part.reshape(CHUNKS, experts, Z, sub, D).transpose(1, 2, 0, 3, 4)
        return to_tokens(exchange(out_part.reshape(experts, Z, capacity, D), "expert"))

    makers["output_slots"] = output_slots
    makers["output_rows"] = lambda: lax.psum_scatter(
        fetch("output_slots").reshape(-1, D), "z", scatter_dimension=0, tiled=True
    )
    ffn_row_grads = step("row_grads", ffn_row_grads)
    logit_mlp_grad = gate_logit_grad(gate_mlp, gate_mlp_grad, mlp_routes, experts)
    normed_two_grad = (
        ffn_row_grads
        + jnp.dot(logit_mlp_grad, router_mlp.astype(F32), precision=HIGHEST)
    )
    hidden_grad = grad_out + norm_back(hidden, scale_two, gain_two, normed_two_grad)
    gate_att_grad = jnp.sum(hidden_grad[None] * att_pairs, axis=2).T
    logit_att_grad = gate_logit_grad(gate_att, gate_att_grad, att_routes, experts)
    gated_hidden = jnp.concatenate(
        [gate_att[:, 0:1] * hidden_grad, gate_att[:, 1:2] * hidden_grad], axis=0
    ).astype(BF16)
    hidden_send = select_rows(table_att, gated_hidden).reshape(experts, capacity, D)
    hidden_in = exchange(
        jnp.stack(halves(hidden_send), axis=1).reshape(experts * ycount, capacity, half), both
    ).reshape(-1, half)
    hidden_in = step("hidden_rows", hidden_in)
    head_part = jnp.dot(hidden_in, wide_output, preferred_element_type=F32).astype(BF16)
    head_part = exchange(head_part.reshape(experts * ycount, capacity, D), both)
    head_part = step("head_slots", head_part)
    head_slots = jnp.sum(
        head_part.reshape(experts, ycount, capacity, D).astype(F32), axis=1
    ).astype(BF16)
    mixed_grad = spread_rows(table_att, head_slots.reshape(2 * tok_rows, D)).reshape(
        2, tok_rows, HEADS, HEAD_DIM
    )
    makers["output_grad"] = lambda *others: lax.psum_scatter(
        outer(after(hidden_in, *others), mixed_in).astype(BF16),
        "z",
        scatter_dimension=0,
        tiled=True,
    )
    query_grad, key_grad, value_grad = attend_backward(
        queries, key_heads, value_heads, allowed, log_sums, mixed_grad
    )
    query_grad = step("query_grads", query_grad)
    keyval_row_grad = jnp.concatenate([key_grad, value_grad], axis=1).astype(BF16)
    query_send = select_rows(table_att, query_grad.astype(BF16)).reshape(experts, capacity, D)
    kv_send = pack(
        jnp.stack([keyval_row_grad[:, e * kv_cols : (e + 1) * kv_cols] for e in range(experts)])
    )
    send = jnp.concatenate([query_send, kv_send], axis=1).reshape(experts, 1, 2 * capacity, D)
    send = jnp.broadcast_to(send, (experts, ycount, 2 * capacity, D))
    got = exchange(send.reshape(experts * ycount, 2 * capacity, D), both)
    got = step("query_rows", got)
    block_out = (hidden + own_first_back(after(fetch("output_rows"), got)).astype(F32)).astype(BF16)
    query_rows = got[:, :capacity].reshape(-1, D)
    kv_rows = unpack(got[:, capacity:]).reshape(-1, kv_cols)
    input_part = lax.dot_general(
        query_rows, wide_query, CONTRACT_LAST, preferred_element_type=F32
    ).astype(BF16)
    normed_part = lax.dot_general(
        kv_rows, wide_kv, CONTRACT_LAST, preferred_element_type=F32
    ).astype(BF16)
    back = jnp.concatenate(
        [
            input_part.reshape(experts * ycount, capacity, half),
            normed_part.reshape(experts * ycount, tok_rows, half),
        ],
        axis=1,
    )
    query_outer = outer(query_in, query_rows).astype(BF16)
    kv_outer = outer(kv_in, kv_rows).astype(BF16)
    back = after(back, query_outer, kv_outer)
    back = exchange(back, both).reshape(experts, ycount, capacity + tok_rows, half)
    back = step("input_slots", back)
    gu_grads = in_order([fetch(f"gate_up_grad_z{k}") for k in range(Z)])
    down_grads = in_order([fetch(f"down_grad_z{k}") for k in range(Z)])
    gate_up_weight_grad = jnp.concatenate(
        [g[:, :slice_ff] for g in gu_grads] + [g[:, slice_ff:] for g in gu_grads], axis=1
    )[None]
    down_weight_grad = jnp.concatenate(down_grads, axis=1)[None]
    output_grad = fetch("output_grad").astype(F32)[None]
    back = jnp.concatenate([back[:, y] for y in range(ycount)], axis=-1)
    input_pairs = (
        spread_rows(table_att, back[:, :capacity].reshape(2 * tok_rows, D))
        .astype(F32)
        .reshape(2, tok_rows, D)
    )
    kv_grad_part = lax.psum_scatter(kv_outer, "z", scatter_dimension=0, tiled=True)
    query_weight_grad = lax.psum_scatter(
        query_outer, "z", scatter_dimension=0, tiled=True
    ).astype(F32)[None]
    kv_grads = exchange(
        jnp.broadcast_to(kv_grad_part[None], (experts, *kv_grad_part.shape)), "expert"
    )
    keyval_grad = jnp.concatenate([kv_grads[e] for e in range(experts)], axis=1).astype(F32)
    normed_one_grad = (
        input_pairs[0] + input_pairs[1] + jnp.sum(back[:, capacity:].astype(F32), axis=0)
    )
    normed_one_grad = normed_one_grad + jnp.dot(
        logit_att_grad, router_att.astype(F32), precision=HIGHEST
    )
    input_grad = natural(
        hidden_grad + norm_back(inputs, scale_one, gain_one, normed_one_grad)
    )

    small_grads = jnp.concatenate(
        [
            jnp.sum(normed_one_grad * inputs * scale_one, axis=0)[None],
            jnp.sum(normed_two_grad * hidden * scale_two, axis=0)[None],
            lax.dot_general(
                logit_att_grad, normed_one.astype(F32), CONTRACT_FIRST, precision=HIGHEST
            ),
            lax.dot_general(
                logit_mlp_grad, normed_two.astype(F32), CONTRACT_FIRST, precision=HIGHEST
            ),
        ],
        axis=0,
    )
    rows = small_grads.shape[0]
    small_grads = jnp.stack(
        [small_grads[:, i * part : (i + 1) * part] for i in range(Z * ycount)]
    )
    small_grads = step("small", exchange(small_grads, ("y", "z")))
    small_grads = jnp.sum(small_grads, axis=0)
    small_grads = exchange(
        jnp.broadcast_to(small_grads[None], (experts, rows, part)), "expert"
    )
    small_grads = jnp.sum(small_grads, axis=0).T
    gains_grad = small_grads[:, :2]
    router_grad = small_grads[:, 2:rows]
    return (
        natural(block_out),
        input_grad,
        gains_grad,
        keyval_grad,
        router_grad,
        query_weight_grad,
        output_grad,
        gate_up_weight_grad,
        down_weight_grad,
    )


def solution(mesh):
    experts, shards = mesh.shape["expert"], mesh.shape["shard"]
    grid = Mesh(mesh.devices.reshape(experts, Z, shards // Z), ("expert", "z", "y"))
    rows = P(("expert", "z", "y"), None)
    shared = P(("z", "y"), None)
    owned = P("expert", ("z", "y"), None)
    in_specs = (rows,) * 6 + (shared,) * 3 + (owned,) * 4
    out_specs = (rows,) * 2 + (shared,) * 3 + (owned,) * 4
    return jax.shard_map(
        per_device, mesh=grid, in_specs=in_specs, out_specs=out_specs, check_vma=False
    )
```
